32 devices in a mesh: rows: 4 (over y, core), heads: 8 (over z, x).
Axes of the slice: x: 2, y: 2, z: 4, core: 2. Of those that a mesh axis runs over, the one named last changes fastest.
Arguments:
- stream: float32 [4, 512, 2048], P('rows'), may hold values from -6 to 6
- doc_starts: int32 [4, 512], P('rows'), may hold values from 0 to 1, as said below
- valid_mask: int32 [4, 512], P('rows'), may hold values from 0 to 1, as said below
- first_gain: float32 [2048], P('heads'), may hold values from 0.5 to 1.5
- w_query: float32 [2048, 2048], P(None, 'heads'), may hold values from -0.125 to 0.125
- w_key: float32 [2048, 2048], P(None, 'heads'), may hold values from -0.125 to 0.125
- w_value: float32 [2048, 2048], P(None, 'heads'), may hold values from -0.125 to 0.125
- w_rate: float32 [2048, 32], P(None, 'heads'), may hold values from -0.125 to 0.125
- b_rate: float32 [32], P('heads'), may hold values from -3 to 3
- inner_weight: float32 [32, 64, 64], P('heads'), may hold values from -0.75 to 0.75
- inner_bias: float32 [32, 64], P('heads'), may hold values from -4 to 4
- inner_gain: float32 [32, 64], P('heads'), may hold values from 0.5 to 1.5
- inner_shift: float32 [32, 64], P('heads'), may hold values from -3 to 3
- post_gain: float32 [2048], P('heads'), may hold values from 0.5 to 1.5
- post_shift: float32 [2048], P('heads'), may hold values from -3 to 3
- w_gate_attn: float32 [2048, 2048], P(None, 'heads'), may hold values from -0.125 to 0.125
- w_out: float32 [2048, 2048], P(None, 'heads'), may hold values from -0.125 to 0.125
- second_gain: float32 [2048], P('heads'), may hold values from 0.5 to 1.5
- w_gate: float32 [2048, 5504], P(None, 'heads'), may hold values from -0.125 to 0.125
- w_up: float32 [2048, 5504], P(None, 'heads'), may hold values from -0.125 to 0.125
- w_down: float32 [5504, 2048], P('heads'), may hold values from -0.078125 to 0.078125
- cotangent: float32 [4, 512, 2048], P('rows', None, 'heads'), may hold values from -6 to 6
Outputs:
- output: float32 [4, 512, 2048], P('rows', None, 'heads')
- grad_stream: float32 [4, 512, 2048], P('rows', None, 'heads')
- grad_first_gain: float32 [2048], P('heads')
- grad_query: float32 [2048, 2048], P(None, 'heads')
- grad_key: float32 [2048, 2048], P(None, 'heads')
- grad_value: float32 [2048, 2048], P(None, 'heads')
- grad_rate: float32 [2048, 32], P(None, 'heads')
- grad_rate_bias: float32 [32], P('heads')
- grad_inner_weight: float32 [32, 64, 64], P('heads')
- grad_inner_bias: float32 [32, 64], P('heads')
- grad_inner_gain: float32 [32, 64], P('heads')
- grad_inner_shift: float32 [32, 64], P('heads')
- grad_post_gain: float32 [2048], P('heads')
- grad_post_shift: float32 [2048], P('heads')
- grad_gate_attn: float32 [2048, 2048], P(None, 'heads')
- grad_out: float32 [2048, 2048], P(None, 'heads')
- grad_second_gain: float32 [2048], P('heads')
- grad_gate: float32 [2048, 5504], P(None, 'heads')
- grad_up: float32 [2048, 5504], P(None, 'heads')
- grad_down: float32 [5504, 2048], P('heads')
- rms_values: float32 [5], replicated
The draws below stay inside these ranges and needn't reach their ends.
Inputs may be any that keep to these rules, and one draw needn't show every extreme that they name: `doc_starts`: every row's first token is 1, and 1 stands only at positions that are multiples of 16. `valid_mask`: in each row the valid tokens are a leading run of 256 tokens or more.
All inputs are finite; a program needn't handle non-finite values.
Results may differ from the reference program's by a relative error of at most 0.0003.
Values sent between devices are 32-bit elements; how exact they have to be, the bound alone decides.
No kernel may reach another device: no remote copies, remote signals or barrier semaphores. Data moves between devices by JAX's collectives and lax.ppermute only.
A program may use at most 192 MiB of HBM per device.

```python
import math
import jax
import jax.numpy as jnp
from jax import lax

D = 2048
HEADS = 32
HD = 64
FF = 5504
MB = 16
LEN = 512
ROWS = 4


def draw_doc_starts(key, part):
    blocks = LEN // MB
    odds = max(2, blocks // 8)
    picks = jax.random.randint(jax.random.fold_in(key, 11), (ROWS, blocks), 0, odds)
    first = (jnp.arange(blocks) == 0)[None, :]
    marks = jnp.where(first | (picks == 0), 1, 0).astype(jnp.int32)
    filler = jnp.zeros((ROWS, blocks, MB - 1), jnp.int32)
    return jnp.concatenate([marks[:, :, None], filler], axis=2).reshape(ROWS, LEN)


def draw_valid_mask(key, part):
    limit = jax.random.randint(jax.random.fold_in(key, 23), (ROWS, 1), LEN // 2, LEN + 1)
    return (jnp.arange(LEN)[None, :] < limit).astype(jnp.int32)


def shard_levels(rng, shape, cuts, low, high):
    factor_of, own = 1.0, jax.random.fold_in(rng, 6)
    for dim, shards_of in cuts:
        steps = jnp.exp(jax.random.uniform(jax.random.fold_in(own, dim), (shards_of,), jnp.float32, low / len(cuts), high / len(cuts)))
        factor_of = factor_of * jnp.repeat(steps, shape[dim] // shards_of).reshape([-1 if axis == dim else 1 for axis in range(len(shape))])
    return factor_of


def gaussian(own_key, dims, spread, bound, pieces=(), kind=jnp.bfloat16):
    loudness = shard_levels(own_key, dims, pieces, -0.22, 0.18) if pieces else 1.0
    entries = jax.random.normal(own_key, dims, jnp.float32) * spread * loudness
    return jnp.minimum(jnp.maximum(entries, -bound), bound).astype(kind)


def setup_inputs(seed: int = 0) -> dict:
    key_list = jax.random.split(jax.random.key(seed), 23)
    return {
        "stream": gaussian(key_list[0], (ROWS, LEN, D), 1.0, 6.0, ((0, 4),), jnp.float32),
        "doc_starts": draw_doc_starts(jax.random.fold_in(key_list[22], 71), 0),
        "valid_mask": draw_valid_mask(jax.random.fold_in(key_list[22], 71), 0),
        "first_gain": jnp.clip(1.0 + 0.1 * jax.random.normal(key_list[3], (D,), jnp.float32), 0.5, 1.5),
        "w_query": gaussian(key_list[4], (D, HEADS * HD), D ** -0.5, 0.125, ((1, 8),), jnp.float32),
        "w_key": gaussian(key_list[5], (D, HEADS * HD), D ** -0.5, 0.125, ((1, 8),), jnp.float32),
        "w_value": gaussian(key_list[6], (D, HEADS * HD), D ** -0.5, 0.125, ((1, 8),), jnp.float32),
        "w_rate": gaussian(key_list[7], (D, HEADS), D ** -0.5, 0.125, ((1, 8),), jnp.float32),
        "b_rate": gaussian(key_list[8], (HEADS,), 1.0, 3.0, ((0, 8),), jnp.float32),
        "inner_weight": gaussian(key_list[9], (HEADS, HD, HD), HD ** -0.5, 0.75, ((0, 8),), jnp.float32),
        "inner_bias": gaussian(key_list[10], (HEADS, HD), 1.0, 4.0, ((0, 8),), jnp.float32),
        "inner_gain": jnp.clip(1.0 + 0.1 * jax.random.normal(key_list[11], (HEADS, HD), jnp.float32), 0.5, 1.5),
        "inner_shift": gaussian(key_list[12], (HEADS, HD), 0.5, 3.0, ((0, 8),), jnp.float32),
        "post_gain": jnp.clip(1.0 + 0.1 * jax.random.normal(key_list[13], (HEADS * HD,), jnp.float32), 0.5, 1.5),
        "post_shift": gaussian(key_list[14], (HEADS * HD,), 0.5, 3.0, ((0, 8),), jnp.float32),
        "w_gate_attn": gaussian(key_list[15], (D, HEADS * HD), D ** -0.5, 0.125, ((1, 8),), jnp.float32),
        "w_out": gaussian(key_list[16], (HEADS * HD, D), (HEADS * HD) ** -0.5, 0.125, ((1, 8),), jnp.float32),
        "second_gain": jnp.clip(1.0 + 0.1 * jax.random.normal(key_list[17], (D,), jnp.float32), 0.5, 1.5),
        "w_gate": gaussian(key_list[18], (D, FF), D ** -0.5, 0.125, ((1, 8),), jnp.float32),
        "w_up": gaussian(key_list[19], (D, FF), D ** -0.5, 0.125, ((1, 8),), jnp.float32),
        "w_down": gaussian(key_list[20], (FF, D), FF ** -0.5, 0.078125, ((0, 8),), jnp.float32),
        "cotangent": gaussian(key_list[21], (ROWS, LEN, D), 1.0, 6.0, ((0, 4), (2, 8)), jnp.float32),
    }


@jax.custom_vjp
def low(v):
    return lax.optimization_barrier(v.astype(jnp.bfloat16)).astype(jnp.float32)

@jax.custom_vjp
def low_back(v):
    return v

def low_keep(v):
    return (low(v), None)

def low_pass(kept, grad):
    return (grad,)

def back_keep(v):
    return (v, None)

def back_low(kept, grad):
    return (low(grad),)
low.defvjp(low_keep, low_pass)
low_back.defvjp(back_keep, back_low)
precise = lax.Precision.HIGHEST
epsilon = 1e-06

def product(left, right):
    return jnp.dot(left, right, precision=precise, preferred_element_type=jnp.float32)

def rms_norm(array, gain):
    return array * lax.rsqrt(lax.optimization_barrier(jnp.mean(array * array, -1, keepdims=True)) + epsilon) * gain

def layer_norm(array, gain, shift):
    center = array - lax.optimization_barrier(jnp.mean(array, -1, keepdims=True))
    return center * lax.rsqrt(lax.optimization_barrier(jnp.mean(center * center, -1, keepdims=True)) + epsilon) * gain + shift

def activate(array):
    return jax.nn.gelu(array, approximate=True)

def inner_step(state, query_rows, key_rows, value_rows, rate_rows, reset_flags, w_init, b_init, norm_gain, norm_shift):
    weight, offset = state
    keep = (reset_flags == 0).astype(jnp.float32)
    weight = keep[:, None, None, None] * weight + (1.0 - keep[:, None, None, None]) * w_init
    offset = keep[:, None, None] * offset + (1.0 - keep[:, None, None]) * b_init
    block_len = query_rows.shape[1]
    recon = jnp.einsum('rihd,rhde->rihe', key_rows, weight, precision=precise) + offset[:, None]
    center = recon - lax.optimization_barrier(jnp.mean(recon, -1, keepdims=True))
    inv_std = lax.rsqrt(lax.optimization_barrier(jnp.mean(center * center, -1, keepdims=True)) + epsilon)
    unit_rows = center * inv_std
    error = (unit_rows * norm_gain + norm_shift - (value_rows - key_rows)) * norm_gain
    inner_grad = inv_std * (error - lax.optimization_barrier(jnp.mean(error, -1, keepdims=True)) - unit_rows * lax.optimization_barrier(jnp.mean(error * unit_rows, -1, keepdims=True)))
    position = jnp.arange(1, block_len + 1, dtype=jnp.float32)
    causal = (jnp.arange(block_len)[:, None] >= jnp.arange(block_len)[None, :]).astype(jnp.float32)
    step_size = causal * jnp.moveaxis(rate_rows, 1, 2)[:, :, None, :] / position[:, None]
    scores = jnp.einsum('rihd,rjhd->rhij', query_rows, key_rows, precision=precise)
    shifted = offset[:, None] - jnp.einsum('rhij,rjhd->rihd', step_size, inner_grad, precision=precise)
    inner_out = jnp.einsum('rihd,rhde->rihe', query_rows, weight, precision=precise) - jnp.einsum('rhij,rjhd->rihd', step_size * scores, inner_grad, precision=precise) + shifted
    last_rate = rate_rows / block_len
    weight = weight - jnp.einsum('rjh,rjhd,rjhe->rhde', last_rate, key_rows, inner_grad, precision=precise)
    offset = offset - jnp.einsum('rjh,rjhe->rhe', last_rate, inner_grad, precision=precise)
    return ((weight, offset), query_rows + layer_norm(inner_out, norm_gain, norm_shift))

def ttt_layer(queries, keys, values, rate, starts, w_init, b_init, norm_gain, norm_shift):
    rows, length, heads, dim = queries.shape
    count = length // MB
    per = math.gcd(count, 8)
    turns = count // per

    def split(array):
        array = array.reshape((rows, turns, per, MB) + array.shape[2:])
        return jnp.moveaxis(array, 0, 2)
    resets = jnp.moveaxis(starts[:, ::MB].reshape(rows, turns, per), 0, 2)

    def turn(state, block):
        block_q, block_k, block_v, block_rate, block_reset = block
        results = []
        for index in range(per):
            state, result = inner_step(state, block_q[index], block_k[index], block_v[index], block_rate[index], block_reset[index], w_init, b_init, norm_gain, norm_shift)
            results.append(result)
        return (state, jnp.stack(results))
    initial = (jnp.zeros((rows, heads, dim, dim), jnp.float32), jnp.zeros((rows, heads, dim), jnp.float32))
    final, results = lax.scan(jax.checkpoint(turn), initial, (split(queries), split(keys), split(values), split(rate), resets))
    return jnp.moveaxis(results, 2, 0).reshape(rows, length, heads, dim)

def forward(stream, params, doc_starts):
    first_gain, w_query, w_key, w_value, w_rate, b_rate, inner_weight, inner_bias, inner_gain, inner_shift, post_gain, post_shift, w_gate_attn, w_out, second_gain, w_gate, w_up, w_down = params
    rows, length, width = stream.shape
    heads, head_dim = inner_bias.shape
    tokens = stream.reshape(rows * length, width)
    normed = rms_norm(tokens, first_gain)
    head_shape = (rows, length, heads, head_dim)
    queries = product(normed, w_query).reshape(head_shape)
    keys = product(normed, w_key).reshape(head_shape)
    values = product(normed, w_value).reshape(head_shape)
    rate = (jax.nn.sigmoid(product(normed, w_rate) + b_rate) / head_dim).reshape(rows, length, heads)
    mixed = ttt_layer(queries, keys, values, rate, doc_starts, inner_weight, inner_bias, inner_gain, inner_shift)
    mixed = mixed.reshape(rows * length, heads * head_dim)
    shaped = layer_norm(mixed, post_gain, post_shift)
    gated = activate(product(normed, w_gate_attn)) * shaped
    attn = product(gated, w_out)
    hidden = tokens + attn
    hnorm = rms_norm(hidden, second_gain)
    ffn = product(jax.nn.silu(product(hnorm, w_gate)) * product(hnorm, w_up), w_down)
    output = hidden + ffn
    return (output.reshape(rows, length, width), (tokens, attn, hidden, ffn, output))

def reference(stream, doc_starts, valid_mask, first_gain, w_query, w_key, w_value, w_rate, b_rate, inner_weight, inner_bias, inner_gain, inner_shift, post_gain, post_shift, w_gate_attn, w_out, second_gain, w_gate, w_up, w_down, cotangent):
    params = (first_gain, w_query, w_key, w_value, w_rate, b_rate, inner_weight, inner_bias, inner_gain, inner_shift, post_gain, post_shift, w_gate_attn, w_out, second_gain, w_gate, w_up, w_down)

    def apply(stream_in, params_in):
        return forward(stream_in, params_in, doc_starts)
    output, pullback, extras = jax.vjp(apply, stream, params, has_aux=True)
    grad_stream, grads = pullback(cotangent)
    grad_first_gain, grad_query, grad_key, grad_value, grad_rate, grad_rate_bias, grad_inner_weight, grad_inner_bias, grad_inner_gain, grad_inner_shift, grad_post_gain, grad_post_shift, grad_gate_attn, grad_out, grad_second_gain, grad_gate, grad_up, grad_down = grads
    weights = valid_mask.reshape(-1).astype(jnp.float32)[:, None]
    denom = jnp.sum(weights) * stream.shape[2]
    rms_values = jnp.sqrt(jnp.stack([jnp.sum(weights * member * member) for member in extras]) / denom)
    return (output, grad_stream, grad_first_gain, grad_query, grad_key, grad_value, grad_rate, grad_rate_bias, grad_inner_weight, grad_inner_bias, grad_inner_gain, grad_inner_shift, grad_post_gain, grad_post_shift, grad_gate_attn, grad_out, grad_second_gain, grad_gate, grad_up, grad_down, rms_values)
```

```python
import functools
import jax, jax.numpy as jnp
from jax import lax
from jax.experimental import pallas as pl
from jax.experimental.pallas import tpu as pltpu

from jax.sharding import PartitionSpec as P

MB = 16
CH = 128
epsilon = 1e-06
f32 = jnp.float32
bf16 = jnp.bfloat16
NN = ((1,), (0,))


def split(x):
    hi = x.astype(bf16)
    return hi, (x - hi.astype(f32)).astype(bf16)


def mm(a, b, dims=NN):
    def one(p, q):
        return lax.dot_general(p, q, (dims, ((), ())), preferred_element_type=f32)

    return one(a[0], b[0]) + (one(a[0], b[1]) + one(a[1], b[0]))


def wide(x):
    hi, lo = split(x)
    return jnp.concatenate([hi, lo], axis=1)


def tall_dot(x, pair):
    rows = x.shape[0]
    cols = pair.shape[1] // 2
    hi, lo = split(x)
    out = lax.dot_general(
        jnp.concatenate([hi, lo], axis=0), pair, (NN, ((), ())), preferred_element_type=f32
    )
    top, low = out[:rows], out[rows:]
    return top[:, :cols] + (top[:, cols:] + low[:, :cols])


def iota(shape, dim):
    return lax.broadcasted_iota(jnp.int32, shape, dim)


def head_sum(x, hd):
    rows, cols = x.shape
    parts = [
        jnp.broadcast_to(jnp.sum(x[i : i + hd], axis=0, keepdims=True), (hd, cols))
        for i in range(0, rows, hd)
    ]
    return parts[0] if len(parts) == 1 else jnp.concatenate(parts, axis=0)


def lane_sum(x):
    return jnp.sum(x, axis=1, keepdims=True)


def coefficients(transposed):
    source = iota((CH, CH), 1 if transposed else 0)
    target = iota((CH, CH), 0 if transposed else 1)
    before = (source // MB < target // MB).astype(f32) * (1.0 / MB)
    inside = ((source // MB == target // MB) & (source <= target)).astype(f32)
    return before, before + inside / ((target % MB) + 1).astype(f32)


def forward_body(
    joined, rate, rate_t, seg, seg_t, w0, b0, gain, shift, mixed, z_out, zb_out, w_out, b_out,
    w_s, b_s, z_s, tau_s, a_s, m_s, *, hd, heads,
):
    pairs = heads * hd // CH
    per = CH // hd
    span = heads * hd
    chunks = joined.shape[0] // CH
    n_inv = 1.0 / hd
    row_head = iota((CH, CH), 0) // hd
    lane_head = iota((CH, CH), 1) // hd
    lane_block = iota((hd, CH), 1) // MB
    block_diag = row_head == lane_head
    w_s[...] = jnp.zeros_like(w_s)
    b_s[...] = jnp.zeros_like(b_s)

    def chunk(c, carry):
        ts = pl.multiple_of(c * CH, CH)
        here = pl.ds(ts, CH)
        seg_row = seg_t[:, here]
        seg_col = seg[here, :]
        last_seg = seg_row[:, CH - 1 : CH]
        prev = jnp.max(jnp.where(iota(seg_t.shape, 1) < ts, seg_t[...], 0.0), keepdims=True)
        carried = seg_row == prev
        in_last = (seg_row == last_seg).astype(f32)
        whole = last_seg == prev
        same = seg_col == seg_row
        before, within = coefficients(False)
        before = jnp.where(same, before, 0.0)
        within = jnp.where(same, within, 0.0)
        for p in range(pairs):
            rows = slice(p * CH, (p + 1) * CH)
            kn = joined[here, span + p * CH : span + (p + 1) * CH]
            qn = joined[here, p * CH : (p + 1) * CH]
            vn = joined[here, 2 * span + p * CH : 2 * span + (p + 1) * CH]
            k_t, q_t, v_t = kn.T, qn.T, vn.T
            ks, kts, qts = split(kn), split(k_t), split(q_t)
            ws, w0s = split(w_s[rows]), split(w0[rows])
            bias = jnp.where(carried, b_s[rows], b0[rows])
            z_s[rows] = jnp.where(carried, mm(ws, kts), mm(w0s, kts)) + bias
            zb_out[rows, here] = jnp.where(carried, mm(ws, qts), mm(w0s, qts)) + bias
            w_out[c, rows] = w_s[rows]
            b_out[c, rows] = b_s[rows]
            tau_s[rows] = gain[rows] * (shift[rows] - v_t + k_t)
            for hh in range(per):
                h = p * per + hh
                own = (row_head == hh).astype(bf16)
                r_col = rate[here, h : h + 1]
                score = mm(ks, (kts[0] * own, kts[1] * own))
                a_s[h] = wide((score + 1.0) * (before * r_col))
                score = mm(ks, (qts[0] * own, qts[1] * own))
                m_s[h] = wide((score + 1.0) * (within * r_col))

        gsq = [jnp.broadcast_to(gain[h * hd : (h + 1) * hd] ** 2, (hd, CH)) for h in range(heads)]
        tsum = [
            jnp.sum(tau_s[h * hd : (h + 1) * hd], axis=0, keepdims=True) * n_inv
            for h in range(heads)
        ]

        def inner(h, z):
            tau = tau_s[h * hd : (h + 1) * hd]
            zg = z * gsq[h]
            m2 = jnp.sum(z * z, axis=0, keepdims=True) * n_inv
            a1 = jnp.sum(zg, axis=0, keepdims=True) * n_inv
            a2 = jnp.sum(z * zg, axis=0, keepdims=True) * n_inv
            a3 = jnp.sum(z * tau, axis=0, keepdims=True) * n_inv
            s = lax.rsqrt(m2 + epsilon)
            c_eu = s * (s * a2 + a3)
            e_mean = s * a1 + tsum[h]
            return (s * s) * (zg - c_eu * z) + s * (tau - e_mean)

        def step(t, zs):
            now = lane_block == t
            new = []
            for h in range(heads):
                g = jnp.where(now, inner(h, zs[h]), 0.0)
                new.append(zs[h] - tall_dot(g, a_s[h]))
            return tuple(new)

        zs = tuple(z_s[h * hd : (h + 1) * hd] for h in range(heads))
        zs = lax.fori_loop(0, CH // MB - 1, step, zs)
        for p in range(pairs):
            rows = slice(p * CH, (p + 1) * CH)
            gs = []
            outs = []
            for hh in range(per):
                h = p * per + hh
                hr = slice(h * hd, (h + 1) * hd)
                z_out[hr, here] = zs[h]
                g = inner(h, zs[h])
                zb = zb_out[hr, here] - tall_dot(g, m_s[h])
                zb_out[hr, here] = zb
                sb = lax.rsqrt(jnp.sum(zb * zb, axis=0, keepdims=True) * n_inv + epsilon)
                outs.append(zb * sb * gain[hr] + shift[hr])
                gs.append(g * (rate_t[h : h + 1, here] * in_last * (1.0 / MB)))
            gw = jnp.concatenate(gs, axis=0)
            lanes = slice(p * CH, (p + 1) * CH)
            mixed[here, lanes] = joined[here, lanes] + jnp.concatenate(outs, axis=0).T
            kn = joined[here, span + p * CH : span + (p + 1) * CH]
            upd = mm(split(gw), split(kn))
            w_s[rows] = jnp.where(whole, w_s[rows], w0[rows]) - jnp.where(block_diag, upd, 0.0)
            b_s[rows] = jnp.where(whole, b_s[rows], b0[rows]) - lane_sum(gw)
        return carry

    lax.fori_loop(0, chunks, chunk, 0)


def ttt_forward(joined, rate, rate_t, seg, seg_t, w0, b0, gain, shift, hd, heads):
    length = joined.shape[0]
    span = heads * hd
    chunks = length // CH
    shape = jax.ShapeDtypeStruct
    return pl.pallas_call(
        functools.partial(forward_body, hd=hd, heads=heads),
        out_shape=(
            shape((length, span), f32),
            shape((span, length), f32),
            shape((span, length), f32),
            shape((chunks, span, CH), f32),
            shape((chunks, span, 1), f32),
        ),
        scratch_shapes=[
            pltpu.VMEM((span, CH), f32),
            pltpu.VMEM((span, 1), f32),
            pltpu.VMEM((span, CH), f32),
            pltpu.VMEM((span, CH), f32),
            pltpu.VMEM((heads, CH, 2 * CH), bf16),
            pltpu.VMEM((heads, CH, 2 * CH), bf16),
        ],
        compiler_params=pltpu.CompilerParams(vmem_limit_bytes=48 << 20),
        name="inner_forward",
    )(joined, rate, rate_t, seg, seg_t, w0, b0, gain, shift)


def backward_body(
    joined, rate_t, seg, seg_t, w0, b0, gain, shift, z_in, zb_in, w_in, b_in, dy,
    dq_out, dk_out, dv_out, dr_out, dw_out, db_out, dg_out, dsh_out,
    dw_s, db_s, p_s, u_s, f_s, bb_s, e2_s, u2_s, gt_s, dzb_s, at_s, sc_s,
    *, hd, heads,
):
    pairs = heads * hd // CH
    per = CH // hd
    span = heads * hd
    chunks = joined.shape[0] // CH
    n_inv = 1.0 / hd
    row_head = iota((CH, CH), 0) // hd
    lane_head = iota((CH, CH), 1) // hd
    lane_block = iota((hd, CH), 1) // MB
    block_diag = row_head == lane_head
    for ref in (dw_s, db_s, dw_out, db_out, dg_out, dsh_out):
        ref[...] = jnp.zeros_like(ref)

    def mean(x):
        return head_sum(x, hd) * n_inv

    def chunk(index, carry):
        c = chunks - 1 - index
        ts = pl.multiple_of(c * CH, CH)
        here = pl.ds(ts, CH)
        seg_row = seg_t[:, here]
        seg_col = seg[here, :]
        last_seg = seg_row[:, CH - 1 : CH]
        prev = jnp.max(jnp.where(iota(seg_t.shape, 1) < ts, seg_t[...], 0.0), keepdims=True)
        carried = seg_row == prev
        carried_col = seg_col == prev
        in_last = (seg_row == last_seg).astype(f32)
        whole = last_seg == prev
        same = seg_col == seg_row
        before, within = coefficients(True)
        before = jnp.where(same, before, 0.0)
        within = jnp.where(same, within, 0.0)
        consts = {}
        for p in range(pairs):
            rows = slice(p * CH, (p + 1) * CH)
            lanes = slice(p * CH, (p + 1) * CH)
            qn = joined[here, p * CH : (p + 1) * CH]
            kn = joined[here, span + p * CH : span + (p + 1) * CH]
            vn = joined[here, 2 * span + p * CH : 2 * span + (p + 1) * CH]
            k_t, v_t, dy_t = kn.T, vn.T, dy[here, lanes].T
            qs, ks, kts = split(qn), split(kn), split(k_t)
            g_col = gain[rows]
            gsq = g_col * g_col
            zb = zb_in[rows, here]
            sb = lax.rsqrt(mean(zb * zb) + epsilon)
            ub = zb * sb
            dg_out[rows] += lane_sum(dy_t * ub)
            dsh_out[rows] += lane_sum(dy_t)
            pb = dy_t * g_col
            dzb = sb * (pb - mean(pb) - ub * mean(pb * ub))
            dzb_s[rows] = dzb
            z = z_in[rows, here]
            s = lax.rsqrt(mean(z * z) + epsilon)
            u = z * s
            gu = gsq * u
            e = gu + g_col * (shift[rows] - v_t + k_t)
            c_eu = mean(e * u)
            g_t = s * (e - mean(e) - u * c_eu)
            gt_s[rows] = g_t
            u_s[rows] = u
            f_s[rows] = g_t + s * gu
            bb_s[rows] = (s * s) * (gsq - c_eu)
            e2_s[rows] = (s * s) * (e + gu)
            u2_s[rows] = s * u
            h1 = s * mean(gu)
            h2 = 2.0 * s * c_eu + s * mean(gu * u)
            dzbs = split(dzb)
            gts = split(g_t)
            dzbn = split(dzb.T)
            from_state = mm(split(dw_s[rows]), kts) + db_s[rows]
            pieces = []
            dq = dy[here, lanes]
            dk = jnp.zeros((CH, CH), f32)
            for hh in range(per):
                h = p * per + hh
                hr = slice(hh * hd, (hh + 1) * hd)
                r_row = rate_t[h : h + 1, here]
                consts[h] = (h1[hh * hd : hh * hd + 1], h2[hh * hd : hh * hd + 1])
                own = (row_head == hh).astype(bf16)
                own_lane = (lane_head == hh).astype(bf16)
                kt_h = (kts[0] * own, kts[1] * own)
                sc = (mm(ks, kt_h) + 1.0) * before
                sc_s[h] = sc
                at_s[h] = wide(sc * r_row)
                scq = (mm(qs, kt_h) + 1.0) * within
                pt = mm(dzbn, (gts[0] * own, gts[1] * own))
                dr_out[h : h + 1, here] = -jnp.sum(pt * scq, axis=0, keepdims=True) - (
                    (1.0 / MB) * in_last
                ) * jnp.sum(g_t[hr] * from_state[hr], axis=0, keepdims=True)
                pm = pt * (within * r_row)
                pms = split(pm)
                pmts = split(pm.T)
                kn_h = (ks[0] * own_lane, ks[1] * own_lane)
                qn_h = (qs[0] * own_lane, qs[1] * own_lane)
                dq = dq - mm(pms, kn_h)
                dk = dk - mm(pmts, qn_h)
                pieces.append(
                    -mm((dzbs[0][hr], dzbs[1][hr]), split(scq * r_row))
                    - from_state[hr] * (r_row * in_last * (1.0 / MB))
                )
            p_s[rows] = jnp.concatenate(pieces, axis=0)
            w0s = split(w0[rows])
            wd = split(w_in[c, rows] - w0[rows])
            zero = jnp.zeros((), bf16)
            dzbn_c = (jnp.where(carried_col, dzbn[0], zero), jnp.where(carried_col, dzbn[1], zero))
            dq_out[here, lanes] = dq + mm(dzbn, w0s) + mm(dzbn_c, wd)
            dk_out[here, lanes] = dk

        def upstream(h, pv):
            hr = slice(h * hd, (h + 1) * hd)
            h1, h2 = consts[h]
            pm = jnp.sum(pv, axis=0, keepdims=True) * n_inv
            q = jnp.sum(pv * u_s[hr], axis=0, keepdims=True) * n_inv
            kf = jnp.sum(pv * f_s[hr], axis=0, keepdims=True) * n_inv
            kappa = kf - h1 * pm - h2 * q
            dz = (pv - pm) * bb_s[hr] - q * e2_s[hr] - kappa * u2_s[hr]
            return dz, pm, q

        def step(index, ps):
            now = lane_block == (CH // MB - 1 - index)
            new = []
            for h in range(heads):
                dz = jnp.where(now, upstream(h, ps[h])[0], 0.0)
                new.append(ps[h] - tall_dot(dz, at_s[h]))
            return tuple(new)

        ps = tuple(p_s[h * hd : (h + 1) * hd] for h in range(heads))
        ps = lax.fori_loop(0, CH // MB - 1, step, ps)

        for p in range(pairs):
            rows = slice(p * CH, (p + 1) * CH)
            lanes = slice(p * CH, (p + 1) * CH)
            qn = joined[here, p * CH : (p + 1) * CH]
            kn = joined[here, span + p * CH : span + (p + 1) * CH]
            vn = joined[here, 2 * span + p * CH : 2 * span + (p + 1) * CH]
            qs, ks = split(qn), split(kn)
            g_t = gt_s[rows]
            gts = split(g_t)
            dzs, des = [], []
            for hh in range(per):
                h = p * per + hh
                hr = slice(h * hd, (h + 1) * hd)
                dz, pm, q = upstream(h, ps[h])
                dzs.append(dz - jnp.sum(dz, axis=0, keepdims=True) * n_inv)
                z = z_in[hr, here]
                s = lax.rsqrt(jnp.sum(z * z, axis=0, keepdims=True) * n_inv + epsilon)
                des.append(s * (ps[h] - pm - u_s[hr] * q))
            dz = jnp.concatenate(dzs, axis=0)
            de = jnp.concatenate(des, axis=0)
            g_col = gain[rows]
            gde = g_col * de
            t_t = shift[rows] + (kn - vn).T
            dg_out[rows] += lane_sum((2.0 * g_col * u_s[rows] + t_t) * de)
            dsh_out[rows] += lane_sum(gde)
            gden = gde.T
            dv_out[here, lanes] = -gden
            dzn = split(dz.T)
            dk = dk_out[here, lanes] + gden
            r_rows = []
            for hh in range(per):
                h = p * per + hh
                r_row = rate_t[h : h + 1, here]
                own = (row_head == hh).astype(bf16)
                own_lane = (lane_head == hh).astype(bf16)
                rt = mm(dzn, (gts[0] * own, gts[1] * own))
                dr_out[h : h + 1, here] -= jnp.sum(rt * sc_s[h], axis=0, keepdims=True)
                ra = rt * (before * r_row)
                dk = dk - mm(split(ra + ra.T), (ks[0] * own_lane, ks[1] * own_lane))
                r_rows.append(jnp.broadcast_to(r_row * in_last * (1.0 / MB), (hd, CH)))
            gw = g_t * jnp.concatenate(r_rows, axis=0)
            w0s = split(w0[rows])
            wd = split(w_in[c, rows] - w0[rows])
            zero = jnp.zeros((), bf16)
            dzn_c = (jnp.where(carried_col, dzn[0], zero), jnp.where(carried_col, dzn[1], zero))
            dk = dk + mm(dzn, w0s) + mm(dzn_c, wd) - mm(split(gw.T), split(dw_s[rows]))
            dk_out[here, lanes] = dk
            dzb = dzb_s[rows]
            dzc = jnp.where(carried, dz, 0.0)
            dzbc = jnp.where(carried, dzb, 0.0)
            diag = jnp.where(block_diag, mm(split(dzc), ks) + mm(split(dzbc), qs), 0.0)
            rest = jnp.where(
                block_diag, mm(split(dz - dzc), ks) + mm(split(dzb - dzbc), qs), 0.0
            )
            dw = dw_s[rows]
            db = db_s[rows]
            dw_out[rows] += jnp.where(whole, 0.0, dw) + rest
            db_out[rows] += jnp.where(whole, 0.0, db) + lane_sum(dz - dzc + dzb - dzbc)
            dw_s[rows] = jnp.where(whole, dw, 0.0) + diag
            db_s[rows] = jnp.where(whole, db, 0.0) + lane_sum(dzc + dzbc)
        return carry

    lax.fori_loop(0, chunks, chunk, 0)


def ttt_backward(joined, rate_t, seg, seg_t, w0, b0, gain, shift, saved, dy, hd, heads):
    length = joined.shape[0]
    span = heads * hd
    shape = jax.ShapeDtypeStruct
    return pl.pallas_call(
        functools.partial(backward_body, hd=hd, heads=heads),
        out_shape=(
            shape((length, span), f32),
            shape((length, span), f32),
            shape((length, span), f32),
            shape((heads, length), f32),
            shape((span, CH), f32),
            shape((span, 1), f32),
            shape((span, 1), f32),
            shape((span, 1), f32),
        ),
        scratch_shapes=[
            pltpu.VMEM((span, CH), f32),
            pltpu.VMEM((span, 1), f32),
        ]
        + [pltpu.VMEM((span, CH), f32)] * 8
        + [
            pltpu.VMEM((heads, CH, 2 * CH), bf16),
            pltpu.VMEM((heads, CH, CH), f32),
        ],
        compiler_params=pltpu.CompilerParams(vmem_limit_bytes=48 << 20),
        name="inner_backward",
    )(joined, rate_t, seg, seg_t, w0, b0, gain, shift, *saved, dy)


def state_in(inner_weight, inner_bias):
    heads, hd, _ = inner_weight.shape
    per = CH // hd
    w_t = jnp.swapaxes(inner_weight, 1, 2)
    w_t = w_t - jnp.mean(w_t, axis=1, keepdims=True)
    placed = [
        jnp.pad(w_t[h], ((0, 0), ((h % per) * hd, CH - hd - (h % per) * hd)))
        for h in range(heads)
    ]
    b = inner_bias - jnp.mean(inner_bias, axis=1, keepdims=True)
    return jnp.concatenate(placed, axis=0), b.reshape(heads * hd, 1)


def state_back(dw, db, heads, hd):
    per = CH // hd
    parts = [
        dw[h * hd : (h + 1) * hd, (h % per) * hd : (h % per + 1) * hd] for h in range(heads)
    ]
    d = jnp.stack(parts)
    d = jnp.swapaxes(d - jnp.mean(d, axis=1, keepdims=True), 1, 2)
    b = db.reshape(heads, hd)
    return d, b - jnp.mean(b, axis=1, keepdims=True)


def product(left, right):
    return jnp.dot(left, right, precision=lax.Precision.HIGH, preferred_element_type=f32)


def left_product(left, right):
    return lax.dot_general(
        left, right, (((0,), (0,)), ((), ())), precision=lax.Precision.HIGH,
        preferred_element_type=f32,
    )


def right_product(left, right):
    return lax.dot_general(
        left, right, (((1,), (1,)), ((), ())), precision=lax.Precision.HIGH,
        preferred_element_type=f32,
    )


def heads_grid():
    size = lax.axis_size("heads")
    deep = 4 if size % 4 == 0 else 1
    return deep, size // deep


def heads_place():
    _, across = heads_grid()
    index = lax.axis_index("heads")
    return index // across, index % across


def shift(value, dz, dx):
    deep, across = heads_grid()
    pairs = [
        (h, (h // across + dz) % deep * across + (h % across + dx) % across)
        for h in range(deep * across)
    ]
    return lax.ppermute(value, "heads", pairs)


def swap(value, axis, bit):
    return lax.ppermute(value, axis, [(i, i ^ bit) for i in range(lax.axis_size(axis))])


def row_shift(value, step):
    size = lax.axis_size("rows")
    return lax.ppermute(value, "rows", [(r, (r + 2 * step) % size) for r in range(size)])


def butterfly(value, axis):
    bit = 1
    while bit < lax.axis_size(axis):
        value = value + swap(value, axis, bit)
        bit *= 2
    return value


def small_gather(value):
    size = lax.axis_size("heads")
    place = jnp.arange(size) == lax.axis_index("heads")
    place = place.reshape((size,) + (1,) * value.ndim)
    return butterfly(jnp.where(place, value[None], 0.0), "heads")


def gather_columns(value, parts=2):
    deep, across = heads_grid()
    z, x = heads_place()
    rows, cols = value.shape
    size = rows // parts
    out = jnp.zeros((rows, cols * deep * across), value.dtype)
    moving = [value[i * size : (i + 1) * size] for i in range(parts)]
    for dz in range(deep):
        if dz:
            moving = [shift(item, 1, 0) for item in moving]
        side = moving
        for dx in range(across):
            if dx:
                side = [shift(item, 0, 1) for item in side]
            column = ((z - dz) % deep * across + (x - dx) % across) * cols
            for i in range(parts):
                out = lax.dynamic_update_slice(out, side[i], (i * size, column))
    return out


def scatter_columns(value, extra=None, parts=2):
    deep, across = heads_grid()
    z, x = heads_place()
    rows, width = value.shape
    cols = width // (deep * across)
    size = rows // parts

    def piece(i, dz, dx):
        column = ((z - dz) % deep * across + (x - dx) % across) * cols
        block = lax.dynamic_slice(value, (i * size, column), (size, cols))
        if extra is not None and i == parts - 1:
            tail = lax.dynamic_slice(extra, (0, column), (extra.shape[0], cols))
            block = jnp.concatenate([block, tail], 0)
        return block

    total = [None] * parts
    for dz in list(range(1, deep)) + [0]:
        for i in range(parts):
            here = None
            for dx in list(range(1, across)) + [0]:
                block = piece(i, dz, dx)
                here = block if here is None else shift(here, 0, 1) + block
            total[i] = here if total[i] is None else shift(total[i], 1, 0) + here
    return jnp.concatenate(total, 0)


def half_of(value, index, axis):
    size = value.shape[axis] // 2
    return lax.dynamic_slice_in_dim(value, index * size, size, axis)


def both_cores(value):
    return jnp.concatenate([value, swap(value, "rows", 1)], 0)


def tokens_half(value, core):
    return jnp.concatenate(
        [half_of(value, core, 1), swap(half_of(value, 1 - core, 1), "rows", 1)], 0
    )


def finish(part, core, axis):
    total = part
    for step in range(1, lax.axis_size("rows") // 2):
        total = total + row_shift(part, step)
    other = swap(total, "rows", 1)
    first = core == 0
    return jnp.concatenate(
        [jnp.where(first, total, other), jnp.where(first, other, total)], axis
    )


def silu_parts(a):
    sig = jax.nn.sigmoid(a)
    return a * sig, sig * (1.0 + a * (1.0 - sig))


def gelu_parts(v):
    k = 0.7978845608028654
    inner = k * (v + 0.044715 * v * v * v)
    th = jnp.tanh(inner)
    slope = 0.5 * (1.0 + th) + 0.5 * v * (1.0 - th * th) * k * (1.0 + 3 * 0.044715 * v * v)
    return 0.5 * v * (1.0 + th), slope


def on_device(
    stream,
    doc_starts,
    valid_mask,
    first_gain,
    w_query,
    w_key,
    w_value,
    w_rate,
    b_rate,
    inner_weight,
    inner_bias,
    inner_gain,
    inner_shift,
    post_gain,
    post_shift,
    w_gate_attn,
    w_out,
    second_gain,
    w_gate,
    w_up,
    w_down,
    cotangent,
):
    _, length, width = stream.shape
    tokens = stream.reshape(length, width)
    slab = second_gain.shape[0]
    column = lax.axis_index("heads") * slab
    core = lax.axis_index("rows") % 2
    heads, hd = inner_bias.shape
    span = heads * hd
    total_span = span * lax.axis_size("heads")
    gains = small_gather(jnp.stack([first_gain, second_gain]))
    gain_one = gains[:, 0].reshape(width)
    gain_two = gains[:, 1].reshape(width)
    grad_output = cotangent.reshape(length, slab)
    dy_full = gather_columns(grad_output)

    w_joined = jnp.concatenate([w_query, w_key, w_value, w_gate_attn, w_rate], axis=1)
    r1 = lax.rsqrt(jnp.mean(tokens * tokens, -1, keepdims=True) + epsilon)
    normed = tokens * r1 * gain_one
    joined = product(normed, w_joined)
    gate_pre = joined[:, 3 * span : 4 * span]
    sig = jax.nn.sigmoid(joined[:, 4 * span :] + b_rate)
    rate = sig / hd
    rate_t = rate.T
    seg = jnp.cumsum(doc_starts.reshape(length)).astype(f32)
    seg, seg_t = seg[:, None], seg[None]
    w0, b0 = state_in(inner_weight, inner_bias)
    gain_col, shift_col = inner_gain.reshape(span, 1), inner_shift.reshape(span, 1)
    mixed, *saved = ttt_forward(
        joined, rate, rate_t, seg, seg_t, w0, b0, gain_col, shift_col, hd, heads
    )
    row_sums = butterfly(jnp.stack([jnp.sum(mixed, 1), jnp.sum(mixed * mixed, 1)]), "heads")
    row_mean = row_sums[0] / total_span
    inv_std = lax.rsqrt(row_sums[1] / total_span - row_mean * row_mean + epsilon)[:, None]
    centered = (mixed - row_mean[:, None]) * inv_std
    shaped = centered * post_gain + post_shift
    gate_act, gate_slope = gelu_parts(gate_pre)
    gathered = gather_columns(gate_act * shaped)
    attn = product(gathered, w_out)
    stream_cols = lax.dynamic_slice_in_dim(tokens, column, slab, 1)
    hidden = stream_cols + attn
    whole = gather_columns(hidden)

    r2 = lax.rsqrt(jnp.mean(whole * whole, -1, keepdims=True) + epsilon)
    hnorm = whole * r2 * gain_two
    a = product(hnorm, w_gate)
    c = product(hnorm, w_up)
    act, slope = silu_parts(a)
    m = act * c
    ffn = scatter_columns(product(m, w_down))
    output = hidden + ffn
    dm = right_product(dy_full, w_down)
    da = dm * c * slope
    dc = dm * act
    dhnorm = right_product(da, w_gate) + right_product(dc, w_up)
    d_gain_two = jnp.sum(dhnorm * whole * r2, 0, keepdims=True)
    weighted = dhnorm * gain_two
    d_whole = r2 * weighted - whole * (r2 * r2 * r2) * jnp.mean(
        whole * weighted, -1, keepdims=True
    )
    pad = jnp.zeros((7, width), f32)
    d_part = scatter_columns(d_whole, jnp.concatenate([d_gain_two, pad], 0))
    d_hidden = grad_output + d_part[:length]
    d_gain_two = d_part[length]

    hnorm_pair = tokens_half(hnorm, core)
    g_gate = finish(left_product(hnorm_pair, both_cores(da)), core, 0)
    g_up = finish(left_product(hnorm_pair, both_cores(dc)), core, 0)
    g_down = finish(left_product(both_cores(m), tokens_half(dy_full, core)), core, 1)

    d_gated = scatter_columns(right_product(d_hidden, w_out))
    g_out = finish(left_product(tokens_half(gathered, core), both_cores(d_hidden)), core, 0)
    d_shaped = d_gated * gate_act
    d_gate_pre = d_gated * shaped * gate_slope
    d_post_gain = jnp.sum(d_shaped * centered, 0)
    d_post_shift = jnp.sum(d_shaped, 0)
    d_center = d_shaped * post_gain
    back_sums = butterfly(
        jnp.stack([jnp.sum(d_center, 1), jnp.sum(d_center * centered, 1)]), "heads"
    )
    d_mixed = inv_std * (
        d_center - back_sums[0][:, None] / total_span
        - centered * back_sums[1][:, None] / total_span
    )
    dq, dk, dv, d_rate, dw, db, dg, dsh = ttt_backward(
        joined, rate_t, seg, seg_t, w0, b0, gain_col, shift_col, saved, d_mixed, hd, heads
    )
    d_inner_weight, d_inner_bias = state_back(dw, db, heads, hd)
    d_rate_pre = d_rate.T * rate * (1.0 - sig)
    d_joined = jnp.concatenate([dq, dk, dv, d_gate_pre, d_rate_pre], 1)
    d_normed = right_product(d_joined, w_joined)
    d_gain_one = jnp.sum(d_normed * tokens * r1, 0, keepdims=True)
    weighted = d_normed * gain_one
    d_tokens = r1 * weighted - tokens * (r1 * r1 * r1) * jnp.mean(
        tokens * weighted, -1, keepdims=True
    )
    d_part = scatter_columns(d_tokens, jnp.concatenate([d_gain_one, pad], 0))
    d_stream = d_hidden + d_part[:length]
    d_gain_one = d_part[length]
    g_joined = finish(left_product(tokens_half(normed, core), both_cores(d_joined)), core, 0)

    weights = valid_mask.reshape(-1).astype(f32)[:, None]
    stats = jnp.stack(
        [
            jnp.sum(weights * member * member)
            for member in (stream_cols, attn, hidden, ffn, output)
        ]
        + [jnp.sum(weights) / lax.axis_size("heads")]
    )
    stats = butterfly(butterfly(stats, "rows"), "heads")
    rms_values = jnp.sqrt(stats[:5] / (stats[5] * width))
    small = [
        d_gain_one, jnp.sum(d_rate_pre, 0), d_inner_weight, d_inner_bias, dg, dsh,
        d_post_gain, d_post_shift, d_gain_two,
    ]
    packed = butterfly(jnp.concatenate([item.reshape(-1) for item in small]), "rows")
    parts = []
    at = 0
    for item in small:
        parts.append(packed[at : at + item.size])
        at += item.size
    return (
        output.reshape(1, length, slab),
        d_stream.reshape(1, length, slab),
        parts[0],
        g_joined[:, :span],
        g_joined[:, span : 2 * span],
        g_joined[:, 2 * span : 3 * span],
        g_joined[:, 4 * span :],
        parts[1],
        parts[2].reshape(heads, hd, hd),
        parts[3].reshape(heads, hd),
        parts[4].reshape(heads, hd),
        parts[5].reshape(heads, hd),
        parts[6],
        parts[7],
        g_joined[:, 3 * span : 4 * span],
        g_out,
        parts[8],
        g_gate,
        g_up,
        g_down,
        rms_values,
    )


def solution(mesh):
    in_specs = (
        P("rows", None, None),
        P("rows", None),
        P("rows", None),
        P("heads"),
        P(None, "heads"),
        P(None, "heads"),
        P(None, "heads"),
        P(None, "heads"),
        P("heads"),
        P("heads", None, None),
        P("heads", None),
        P("heads", None),
        P("heads", None),
        P("heads"),
        P("heads"),
        P(None, "heads"),
        P(None, "heads"),
        P("heads"),
        P(None, "heads"),
        P(None, "heads"),
        P("heads", None),
        P("rows", None, "heads"),
    )
    out_specs = (
        P("rows", None, "heads"),
        P("rows", None, "heads"),
        P("heads"),
        P(None, "heads"),
        P(None, "heads"),
        P(None, "heads"),
        P(None, "heads"),
        P("heads"),
        P("heads", None, None),
        P("heads", None),
        P("heads", None),
        P("heads", None),
        P("heads"),
        P("heads"),
        P(None, "heads"),
        P(None, "heads"),
        P("heads"),
        P(None, "heads"),
        P(None, "heads"),
        P("heads", None),
        P(),
    )
    return jax.shard_map(
        on_device, mesh=mesh, in_specs=in_specs, out_specs=out_specs, check_vma=False
    )
```

```python
import functools
import jax, jax.numpy as jnp
from jax import lax
from jax.experimental import pallas as pl
from jax.experimental.pallas import tpu as pltpu

from jax.sharding import PartitionSpec as P

MB = 16
CH = 128
epsilon = 1e-06
f32 = jnp.float32
bf16 = jnp.bfloat16
NN = ((1,), (0,))


def split(x):
    hi = x.astype(bf16)
    return hi, (x - hi.astype(f32)).astype(bf16)


def mm(a, b, dims=NN):
    def one(p, q):
        return lax.dot_general(p, q, (dims, ((), ())), preferred_element_type=f32)

    return one(a[0], b[0]) + (one(a[0], b[1]) + one(a[1], b[0]))


def wide(x):
    hi, lo = split(x)
    return jnp.concatenate([hi, lo], axis=1)


def tall_dot(x, pair):
    rows = x.shape[0]
    cols = pair.shape[1] // 2
    hi, lo = split(x)
    out = lax.dot_general(
        jnp.concatenate([hi, lo], axis=0), pair, (NN, ((), ())), preferred_element_type=f32
    )
    top, low = out[:rows], out[rows:]
    return top[:, :cols] + (top[:, cols:] + low[:, :cols])


def iota(shape, dim):
    return lax.broadcasted_iota(jnp.int32, shape, dim)


def head_sum(x, hd):
    rows, cols = x.shape
    parts = [
        jnp.broadcast_to(jnp.sum(x[i : i + hd], axis=0, keepdims=True), (hd, cols))
        for i in range(0, rows, hd)
    ]
    return parts[0] if len(parts) == 1 else jnp.concatenate(parts, axis=0)


def lane_sum(x):
    return jnp.sum(x, axis=1, keepdims=True)


def coefficients(transposed):
    source = iota((CH, CH), 1 if transposed else 0)
    target = iota((CH, CH), 0 if transposed else 1)
    before = (source // MB < target // MB).astype(f32) * (1.0 / MB)
    inside = ((source // MB == target // MB) & (source <= target)).astype(f32)
    return before, before + inside / ((target % MB) + 1).astype(f32)


def forward_body(
    joined, rate, rate_t, seg, seg_t, w0, b0, gain, shift, mixed, z_out, zb_out, w_out, b_out,
    w_s, b_s, z_s, tau_s, a_s, m_s, *, hd, heads,
):
    pairs = heads * hd // CH
    per = CH // hd
    span = heads * hd
    chunks = joined.shape[0] // CH
    n_inv = 1.0 / hd
    row_head = iota((CH, CH), 0) // hd
    lane_head = iota((CH, CH), 1) // hd
    lane_block = iota((hd, CH), 1) // MB
    block_diag = row_head == lane_head
    w_s[...] = jnp.zeros_like(w_s)
    b_s[...] = jnp.zeros_like(b_s)

    def chunk(c, carry):
        ts = pl.multiple_of(c * CH, CH)
        here = pl.ds(ts, CH)
        seg_row = seg_t[:, here]
        seg_col = seg[here, :]
        last_seg = seg_row[:, CH - 1 : CH]
        prev = jnp.max(jnp.where(iota(seg_t.shape, 1) < ts, seg_t[...], 0.0), keepdims=True)
        carried = seg_row == prev
        in_last = (seg_row == last_seg).astype(f32)
        whole = last_seg == prev
        same = seg_col == seg_row
        before, within = coefficients(False)
        before = jnp.where(same, before, 0.0)
        within = jnp.where(same, within, 0.0)
        for p in range(pairs):
            rows = slice(p * CH, (p + 1) * CH)
            kn = joined[here, span + p * CH : span + (p + 1) * CH]
            qn = joined[here, p * CH : (p + 1) * CH]
            vn = joined[here, 2 * span + p * CH : 2 * span + (p + 1) * CH]
            k_t, q_t, v_t = kn.T, qn.T, vn.T
            ks, kts, qts = split(kn), split(k_t), split(q_t)
            ws, w0s = split(w_s[rows]), split(w0[rows])
            bias = jnp.where(carried, b_s[rows], b0[rows])
            z_s[rows] = jnp.where(carried, mm(ws, kts), mm(w0s, kts)) + bias
            zb_out[rows, here] = jnp.where(carried, mm(ws, qts), mm(w0s, qts)) + bias
            w_out[c, rows] = w_s[rows]
            b_out[c, rows] = b_s[rows]
            tau_s[rows] = gain[rows] * (shift[rows] - v_t + k_t)
            for hh in range(per):
                h = p * per + hh
                own = (row_head == hh).astype(bf16)
                r_col = rate[here, h : h + 1]
                score = mm(ks, (kts[0] * own, kts[1] * own))
                a_s[h] = wide((score + 1.0) * (before * r_col))
                score = mm(ks, (qts[0] * own, qts[1] * own))
                m_s[h] = wide((score + 1.0) * (within * r_col))

        gsq = [jnp.broadcast_to(gain[h * hd : (h + 1) * hd] ** 2, (hd, CH)) for h in range(heads)]
        tsum = [
            jnp.sum(tau_s[h * hd : (h + 1) * hd], axis=0, keepdims=True) * n_inv
            for h in range(heads)
        ]

        def inner(h, z):
            tau = tau_s[h * hd : (h + 1) * hd]
            zg = z * gsq[h]
            m2 = jnp.sum(z * z, axis=0, keepdims=True) * n_inv
            a1 = jnp.sum(zg, axis=0, keepdims=True) * n_inv
            a2 = jnp.sum(z * zg, axis=0, keepdims=True) * n_inv
            a3 = jnp.sum(z * tau, axis=0, keepdims=True) * n_inv
            s = lax.rsqrt(m2 + epsilon)
            c_eu = s * (s * a2 + a3)
            e_mean = s * a1 + tsum[h]
            return (s * s) * (zg - c_eu * z) + s * (tau - e_mean)

        def step(t, zs):
            now = lane_block == t
            new = []
            for h in range(heads):
                g = jnp.where(now, inner(h, zs[h]), 0.0)
                new.append(zs[h] - tall_dot(g, a_s[h]))
            return tuple(new)

        zs = tuple(z_s[h * hd : (h + 1) * hd] for h in range(heads))
        zs = lax.fori_loop(0, CH // MB - 1, step, zs)
        for p in range(pairs):
            rows = slice(p * CH, (p + 1) * CH)
            gs = []
            outs = []
            for hh in range(per):
                h = p * per + hh
                hr = slice(h * hd, (h + 1) * hd)
                z_out[hr, here] = zs[h]
                g = inner(h, zs[h])
                zb = zb_out[hr, here] - tall_dot(g, m_s[h])
                zb_out[hr, here] = zb
                sb = lax.rsqrt(jnp.sum(zb * zb, axis=0, keepdims=True) * n_inv + epsilon)
                outs.append(zb * sb * gain[hr] + shift[hr])
                gs.append(g * (rate_t[h : h + 1, here] * in_last * (1.0 / MB)))
            gw = jnp.concatenate(gs, axis=0)
            lanes = slice(p * CH, (p + 1) * CH)
            mixed[here, lanes] = joined[here, lanes] + jnp.concatenate(outs, axis=0).T
            kn = joined[here, span + p * CH : span + (p + 1) * CH]
            upd = mm(split(gw), split(kn))
            w_s[rows] = jnp.where(whole, w_s[rows], w0[rows]) - jnp.where(block_diag, upd, 0.0)
            b_s[rows] = jnp.where(whole, b_s[rows], b0[rows]) - lane_sum(gw)
        return carry

    lax.fori_loop(0, chunks, chunk, 0)


def ttt_forward(joined, rate, rate_t, seg, seg_t, w0, b0, gain, shift, hd, heads):
    length = joined.shape[0]
    span = heads * hd
    chunks = length // CH
    shape = jax.ShapeDtypeStruct
    return pl.pallas_call(
        functools.partial(forward_body, hd=hd, heads=heads),
        out_shape=(
            shape((length, span), f32),
            shape((span, length), f32),
            shape((span, length), f32),
            shape((chunks, span, CH), f32),
            shape((chunks, span, 1), f32),
        ),
        scratch_shapes=[
            pltpu.VMEM((span, CH), f32),
            pltpu.VMEM((span, 1), f32),
            pltpu.VMEM((span, CH), f32),
            pltpu.VMEM((span, CH), f32),
            pltpu.VMEM((heads, CH, 2 * CH), bf16),
            pltpu.VMEM((heads, CH, 2 * CH), bf16),
        ],
        compiler_params=pltpu.CompilerParams(vmem_limit_bytes=48 << 20),
        name="inner_forward",
    )(joined, rate, rate_t, seg, seg_t, w0, b0, gain, shift)


def backward_body(
    joined, rate_t, seg, seg_t, w0, b0, gain, shift, z_in, zb_in, w_in, b_in, dy,
    dq_out, dk_out, dv_out, dr_out, dw_out, db_out, dg_out, dsh_out,
    dw_s, db_s, p_s, u_s, f_s, bb_s, e2_s, u2_s, gt_s, dzb_s, at_s, sc_s,
    *, hd, heads,
):
    pairs = heads * hd // CH
    per = CH // hd
    span = heads * hd
    chunks = joined.shape[0] // CH
    n_inv = 1.0 / hd
    row_head = iota((CH, CH), 0) // hd
    lane_head = iota((CH, CH), 1) // hd
    lane_block = iota((hd, CH), 1) // MB
    block_diag = row_head == lane_head
    for ref in (dw_s, db_s, dw_out, db_out, dg_out, dsh_out):
        ref[...] = jnp.zeros_like(ref)

    def mean(x):
        return head_sum(x, hd) * n_inv

    def chunk(index, carry):
        c = chunks - 1 - index
        ts = pl.multiple_of(c * CH, CH)
        here = pl.ds(ts, CH)
        seg_row = seg_t[:, here]
        seg_col = seg[here, :]
        last_seg = seg_row[:, CH - 1 : CH]
        prev = jnp.max(jnp.where(iota(seg_t.shape, 1) < ts, seg_t[...], 0.0), keepdims=True)
        carried = seg_row == prev
        carried_col = seg_col == prev
        in_last = (seg_row == last_seg).astype(f32)
        whole = last_seg == prev
        same = seg_col == seg_row
        before, within = coefficients(True)
        before = jnp.where(same, before, 0.0)
        within = jnp.where(same, within, 0.0)
        consts = {}
        for p in range(pairs):
            rows = slice(p * CH, (p + 1) * CH)
            lanes = slice(p * CH, (p + 1) * CH)
            qn = joined[here, p * CH : (p + 1) * CH]
            kn = joined[here, span + p * CH : span + (p + 1) * CH]
            vn = joined[here, 2 * span + p * CH : 2 * span + (p + 1) * CH]
            k_t, v_t, dy_t = kn.T, vn.T, dy[here, lanes].T
            qs, ks, kts = split(qn), split(kn), split(k_t)
            g_col = gain[rows]
            gsq = g_col * g_col
            zb = zb_in[rows, here]
            sb = lax.rsqrt(mean(zb * zb) + epsilon)
            ub = zb * sb
            dg_out[rows] += lane_sum(dy_t * ub)
            dsh_out[rows] += lane_sum(dy_t)
            pb = dy_t * g_col
            dzb = sb * (pb - mean(pb) - ub * mean(pb * ub))
            dzb_s[rows] = dzb
            z = z_in[rows, here]
            s = lax.rsqrt(mean(z * z) + epsilon)
            u = z * s
            gu = gsq * u
            e = gu + g_col * (shift[rows] - v_t + k_t)
            c_eu = mean(e * u)
            g_t = s * (e - mean(e) - u * c_eu)
            gt_s[rows] = g_t
            u_s[rows] = u
            f_s[rows] = g_t + s * gu
            bb_s[rows] = (s * s) * (gsq - c_eu)
            e2_s[rows] = (s * s) * (e + gu)
            u2_s[rows] = s * u
            h1 = s * mean(gu)
            h2 = 2.0 * s * c_eu + s * mean(gu * u)
            dzbs = split(dzb)
            gts = split(g_t)
            dzbn = split(dzb.T)
            from_state = mm(split(dw_s[rows]), kts) + db_s[rows]
            pieces = []
            dq = dy[here, lanes]
            dk = jnp.zeros((CH, CH), f32)
            for hh in range(per):
                h = p * per + hh
                hr = slice(hh * hd, (hh + 1) * hd)
                r_row = rate_t[h : h + 1, here]
                consts[h] = (h1[hh * hd : hh * hd + 1], h2[hh * hd : hh * hd + 1])
                own = (row_head == hh).astype(bf16)
                own_lane = (lane_head == hh).astype(bf16)
                kt_h = (kts[0] * own, kts[1] * own)
                sc = (mm(ks, kt_h) + 1.0) * before
                sc_s[h] = sc
                at_s[h] = wide(sc * r_row)
                scq = (mm(qs, kt_h) + 1.0) * within
                pt = mm(dzbn, (gts[0] * own, gts[1] * own))
                dr_out[h : h + 1, here] = -jnp.sum(pt * scq, axis=0, keepdims=True) - (
                    (1.0 / MB) * in_last
                ) * jnp.sum(g_t[hr] * from_state[hr], axis=0, keepdims=True)
                pm = pt * (within * r_row)
                pms = split(pm)
                pmts = split(pm.T)
                kn_h = (ks[0] * own_lane, ks[1] * own_lane)
                qn_h = (qs[0] * own_lane, qs[1] * own_lane)
                dq = dq - mm(pms, kn_h)
                dk = dk - mm(pmts, qn_h)
                pieces.append(
                    -mm((dzbs[0][hr], dzbs[1][hr]), split(scq * r_row))
                    - from_state[hr] * (r_row * in_last * (1.0 / MB))
                )
            p_s[rows] = jnp.concatenate(pieces, axis=0)
            w0s = split(w0[rows])
            wd = split(w_in[c, rows] - w0[rows])
            zero = jnp.zeros((), bf16)
            dzbn_c = (jnp.where(carried_col, dzbn[0], zero), jnp.where(carried_col, dzbn[1], zero))
            dq_out[here, lanes] = dq + mm(dzbn, w0s) + mm(dzbn_c, wd)
            dk_out[here, lanes] = dk

        def upstream(h, pv):
            hr = slice(h * hd, (h + 1) * hd)
            h1, h2 = consts[h]
            pm = jnp.sum(pv, axis=0, keepdims=True) * n_inv
            q = jnp.sum(pv * u_s[hr], axis=0, keepdims=True) * n_inv
            kf = jnp.sum(pv * f_s[hr], axis=0, keepdims=True) * n_inv
            kappa = kf - h1 * pm - h2 * q
            dz = (pv - pm) * bb_s[hr] - q * e2_s[hr] - kappa * u2_s[hr]
            return dz, pm, q

        def step(index, ps):
            now = lane_block == (CH // MB - 1 - index)
            new = []
            for h in range(heads):
                dz = jnp.where(now, upstream(h, ps[h])[0], 0.0)
                new.append(ps[h] - tall_dot(dz, at_s[h]))
            return tuple(new)

        ps = tuple(p_s[h * hd : (h + 1) * hd] for h in range(heads))
        ps = lax.fori_loop(0, CH // MB - 1, step, ps)

        for p in range(pairs):
            rows = slice(p * CH, (p + 1) * CH)
            lanes = slice(p * CH, (p + 1) * CH)
            qn = joined[here, p * CH : (p + 1) * CH]
            kn = joined[here, span + p * CH : span + (p + 1) * CH]
            vn = joined[here, 2 * span + p * CH : 2 * span + (p + 1) * CH]
            qs, ks = split(qn), split(kn)
            g_t = gt_s[rows]
            gts = split(g_t)
            dzs, des = [], []
            for hh in range(per):
                h = p * per + hh
                hr = slice(h * hd, (h + 1) * hd)
                dz, pm, q = upstream(h, ps[h])
                dzs.append(dz - jnp.sum(dz, axis=0, keepdims=True) * n_inv)
                z = z_in[hr, here]
                s = lax.rsqrt(jnp.sum(z * z, axis=0, keepdims=True) * n_inv + epsilon)
                des.append(s * (ps[h] - pm - u_s[hr] * q))
            dz = jnp.concatenate(dzs, axis=0)
            de = jnp.concatenate(des, axis=0)
            g_col = gain[rows]
            gde = g_col * de
            t_t = shift[rows] + (kn - vn).T
            dg_out[rows] += lane_sum((2.0 * g_col * u_s[rows] + t_t) * de)
            dsh_out[rows] += lane_sum(gde)
            gden = gde.T
            dv_out[here, lanes] = -gden
            dzn = split(dz.T)
            dk = dk_out[here, lanes] + gden
            r_rows = []
            for hh in range(per):
                h = p * per + hh
                r_row = rate_t[h : h + 1, here]
                own = (row_head == hh).astype(bf16)
                own_lane = (lane_head == hh).astype(bf16)
                rt = mm(dzn, (gts[0] * own, gts[1] * own))
                dr_out[h : h + 1, here] -= jnp.sum(rt * sc_s[h], axis=0, keepdims=True)
                ra = rt * (before * r_row)
                dk = dk - mm(split(ra + ra.T), (ks[0] * own_lane, ks[1] * own_lane))
                r_rows.append(jnp.broadcast_to(r_row * in_last * (1.0 / MB), (hd, CH)))
            gw = g_t * jnp.concatenate(r_rows, axis=0)
            w0s = split(w0[rows])
            wd = split(w_in[c, rows] - w0[rows])
            zero = jnp.zeros((), bf16)
            dzn_c = (jnp.where(carried_col, dzn[0], zero), jnp.where(carried_col, dzn[1], zero))
            dk = dk + mm(dzn, w0s) + mm(dzn_c, wd) - mm(split(gw.T), split(dw_s[rows]))
            dk_out[here, lanes] = dk
            dzb = dzb_s[rows]
            dzc = jnp.where(carried, dz, 0.0)
            dzbc = jnp.where(carried, dzb, 0.0)
            diag = jnp.where(block_diag, mm(split(dzc), ks) + mm(split(dzbc), qs), 0.0)
            rest = jnp.where(
                block_diag, mm(split(dz - dzc), ks) + mm(split(dzb - dzbc), qs), 0.0
            )
            dw = dw_s[rows]
            db = db_s[rows]
            dw_out[rows] += jnp.where(whole, 0.0, dw) + rest
            db_out[rows] += jnp.where(whole, 0.0, db) + lane_sum(dz - dzc + dzb - dzbc)
            dw_s[rows] = jnp.where(whole, dw, 0.0) + diag
            db_s[rows] = jnp.where(whole, db, 0.0) + lane_sum(dzc + dzbc)
        return carry

    lax.fori_loop(0, chunks, chunk, 0)


def ttt_backward(joined, rate_t, seg, seg_t, w0, b0, gain, shift, saved, dy, hd, heads):
    length = joined.shape[0]
    span = heads * hd
    shape = jax.ShapeDtypeStruct
    return pl.pallas_call(
        functools.partial(backward_body, hd=hd, heads=heads),
        out_shape=(
            shape((length, span), f32),
            shape((length, span), f32),
            shape((length, span), f32),
            shape((heads, length), f32),
            shape((span, CH), f32),
            shape((span, 1), f32),
            shape((span, 1), f32),
            shape((span, 1), f32),
        ),
        scratch_shapes=[
            pltpu.VMEM((span, CH), f32),
            pltpu.VMEM((span, 1), f32),
        ]
        + [pltpu.VMEM((span, CH), f32)] * 8
        + [
            pltpu.VMEM((heads, CH, 2 * CH), bf16),
            pltpu.VMEM((heads, CH, CH), f32),
        ],
        compiler_params=pltpu.CompilerParams(vmem_limit_bytes=48 << 20),
        name="inner_backward",
    )(joined, rate_t, seg, seg_t, w0, b0, gain, shift, *saved, dy)


def state_in(inner_weight, inner_bias):
    heads, hd, _ = inner_weight.shape
    per = CH // hd
    w_t = jnp.swapaxes(inner_weight, 1, 2)
    w_t = w_t - jnp.mean(w_t, axis=1, keepdims=True)
    placed = [
        jnp.pad(w_t[h], ((0, 0), ((h % per) * hd, CH - hd - (h % per) * hd)))
        for h in range(heads)
    ]
    b = inner_bias - jnp.mean(inner_bias, axis=1, keepdims=True)
    return jnp.concatenate(placed, axis=0), b.reshape(heads * hd, 1)


def state_back(dw, db, heads, hd):
    per = CH // hd
    parts = [
        dw[h * hd : (h + 1) * hd, (h % per) * hd : (h % per + 1) * hd] for h in range(heads)
    ]
    d = jnp.stack(parts)
    d = jnp.swapaxes(d - jnp.mean(d, axis=1, keepdims=True), 1, 2)
    b = db.reshape(heads, hd)
    return d, b - jnp.mean(b, axis=1, keepdims=True)


def product(left, right):
    return jnp.dot(left, right, precision=lax.Precision.HIGH, preferred_element_type=f32)


def left_product(left, right):
    return lax.dot_general(
        left, right, (((0,), (0,)), ((), ())), precision=lax.Precision.HIGH,
        preferred_element_type=f32,
    )


def right_product(left, right):
    return lax.dot_general(
        left, right, (((1,), (1,)), ((), ())), precision=lax.Precision.HIGH,
        preferred_element_type=f32,
    )


def heads_grid():
    size = lax.axis_size("heads")
    deep = 4 if size % 4 == 0 else 1
    return deep, size // deep


def heads_place():
    _, across = heads_grid()
    index = lax.axis_index("heads")
    return index // across, index % across


def shift(value, dz, dx):
    deep, across = heads_grid()
    pairs = [
        (h, (h // across + dz) % deep * across + (h % across + dx) % across)
        for h in range(deep * across)
    ]
    return lax.ppermute(value, "heads", pairs)


def swap(value, axis, bit):
    return lax.ppermute(value, axis, [(i, i ^ bit) for i in range(lax.axis_size(axis))])


def row_shift(value, step):
    size = lax.axis_size("rows")
    return lax.ppermute(value, "rows", [(r, (r + 2 * step) % size) for r in range(size)])


def butterfly(value, axis):
    bit = 1
    while bit < lax.axis_size(axis):
        value = value + swap(value, axis, bit)
        bit *= 2
    return value


def small_gather(value):
    size = lax.axis_size("heads")
    place = jnp.arange(size) == lax.axis_index("heads")
    place = place.reshape((size,) + (1,) * value.ndim)
    return butterfly(jnp.where(place, value[None], 0.0), "heads")


def gather_columns(value, parts=2):
    deep, across = heads_grid()
    z, x = heads_place()
    rows, cols = value.shape
    size = rows // parts
    out = jnp.zeros((rows, cols * deep * across), value.dtype)
    moving = [value[i * size : (i + 1) * size] for i in range(parts)]
    for dz in range(deep):
        if dz:
            moving = [shift(item, 1, 0) for item in moving]
        side = moving
        for dx in range(across):
            if dx:
                side = [shift(item, 0, 1) for item in side]
            column = ((z - dz) % deep * across + (x - dx) % across) * cols
            for i in range(parts):
                out = lax.dynamic_update_slice(out, side[i], (i * size, column))
    return out


def scatter_columns(value, extra=None, parts=2):
    deep, across = heads_grid()
    z, x = heads_place()
    rows, width = value.shape
    cols = width // (deep * across)
    size = rows // parts

    def piece(i, dz, dx):
        column = ((z - dz) % deep * across + (x - dx) % across) * cols
        block = lax.dynamic_slice(value, (i * size, column), (size, cols))
        if extra is not None and i == parts - 1:
            tail = lax.dynamic_slice(extra, (0, column), (extra.shape[0], cols))
            block = jnp.concatenate([block, tail], 0)
        return block

    total = [None] * parts
    for dz in list(range(1, deep)) + [0]:
        for i in range(parts):
            here = None
            for dx in list(range(1, across)) + [0]:
                block = piece(i, dz, dx)
                here = block if here is None else shift(here, 0, 1) + block
            total[i] = here if total[i] is None else shift(total[i], 1, 0) + here
    return jnp.concatenate(total, 0)


def half_of(value, index, axis):
    size = value.shape[axis] // 2
    return lax.dynamic_slice_in_dim(value, index * size, size, axis)


def both_cores(value):
    return jnp.concatenate([value, swap(value, "rows", 1)], 0)


def tokens_half(value, core):
    return jnp.concatenate(
        [half_of(value, core, 1), swap(half_of(value, 1 - core, 1), "rows", 1)], 0
    )


def chips_along():
    return lax.axis_size("rows") // 2


def other_chips(value):
    return [row_shift(value, step) for step in range(1, chips_along())]


def place_body(own, other, *rest, axis, widths):
    outs, sems = rest[:-1], rest[-1]
    core = lax.axis_index("rows") % 2
    size = own.shape[axis]
    copies = []
    at = 0
    for i, (out, width) in enumerate(zip(outs, widths)):
        for j, ref in enumerate((own, other)):
            start = pl.multiple_of((core if j == 0 else 1 - core) * size, 128)
            if axis == 0:
                src, dst = ref.at[:, pl.ds(at, width)], out.at[pl.ds(start, size), :]
            else:
                src, dst = ref, out.at[:, pl.ds(start, size)]
            copies.append(pltpu.make_async_copy(src, dst, sems.at[2 * i + j]))
        at += width
    for copy in copies:
        copy.start()
    for copy in copies:
        copy.wait()


def place(own, other, axis, widths):
    rows, cols = own.shape
    if axis == 0:
        shapes = [(2 * rows, width) for width in widths]
    else:
        shapes = [(rows, 2 * cols)]
    hbm = pl.BlockSpec(memory_space=pl.ANY)
    out = pl.pallas_call(
        functools.partial(place_body, axis=axis, widths=widths),
        out_shape=[jax.ShapeDtypeStruct(shape, f32) for shape in shapes],
        in_specs=[hbm, hbm],
        out_specs=[hbm] * len(shapes),
        scratch_shapes=[pltpu.SemaphoreType.DMA((2 * len(shapes),))],
        name="place",
    )(own, other)
    return out


def finish(total, axis, widths=None):
    other = swap(total, "rows", 1)
    widths = (total.shape[1],) if widths is None else widths
    return place(total, other, axis, widths), other


def row_products(lefts, rights):
    total = None
    for left, right in zip(lefts, rights):
        part = left_product(left, both_cores(right))
        total = part if total is None else total + part
    return total


def silu_parts(a):
    sig = jax.nn.sigmoid(a)
    return a * sig, sig * (1.0 + a * (1.0 - sig))


def gelu_parts(v):
    k = 0.7978845608028654
    inner = k * (v + 0.044715 * v * v * v)
    th = jnp.tanh(inner)
    slope = 0.5 * (1.0 + th) + 0.5 * v * (1.0 - th * th) * k * (1.0 + 3 * 0.044715 * v * v)
    return 0.5 * v * (1.0 + th), slope


def on_device(
    stream,
    doc_starts,
    valid_mask,
    first_gain,
    w_query,
    w_key,
    w_value,
    w_rate,
    b_rate,
    inner_weight,
    inner_bias,
    inner_gain,
    inner_shift,
    post_gain,
    post_shift,
    w_gate_attn,
    w_out,
    second_gain,
    w_gate,
    w_up,
    w_down,
    cotangent,
):
    _, length, width = stream.shape
    tokens = stream.reshape(length, width)
    slab = second_gain.shape[0]
    column = lax.axis_index("heads") * slab
    core = lax.axis_index("rows") % 2
    heads, hd = inner_bias.shape
    span = heads * hd
    total_span = span * lax.axis_size("heads")
    gains = small_gather(jnp.stack([first_gain, second_gain]))
    gain_one = gains[:, 0].reshape(width)
    gain_two = gains[:, 1].reshape(width)
    grad_output = cotangent.reshape(length, slab)
    dy_full = gather_columns(grad_output)

    w_joined = jnp.concatenate([w_query, w_key, w_value, w_gate_attn, w_rate], axis=1)
    r1 = lax.rsqrt(jnp.mean(tokens * tokens, -1, keepdims=True) + epsilon)
    unit = tokens * r1
    unit_pair = tokens_half(unit, core)
    unit_pairs = [unit_pair] + other_chips(unit_pair)
    normed = unit * gain_one
    joined = product(normed, w_joined)
    gate_pre = joined[:, 3 * span : 4 * span]
    sig = jax.nn.sigmoid(joined[:, 4 * span :] + b_rate)
    rate = sig / hd
    rate_t = rate.T
    seg = jnp.cumsum(doc_starts.reshape(length)).astype(f32)
    seg, seg_t = seg[:, None], seg[None]
    w0, b0 = state_in(inner_weight, inner_bias)
    gain_col, shift_col = inner_gain.reshape(span, 1), inner_shift.reshape(span, 1)
    mixed, *saved = ttt_forward(
        joined, rate, rate_t, seg, seg_t, w0, b0, gain_col, shift_col, hd, heads
    )
    row_sums = butterfly(jnp.stack([jnp.sum(mixed, 1), jnp.sum(mixed * mixed, 1)]), "heads")
    row_mean = row_sums[0] / total_span
    inv_std = lax.rsqrt(row_sums[1] / total_span - row_mean * row_mean + epsilon)[:, None]
    centered = (mixed - row_mean[:, None]) * inv_std
    shaped = centered * post_gain + post_shift
    gate_act, gate_slope = gelu_parts(gate_pre)
    gathered = gather_columns(gate_act * shaped)
    gathered_pair = tokens_half(gathered, core)
    gathered_pairs = [gathered_pair] + other_chips(gathered_pair)
    attn = product(gathered, w_out)
    stream_cols = lax.dynamic_slice_in_dim(tokens, column, slab, 1)
    hidden = stream_cols + attn
    whole = gather_columns(hidden)

    r2 = lax.rsqrt(jnp.mean(whole * whole, -1, keepdims=True) + epsilon)
    hnorm = whole * r2 * gain_two
    hnorm_pair = tokens_half(hnorm, core)
    hnorm_pairs = [hnorm_pair] + other_chips(hnorm_pair)
    a = product(hnorm, w_gate)
    c = product(hnorm, w_up)
    act, slope = silu_parts(a)
    m = act * c
    ffn = scatter_columns(product(m, w_down))
    output = hidden + ffn
    dm = right_product(dy_full, w_down)
    da = dm * c * slope
    dc = dm * act
    dhnorm = right_product(da, w_gate) + right_product(dc, w_up)
    d_gain_two = jnp.sum(dhnorm * whole * r2, 0, keepdims=True)
    weighted = dhnorm * gain_two
    d_whole = r2 * weighted - whole * (r2 * r2 * r2) * jnp.mean(
        whole * weighted, -1, keepdims=True
    )
    pad = jnp.zeros((7, width), f32)
    d_part = scatter_columns(d_whole, jnp.concatenate([d_gain_two, pad], 0))
    d_hidden = grad_output + d_part[:length]
    d_gain_two = d_part[length]

    (g_gate,), _ = finish(row_products(hnorm_pairs, [da] + other_chips(da)), 0)
    (g_up,), _ = finish(row_products(hnorm_pairs, [dc] + other_chips(dc)), 0)
    g_down = left_product(both_cores(m), tokens_half(dy_full, core))

    d_gated = scatter_columns(right_product(d_hidden, w_out))
    (g_out,), _ = finish(row_products(gathered_pairs, [d_hidden] + other_chips(d_hidden)), 0)
    d_shaped = d_gated * gate_act
    d_gate_pre = d_gated * shaped * gate_slope
    d_post_gain = jnp.sum(d_shaped * centered, 0)
    d_post_shift = jnp.sum(d_shaped, 0)
    d_center = d_shaped * post_gain
    back_sums = butterfly(
        jnp.stack([jnp.sum(d_center, 1), jnp.sum(d_center * centered, 1)]), "heads"
    )
    d_mixed = inv_std * (
        d_center - back_sums[0][:, None] / total_span
        - centered * back_sums[1][:, None] / total_span
    )
    dq, dk, dv, d_rate, dw, db, dg, dsh = ttt_backward(
        joined, rate_t, seg, seg_t, w0, b0, gain_col, shift_col, saved, d_mixed, hd, heads
    )
    d_inner_weight, d_inner_bias = state_back(dw, db, heads, hd)
    d_rate_pre = d_rate.T * rate * (1.0 - sig)
    d_joined = jnp.concatenate([dq, dk, dv, d_gate_pre, d_rate_pre], 1)
    d_normed = right_product(d_joined, w_joined)
    d_gain_one = jnp.sum(d_normed * tokens * r1, 0, keepdims=True)
    weighted = d_normed * gain_one
    d_tokens = r1 * weighted - tokens * (r1 * r1 * r1) * jnp.mean(
        tokens * weighted, -1, keepdims=True
    )
    d_part = scatter_columns(d_tokens, jnp.concatenate([d_gain_one, pad], 0))
    d_stream = d_hidden + d_part[:length]
    d_gain_one = d_part[length]
    gain_half = half_of(gain_one, core, 0)
    g_joined = row_products(
        [pair * gain_half for pair in unit_pairs], [d_joined] + other_chips(d_joined)
    )
    (g_query, g_key, g_value, g_gate_attn), other = finish(g_joined, 0, (span,) * 4)
    ends = (g_joined[:, 4 * span :], other[:, 4 * span :])
    g_rate = jnp.where(
        core == 0, jnp.concatenate(ends, 0), jnp.concatenate(ends[::-1], 0)
    )
    g_down = sum(other_chips(g_down), g_down)
    (g_down,), _ = finish(g_down, 1)

    weights = valid_mask.reshape(-1).astype(f32)[:, None]
    stats = jnp.stack(
        [
            jnp.sum(weights * member * member)
            for member in (stream_cols, attn, hidden, ffn, output)
        ]
        + [jnp.sum(weights) / lax.axis_size("heads")]
    )
    stats = butterfly(butterfly(stats, "rows"), "heads")
    rms_values = jnp.sqrt(stats[:5] / (stats[5] * width))
    small = [
        d_gain_one, jnp.sum(d_rate_pre, 0), d_inner_weight, d_inner_bias, dg, dsh,
        d_post_gain, d_post_shift, d_gain_two,
    ]
    packed = butterfly(jnp.concatenate([item.reshape(-1) for item in small]), "rows")
    parts = []
    at = 0
    for item in small:
        parts.append(packed[at : at + item.size])
        at += item.size
    return (
        output.reshape(1, length, slab),
        d_stream.reshape(1, length, slab),
        parts[0],
        g_query,
        g_key,
        g_value,
        g_rate,
        parts[1],
        parts[2].reshape(heads, hd, hd),
        parts[3].reshape(heads, hd),
        parts[4].reshape(heads, hd),
        parts[5].reshape(heads, hd),
        parts[6],
        parts[7],
        g_gate_attn,
        g_out,
        parts[8],
        g_gate,
        g_up,
        g_down,
        rms_values,
    )


def solution(mesh):
    in_specs = (
        P("rows", None, None),
        P("rows", None),
        P("rows", None),
        P("heads"),
        P(None, "heads"),
        P(None, "heads"),
        P(None, "heads"),
        P(None, "heads"),
        P("heads"),
        P("heads", None, None),
        P("heads", None),
        P("heads", None),
        P("heads", None),
        P("heads"),
        P("heads"),
        P(None, "heads"),
        P(None, "heads"),
        P("heads"),
        P(None, "heads"),
        P(None, "heads"),
        P("heads", None),
        P("rows", None, "heads"),
    )
    out_specs = (
        P("rows", None, "heads"),
        P("rows", None, "heads"),
        P("heads"),
        P(None, "heads"),
        P(None, "heads"),
        P(None, "heads"),
        P(None, "heads"),
        P("heads"),
        P("heads", None, None),
        P("heads", None),
        P("heads", None),
        P("heads", None),
        P("heads"),
        P("heads"),
        P(None, "heads"),
        P(None, "heads"),
        P("heads"),
        P(None, "heads"),
        P(None, "heads"),
        P("heads", None),
        P(),
    )
    return jax.shard_map(
        on_device, mesh=mesh, in_specs=in_specs, out_specs=out_specs, check_vma=False
    )
```

```python
import functools
import jax, jax.numpy as jnp
from jax import lax
from jax.experimental import pallas as pl
from jax.experimental.pallas import tpu as pltpu

from jax.sharding import PartitionSpec as P

MB = 16
CH = 128
epsilon = 1e-06
f32 = jnp.float32
bf16 = jnp.bfloat16
NN = ((1,), (0,))


def split(x):
    hi = x.astype(bf16)
    return hi, (x - hi.astype(f32)).astype(bf16)


def mm(a, b, dims=NN):
    def one(p, q):
        return lax.dot_general(p, q, (dims, ((), ())), preferred_element_type=f32)

    return one(a[0], b[0]) + (one(a[0], b[1]) + one(a[1], b[0]))


def wide(x):
    hi, lo = split(x)
    return jnp.concatenate([hi, lo], axis=1)


def tall_dot(x, pair):
    rows = x.shape[0]
    cols = pair.shape[1] // 2
    hi, lo = split(x)
    out = lax.dot_general(
        jnp.concatenate([hi, lo], axis=0), pair, (NN, ((), ())), preferred_element_type=f32
    )
    top, low = out[:rows], out[rows:]
    return top[:, :cols] + (top[:, cols:] + low[:, :cols])


def iota(shape, dim):
    return lax.broadcasted_iota(jnp.int32, shape, dim)


def head_sum(x, hd):
    rows, cols = x.shape
    parts = [
        jnp.broadcast_to(jnp.sum(x[i : i + hd], axis=0, keepdims=True), (hd, cols))
        for i in range(0, rows, hd)
    ]
    return parts[0] if len(parts) == 1 else jnp.concatenate(parts, axis=0)


def lane_sum(x):
    return jnp.sum(x, axis=1, keepdims=True)


def coefficients(transposed):
    source = iota((CH, CH), 1 if transposed else 0)
    target = iota((CH, CH), 0 if transposed else 1)
    before = (source // MB < target // MB).astype(f32) * (1.0 / MB)
    inside = ((source // MB == target // MB) & (source <= target)).astype(f32)
    return before, before + inside / ((target % MB) + 1).astype(f32)


def forward_body(
    joined, rate, rate_t, seg, seg_t, w0, b0, gain, shift, mixed, z_out, zb_out, w_out, b_out,
    w_s, b_s, z_s, tau_s, a_s, m_s, *, hd, heads,
):
    pairs = heads * hd // CH
    per = CH // hd
    span = heads * hd
    chunks = joined.shape[0] // CH
    n_inv = 1.0 / hd
    row_head = iota((CH, CH), 0) // hd
    lane_head = iota((CH, CH), 1) // hd
    lane_block = iota((hd, CH), 1) // MB
    block_diag = row_head == lane_head
    w_s[...] = jnp.zeros_like(w_s)
    b_s[...] = jnp.zeros_like(b_s)

    def chunk(c, carry):
        ts = pl.multiple_of(c * CH, CH)
        here = pl.ds(ts, CH)
        seg_row = seg_t[:, here]
        seg_col = seg[here, :]
        last_seg = seg_row[:, CH - 1 : CH]
        prev = jnp.max(jnp.where(iota(seg_t.shape, 1) < ts, seg_t[...], 0.0), keepdims=True)
        carried = seg_row == prev
        in_last = (seg_row == last_seg).astype(f32)
        whole = last_seg == prev
        same = seg_col == seg_row
        before, within = coefficients(False)
        before = jnp.where(same, before, 0.0)
        within = jnp.where(same, within, 0.0)
        for p in range(pairs):
            rows = slice(p * CH, (p + 1) * CH)
            kn = joined[here, span + p * CH : span + (p + 1) * CH]
            qn = joined[here, p * CH : (p + 1) * CH]
            vn = joined[here, 2 * span + p * CH : 2 * span + (p + 1) * CH]
            k_t, q_t, v_t = kn.T, qn.T, vn.T
            ks, kts, qts = split(kn), split(k_t), split(q_t)
            ws, w0s = split(w_s[rows]), split(w0[rows])
            bias = jnp.where(carried, b_s[rows], b0[rows])
            z_s[rows] = jnp.where(carried, mm(ws, kts), mm(w0s, kts)) + bias
            zb_out[rows, here] = jnp.where(carried, mm(ws, qts), mm(w0s, qts)) + bias
            w_out[c, rows] = w_s[rows]
            b_out[c, rows] = b_s[rows]
            tau_s[rows] = gain[rows] * (shift[rows] - v_t + k_t)
            for hh in range(per):
                h = p * per + hh
                own = (row_head == hh).astype(bf16)
                r_col = rate[here, h : h + 1]
                score = mm(ks, (kts[0] * own, kts[1] * own))
                a_s[h] = wide((score + 1.0) * (before * r_col))
                score = mm(ks, (qts[0] * own, qts[1] * own))
                m_s[h] = wide((score + 1.0) * (within * r_col))

        gsq = [jnp.broadcast_to(gain[h * hd : (h + 1) * hd] ** 2, (hd, CH)) for h in range(heads)]
        tsum = [
            jnp.sum(tau_s[h * hd : (h + 1) * hd], axis=0, keepdims=True) * n_inv
            for h in range(heads)
        ]

        def inner(h, z):
            tau = tau_s[h * hd : (h + 1) * hd]
            zg = z * gsq[h]
            m2 = jnp.sum(z * z, axis=0, keepdims=True) * n_inv
            a1 = jnp.sum(zg, axis=0, keepdims=True) * n_inv
            a2 = jnp.sum(z * zg, axis=0, keepdims=True) * n_inv
            a3 = jnp.sum(z * tau, axis=0, keepdims=True) * n_inv
            s = lax.rsqrt(m2 + epsilon)
            c_eu = s * (s * a2 + a3)
            e_mean = s * a1 + tsum[h]
            return (s * s) * (zg - c_eu * z) + s * (tau - e_mean)

        def step(t, zs):
            now = lane_block == t
            new = []
            for h in range(heads):
                g = jnp.where(now, inner(h, zs[h]), 0.0)
                new.append(zs[h] - tall_dot(g, a_s[h]))
            return tuple(new)

        zs = tuple(z_s[h * hd : (h + 1) * hd] for h in range(heads))
        zs = lax.fori_loop(0, CH // MB - 1, step, zs)
        for p in range(pairs):
            rows = slice(p * CH, (p + 1) * CH)
            gs = []
            outs = []
            for hh in range(per):
                h = p * per + hh
                hr = slice(h * hd, (h + 1) * hd)
                z_out[hr, here] = zs[h]
                g = inner(h, zs[h])
                zb = zb_out[hr, here] - tall_dot(g, m_s[h])
                zb_out[hr, here] = zb
                sb = lax.rsqrt(jnp.sum(zb * zb, axis=0, keepdims=True) * n_inv + epsilon)
                outs.append(zb * sb * gain[hr] + shift[hr])
                gs.append(g * (rate_t[h : h + 1, here] * in_last * (1.0 / MB)))
            gw = jnp.concatenate(gs, axis=0)
            lanes = slice(p * CH, (p + 1) * CH)
            mixed[here, lanes] = joined[here, lanes] + jnp.concatenate(outs, axis=0).T
            kn = joined[here, span + p * CH : span + (p + 1) * CH]
            upd = mm(split(gw), split(kn))
            w_s[rows] = jnp.where(whole, w_s[rows], w0[rows]) - jnp.where(block_diag, upd, 0.0)
            b_s[rows] = jnp.where(whole, b_s[rows], b0[rows]) - lane_sum(gw)
        return carry

    lax.fori_loop(0, chunks, chunk, 0)


def ttt_forward(joined, rate, rate_t, seg, seg_t, w0, b0, gain, shift, hd, heads):
    length = joined.shape[0]
    span = heads * hd
    chunks = length // CH
    shape = jax.ShapeDtypeStruct
    return pl.pallas_call(
        functools.partial(forward_body, hd=hd, heads=heads),
        out_shape=(
            shape((length, span), f32),
            shape((span, length), f32),
            shape((span, length), f32),
            shape((chunks, span, CH), f32),
            shape((chunks, span, 1), f32),
        ),
        scratch_shapes=[
            pltpu.VMEM((span, CH), f32),
            pltpu.VMEM((span, 1), f32),
            pltpu.VMEM((span, CH), f32),
            pltpu.VMEM((span, CH), f32),
            pltpu.VMEM((heads, CH, 2 * CH), bf16),
            pltpu.VMEM((heads, CH, 2 * CH), bf16),
        ],
        compiler_params=pltpu.CompilerParams(vmem_limit_bytes=48 << 20),
        name="inner_forward",
    )(joined, rate, rate_t, seg, seg_t, w0, b0, gain, shift)


def backward_body(
    joined, rate_t, seg, seg_t, w0, b0, gain, shift, z_in, zb_in, w_in, b_in, dy,
    dq_out, dk_out, dv_out, dr_out, dw_out, db_out, dg_out, dsh_out,
    dw_s, db_s, p_s, u_s, f_s, bb_s, e2_s, u2_s, gt_s, dzb_s, at_s, sc_s,
    *, hd, heads,
):
    pairs = heads * hd // CH
    per = CH // hd
    span = heads * hd
    chunks = joined.shape[0] // CH
    n_inv = 1.0 / hd
    row_head = iota((CH, CH), 0) // hd
    lane_head = iota((CH, CH), 1) // hd
    lane_block = iota((hd, CH), 1) // MB
    block_diag = row_head == lane_head
    for ref in (dw_s, db_s, dw_out, db_out, dg_out, dsh_out):
        ref[...] = jnp.zeros_like(ref)

    def mean(x):
        return head_sum(x, hd) * n_inv

    def chunk(index, carry):
        c = chunks - 1 - index
        ts = pl.multiple_of(c * CH, CH)
        here = pl.ds(ts, CH)
        seg_row = seg_t[:, here]
        seg_col = seg[here, :]
        last_seg = seg_row[:, CH - 1 : CH]
        prev = jnp.max(jnp.where(iota(seg_t.shape, 1) < ts, seg_t[...], 0.0), keepdims=True)
        carried = seg_row == prev
        carried_col = seg_col == prev
        in_last = (seg_row == last_seg).astype(f32)
        whole = last_seg == prev
        same = seg_col == seg_row
        before, within = coefficients(True)
        before = jnp.where(same, before, 0.0)
        within = jnp.where(same, within, 0.0)
        consts = {}
        for p in range(pairs):
            rows = slice(p * CH, (p + 1) * CH)
            lanes = slice(p * CH, (p + 1) * CH)
            qn = joined[here, p * CH : (p + 1) * CH]
            kn = joined[here, span + p * CH : span + (p + 1) * CH]
            vn = joined[here, 2 * span + p * CH : 2 * span + (p + 1) * CH]
            k_t, v_t, dy_t = kn.T, vn.T, dy[here, lanes].T
            qs, ks, kts = split(qn), split(kn), split(k_t)
            g_col = gain[rows]
            gsq = g_col * g_col
            zb = zb_in[rows, here]
            sb = lax.rsqrt(mean(zb * zb) + epsilon)
            ub = zb * sb
            dg_out[rows] += lane_sum(dy_t * ub)
            dsh_out[rows] += lane_sum(dy_t)
            pb = dy_t * g_col
            dzb = sb * (pb - mean(pb) - ub * mean(pb * ub))
            dzb_s[rows] = dzb
            z = z_in[rows, here]
            s = lax.rsqrt(mean(z * z) + epsilon)
            u = z * s
            gu = gsq * u
            e = gu + g_col * (shift[rows] - v_t + k_t)
            c_eu = mean(e * u)
            g_t = s * (e - mean(e) - u * c_eu)
            gt_s[rows] = g_t
            u_s[rows] = u
            f_s[rows] = g_t + s * gu
            bb_s[rows] = (s * s) * (gsq - c_eu)
            e2_s[rows] = (s * s) * (e + gu)
            u2_s[rows] = s * u
            h1 = s * mean(gu)
            h2 = 2.0 * s * c_eu + s * mean(gu * u)
            dzbs = split(dzb)
            gts = split(g_t)
            dzbn = split(dzb.T)
            from_state = mm(split(dw_s[rows]), kts) + db_s[rows]
            pieces = []
            dq = dy[here, lanes]
            dk = jnp.zeros((CH, CH), f32)
            for hh in range(per):
                h = p * per + hh
                hr = slice(hh * hd, (hh + 1) * hd)
                r_row = rate_t[h : h + 1, here]
                consts[h] = (h1[hh * hd : hh * hd + 1], h2[hh * hd : hh * hd + 1])
                own = (row_head == hh).astype(bf16)
                own_lane = (lane_head == hh).astype(bf16)
                kt_h = (kts[0] * own, kts[1] * own)
                sc = (mm(ks, kt_h) + 1.0) * before
                sc_s[h] = sc
                at_s[h] = wide(sc * r_row)
                scq = (mm(qs, kt_h) + 1.0) * within
                pt = mm(dzbn, (gts[0] * own, gts[1] * own))
                dr_out[h : h + 1, here] = -jnp.sum(pt * scq, axis=0, keepdims=True) - (
                    (1.0 / MB) * in_last
                ) * jnp.sum(g_t[hr] * from_state[hr], axis=0, keepdims=True)
                pm = pt * (within * r_row)
                pms = split(pm)
                pmts = split(pm.T)
                kn_h = (ks[0] * own_lane, ks[1] * own_lane)
                qn_h = (qs[0] * own_lane, qs[1] * own_lane)
                dq = dq - mm(pms, kn_h)
                dk = dk - mm(pmts, qn_h)
                pieces.append(
                    -mm((dzbs[0][hr], dzbs[1][hr]), split(scq * r_row))
                    - from_state[hr] * (r_row * in_last * (1.0 / MB))
                )
            p_s[rows] = jnp.concatenate(pieces, axis=0)
            w0s = split(w0[rows])
            wd = split(w_in[c, rows] - w0[rows])
            zero = jnp.zeros((), bf16)
            dzbn_c = (jnp.where(carried_col, dzbn[0], zero), jnp.where(carried_col, dzbn[1], zero))
            dq_out[here, lanes] = dq + mm(dzbn, w0s) + mm(dzbn_c, wd)
            dk_out[here, lanes] = dk

        def upstream(h, pv):
            hr = slice(h * hd, (h + 1) * hd)
            h1, h2 = consts[h]
            pm = jnp.sum(pv, axis=0, keepdims=True) * n_inv
            q = jnp.sum(pv * u_s[hr], axis=0, keepdims=True) * n_inv
            kf = jnp.sum(pv * f_s[hr], axis=0, keepdims=True) * n_inv
            kappa = kf - h1 * pm - h2 * q
            dz = (pv - pm) * bb_s[hr] - q * e2_s[hr] - kappa * u2_s[hr]
            return dz, pm, q

        def step(index, ps):
            now = lane_block == (CH // MB - 1 - index)
            new = []
            for h in range(heads):
                dz = jnp.where(now, upstream(h, ps[h])[0], 0.0)
                new.append(ps[h] - tall_dot(dz, at_s[h]))
            return tuple(new)

        ps = tuple(p_s[h * hd : (h + 1) * hd] for h in range(heads))
        ps = lax.fori_loop(0, CH // MB - 1, step, ps)

        for p in range(pairs):
            rows = slice(p * CH, (p + 1) * CH)
            lanes = slice(p * CH, (p + 1) * CH)
            qn = joined[here, p * CH : (p + 1) * CH]
            kn = joined[here, span + p * CH : span + (p + 1) * CH]
            vn = joined[here, 2 * span + p * CH : 2 * span + (p + 1) * CH]
            qs, ks = split(qn), split(kn)
            g_t = gt_s[rows]
            gts = split(g_t)
            dzs, des = [], []
            for hh in range(per):
                h = p * per + hh
                hr = slice(h * hd, (h + 1) * hd)
                dz, pm, q = upstream(h, ps[h])
                dzs.append(dz - jnp.sum(dz, axis=0, keepdims=True) * n_inv)
                z = z_in[hr, here]
                s = lax.rsqrt(jnp.sum(z * z, axis=0, keepdims=True) * n_inv + epsilon)
                des.append(s * (ps[h] - pm - u_s[hr] * q))
            dz = jnp.concatenate(dzs, axis=0)
            de = jnp.concatenate(des, axis=0)
            g_col = gain[rows]
            gde = g_col * de
            t_t = shift[rows] + (kn - vn).T
            dg_out[rows] += lane_sum((2.0 * g_col * u_s[rows] + t_t) * de)
            dsh_out[rows] += lane_sum(gde)
            gden = gde.T
            dv_out[here, lanes] = -gden
            dzn = split(dz.T)
            dk = dk_out[here, lanes] + gden
            r_rows = []
            for hh in range(per):
                h = p * per + hh
                r_row = rate_t[h : h + 1, here]
                own = (row_head == hh).astype(bf16)
                own_lane = (lane_head == hh).astype(bf16)
                rt = mm(dzn, (gts[0] * own, gts[1] * own))
                dr_out[h : h + 1, here] -= jnp.sum(rt * sc_s[h], axis=0, keepdims=True)
                ra = rt * (before * r_row)
                dk = dk - mm(split(ra + ra.T), (ks[0] * own_lane, ks[1] * own_lane))
                r_rows.append(jnp.broadcast_to(r_row * in_last * (1.0 / MB), (hd, CH)))
            gw = g_t * jnp.concatenate(r_rows, axis=0)
            w0s = split(w0[rows])
            wd = split(w_in[c, rows] - w0[rows])
            zero = jnp.zeros((), bf16)
            dzn_c = (jnp.where(carried_col, dzn[0], zero), jnp.where(carried_col, dzn[1], zero))
            dk = dk + mm(dzn, w0s) + mm(dzn_c, wd) - mm(split(gw.T), split(dw_s[rows]))
            dk_out[here, lanes] = dk
            dzb = dzb_s[rows]
            dzc = jnp.where(carried, dz, 0.0)
            dzbc = jnp.where(carried, dzb, 0.0)
            diag = jnp.where(block_diag, mm(split(dzc), ks) + mm(split(dzbc), qs), 0.0)
            rest = jnp.where(
                block_diag, mm(split(dz - dzc), ks) + mm(split(dzb - dzbc), qs), 0.0
            )
            dw = dw_s[rows]
            db = db_s[rows]
            dw_out[rows] += jnp.where(whole, 0.0, dw) + rest
            db_out[rows] += jnp.where(whole, 0.0, db) + lane_sum(dz - dzc + dzb - dzbc)
            dw_s[rows] = jnp.where(whole, dw, 0.0) + diag
            db_s[rows] = jnp.where(whole, db, 0.0) + lane_sum(dzc + dzbc)
        return carry

    lax.fori_loop(0, chunks, chunk, 0)


def ttt_backward(joined, rate_t, seg, seg_t, w0, b0, gain, shift, saved, dy, hd, heads):
    length = joined.shape[0]
    span = heads * hd
    shape = jax.ShapeDtypeStruct
    return pl.pallas_call(
        functools.partial(backward_body, hd=hd, heads=heads),
        out_shape=(
            shape((length, span), f32),
            shape((length, span), f32),
            shape((length, span), f32),
            shape((heads, length), f32),
            shape((span, CH), f32),
            shape((span, 1), f32),
            shape((span, 1), f32),
            shape((span, 1), f32),
        ),
        scratch_shapes=[
            pltpu.VMEM((span, CH), f32),
            pltpu.VMEM((span, 1), f32),
        ]
        + [pltpu.VMEM((span, CH), f32)] * 8
        + [
            pltpu.VMEM((heads, CH, 2 * CH), bf16),
            pltpu.VMEM((heads, CH, CH), f32),
        ],
        compiler_params=pltpu.CompilerParams(vmem_limit_bytes=48 << 20),
        name="inner_backward",
    )(joined, rate_t, seg, seg_t, w0, b0, gain, shift, *saved, dy)


def state_in(inner_weight, inner_bias):
    heads, hd, _ = inner_weight.shape
    per = CH // hd
    w_t = jnp.swapaxes(inner_weight, 1, 2)
    w_t = w_t - jnp.mean(w_t, axis=1, keepdims=True)
    placed = [
        jnp.pad(w_t[h], ((0, 0), ((h % per) * hd, CH - hd - (h % per) * hd)))
        for h in range(heads)
    ]
    b = inner_bias - jnp.mean(inner_bias, axis=1, keepdims=True)
    return jnp.concatenate(placed, axis=0), b.reshape(heads * hd, 1)


def state_back(dw, db, heads, hd):
    per = CH // hd
    parts = [
        dw[h * hd : (h + 1) * hd, (h % per) * hd : (h % per + 1) * hd] for h in range(heads)
    ]
    d = jnp.stack(parts)
    d = jnp.swapaxes(d - jnp.mean(d, axis=1, keepdims=True), 1, 2)
    b = db.reshape(heads, hd)
    return d, b - jnp.mean(b, axis=1, keepdims=True)


def product(left, right):
    return jnp.dot(left, right, precision=lax.Precision.HIGH, preferred_element_type=f32)


def left_product(left, right):
    return lax.dot_general(
        left, right, (((0,), (0,)), ((), ())), precision=lax.Precision.HIGH,
        preferred_element_type=f32,
    )


def right_product(left, right):
    return lax.dot_general(
        left, right, (((1,), (1,)), ((), ())), precision=lax.Precision.HIGH,
        preferred_element_type=f32,
    )


def heads_grid():
    size = lax.axis_size("heads")
    deep = 4 if size % 4 == 0 else 1
    return deep, size // deep


def heads_place():
    _, across = heads_grid()
    index = lax.axis_index("heads")
    return index // across, index % across


def shift(value, dz, dx):
    deep, across = heads_grid()
    pairs = [
        (h, (h // across + dz) % deep * across + (h % across + dx) % across)
        for h in range(deep * across)
    ]
    return lax.ppermute(value, "heads", pairs)


def swap(value, axis, bit):
    return lax.ppermute(value, axis, [(i, i ^ bit) for i in range(lax.axis_size(axis))])


def row_shift(value, step):
    size = lax.axis_size("rows")
    return lax.ppermute(value, "rows", [(r, (r + 2 * step) % size) for r in range(size)])


def butterfly(value, axis):
    bit = 1
    while bit < lax.axis_size(axis):
        value = value + swap(value, axis, bit)
        bit *= 2
    return value


def small_gather(value):
    size = lax.axis_size("heads")
    place = jnp.arange(size) == lax.axis_index("heads")
    place = place.reshape((size,) + (1,) * value.ndim)
    return butterfly(jnp.where(place, value[None], 0.0), "heads")


def gather_columns(value, hooks=(), parts=2):
    deep, across = heads_grid()
    z, x = heads_place()
    rows, cols = value.shape
    size = rows // parts
    out = jnp.zeros((rows, cols * deep * across), value.dtype)
    moving = [value[i * size : (i + 1) * size] for i in range(parts)]
    for dz in range(deep):
        if dz:
            moving = [shift(item, 1, 0) for item in moving]
            if dz <= len(hooks):
                moving[0] = hooks[dz - 1](moving[0])
        side = moving
        for dx in range(across):
            if dx:
                side = [shift(item, 0, 1) for item in side]
            column = ((z - dz) % deep * across + (x - dx) % across) * cols
            for i in range(parts):
                out = lax.dynamic_update_slice(out, side[i], (i * size, column))
    return out


def scatter_columns(value, extra=None, hooks=(), parts=2):
    deep, across = heads_grid()
    z, x = heads_place()
    rows, width = value.shape
    cols = width // (deep * across)
    size = rows // parts

    def piece(i, dz, dx):
        column = ((z - dz) % deep * across + (x - dx) % across) * cols
        block = lax.dynamic_slice(value, (i * size, column), (size, cols))
        if extra is not None and i == parts - 1:
            tail = lax.dynamic_slice(extra, (0, column), (extra.shape[0], cols))
            block = jnp.concatenate([block, tail], 0)
        return block

    total = [None] * parts
    for turn, dz in enumerate(list(range(1, deep)) + [0]):
        if 1 <= turn <= len(hooks):
            total[0] = hooks[turn - 1](total[0])
        for i in range(parts):
            here = None
            for dx in list(range(1, across)) + [0]:
                block = piece(i, dz, dx)
                here = block if here is None else shift(here, 0, 1) + block
            total[i] = here if total[i] is None else shift(total[i], 1, 0) + here
    return jnp.concatenate(total, 0)


def half_of(value, index, axis):
    size = value.shape[axis] // 2
    return lax.dynamic_slice_in_dim(value, index * size, size, axis)


def both_cores(value):
    return jnp.concatenate([value, swap(value, "rows", 1)], 0)


def tokens_half(value, core):
    return jnp.concatenate(
        [half_of(value, core, 1), swap(half_of(value, 1 - core, 1), "rows", 1)], 0
    )


def chips_along():
    return lax.axis_size("rows") // 2


def other_chips(value):
    return [row_shift(value, step) for step in range(1, chips_along())]


def place_body(core, own, other, *outs, axis, widths):
    first = core[0] == 0
    at = 0
    for out, width in zip(outs, widths):
        mine, its = (own[:, at : at + width], other[:, at : at + width]) if axis == 0 else (own[...], other[...])
        low = jnp.where(first, mine, its)
        high = jnp.where(first, its, mine)
        if axis == 0:
            out[0] = low
            out[1] = high
        else:
            out[:, : low.shape[1]] = low
            out[:, low.shape[1] :] = high
        at += width


def place(own, other, core, axis, widths):
    rows, cols = own.shape
    steps = max(n for n in (1, 2, 4) if rows % (8 * n) == 0)
    size = rows // steps
    part = pl.BlockSpec((size, cols), lambda i: (i, 0))
    if axis == 0:
        shapes = [(2, rows, width) for width in widths]
        specs = [pl.BlockSpec((2, size, width), lambda i: (0, i, 0)) for width in widths]
    else:
        shapes = [(rows, 2 * cols)]
        specs = [pl.BlockSpec((size, 2 * cols), lambda i: (i, 0))]
    out = pl.pallas_call(
        functools.partial(place_body, axis=axis, widths=widths),
        grid=(steps,),
        out_shape=[jax.ShapeDtypeStruct(shape, f32) for shape in shapes],
        in_specs=[pl.BlockSpec(memory_space=pltpu.SMEM), part, part],
        out_specs=specs,
        compiler_params=pltpu.CompilerParams(vmem_limit_bytes=48 << 20),
        name="place",
    )(core.reshape(1).astype(jnp.int32), own, other)
    return [o.reshape(2 * rows, -1) if axis == 0 else o for o in out]


def finish(total, core, axis, widths=None):
    widths = (total.shape[1],) if widths is None else widths
    return place(total, swap(total, "rows", 1), core, axis, widths)


def row_products(lefts, rights):
    total = None
    for left, right in zip(lefts, rights):
        part = left_product(left, right)
        total = part if total is None else total + part
    return total


class Along:
    def __init__(self, value, parts=4):
        size = value.shape[0] // parts
        self.own = value
        self.pieces = [
            [row_shift(value[i * size : (i + 1) * size], step) for i in range(parts)]
            for step in range(1, chips_along())
        ]

    def tie(self, i, main):
        for step in self.pieces:
            main, step[i] = lax.optimization_barrier((main, step[i]))
        return main

    def all(self):
        return [self.own] + [
            step[0] if len(step) == 1 else jnp.concatenate(step, 0) for step in self.pieces
        ]


def silu_parts(a):
    sig = jax.nn.sigmoid(a)
    return a * sig, sig * (1.0 + a * (1.0 - sig))


def gelu_parts(v):
    k = 0.7978845608028654
    inner = k * (v + 0.044715 * v * v * v)
    th = jnp.tanh(inner)
    slope = 0.5 * (1.0 + th) + 0.5 * v * (1.0 - th * th) * k * (1.0 + 3 * 0.044715 * v * v)
    return 0.5 * v * (1.0 + th), slope


def on_device(
    stream,
    doc_starts,
    valid_mask,
    first_gain,
    w_query,
    w_key,
    w_value,
    w_rate,
    b_rate,
    inner_weight,
    inner_bias,
    inner_gain,
    inner_shift,
    post_gain,
    post_shift,
    w_gate_attn,
    w_out,
    second_gain,
    w_gate,
    w_up,
    w_down,
    cotangent,
):
    _, length, width = stream.shape
    tokens = stream.reshape(length, width)
    slab = second_gain.shape[0]
    column = lax.axis_index("heads") * slab
    core = lax.axis_index("rows") % 2
    heads, hd = inner_bias.shape
    span = heads * hd
    total_span = span * lax.axis_size("heads")
    gains = small_gather(jnp.stack([first_gain, second_gain]))
    gain_one = gains[:, 0].reshape(width)
    gain_two = gains[:, 1].reshape(width)
    grad_output = cotangent.reshape(length, slab)
    dy_full = gather_columns(grad_output)

    w_joined = jnp.concatenate([w_query, w_key, w_value, w_gate_attn], axis=1)
    r1 = lax.rsqrt(jnp.mean(tokens * tokens, -1, keepdims=True) + epsilon)
    unit = tokens * r1
    unit_y = Along(tokens_half(unit, core))
    normed = unit * gain_one
    joined = product(normed, w_joined)
    rate_pre = lax.dot_general(
        w_rate, normed, (((0,), (1,)), ((), ())), precision=lax.Precision.HIGH,
        preferred_element_type=f32,
    )
    joined = unit_y.tie(0, joined)
    gate_pre = joined[:, 3 * span :]
    sig = jax.nn.sigmoid(rate_pre + b_rate[:, None])
    rate_t = sig / hd
    rate = rate_t.T
    seg = jnp.cumsum(doc_starts.reshape(length)).astype(f32)
    seg, seg_t = seg[:, None], seg[None]
    w0, b0 = state_in(inner_weight, inner_bias)
    gain_col, shift_col = inner_gain.reshape(span, 1), inner_shift.reshape(span, 1)
    mixed, *saved = ttt_forward(
        joined, rate, rate_t, seg, seg_t, w0, b0, gain_col, shift_col, hd, heads
    )
    mixed = unit_y.tie(1, mixed)
    row_sums = butterfly(jnp.stack([jnp.sum(mixed, 1), jnp.sum(mixed * mixed, 1)]), "heads")
    row_mean = row_sums[0] / total_span
    inv_std = lax.rsqrt(row_sums[1] / total_span - row_mean * row_mean + epsilon)[:, None]
    centered = (mixed - row_mean[:, None]) * inv_std
    shaped = centered * post_gain + post_shift
    gate_act, gate_slope = gelu_parts(gate_pre)
    gathered = gather_columns(
        gate_act * shaped,
        [functools.partial(unit_y.tie, 2), functools.partial(unit_y.tie, 3)],
    )
    gathered_y = Along(tokens_half(gathered, core))
    attn = product(gathered, w_out)
    stream_cols = lax.dynamic_slice_in_dim(tokens, column, slab, 1)
    hidden = stream_cols + attn
    whole = gather_columns(
        hidden, [lambda v: v, functools.partial(gathered_y.tie, 0)],
    )

    r2 = lax.rsqrt(jnp.mean(whole * whole, -1, keepdims=True) + epsilon)
    hnorm = whole * r2 * gain_two
    hnorm_y = Along(tokens_half(hnorm, core))
    a = product(hnorm, w_gate)
    a = gathered_y.tie(1, a)
    c = product(hnorm, w_up)
    act, slope = silu_parts(a)
    m = act * c
    ffn_part = gathered_y.tie(2, product(m, w_down))
    dm = right_product(dy_full, w_down)
    da = dm * c * slope
    dc = dm * act
    da_y, dc_y = Along(da, 1), Along(dc, 1)
    dhnorm = right_product(da, w_gate) + right_product(dc, w_up)
    d_gain_two = jnp.sum(dhnorm * whole * r2, 0, keepdims=True)
    weighted = dhnorm * gain_two
    d_whole = r2 * weighted - whole * (r2 * r2 * r2) * jnp.mean(
        whole * weighted, -1, keepdims=True
    )
    pad = jnp.zeros((7, width), f32)
    d_part = scatter_columns(
        d_whole,
        jnp.concatenate([d_gain_two, pad], 0),
        [
            functools.partial(gathered_y.tie, 3),
            functools.partial(hnorm_y.tie, 0),
            functools.partial(hnorm_y.tie, 1),
        ],
    )
    d_hidden = grad_output + d_part[:length]
    d_gain_two = d_part[length]
    d_hidden_y = Along(d_hidden, 1)
    g_down = left_product(both_cores(m), tokens_half(dy_full, core))

    d_gated = scatter_columns(
        right_product(d_hidden, w_out),
        None,
        [
            functools.partial(hnorm_y.tie, 2),
            functools.partial(hnorm_y.tie, 3),
            functools.partial(da_y.tie, 0),
        ],
    )
    ffn = scatter_columns(ffn_part)
    output = hidden + ffn
    d_shaped = d_gated * gate_act
    d_gate_pre = d_gated * shaped * gate_slope
    d_post_gain = jnp.sum(d_shaped * centered, 0)
    d_post_shift = jnp.sum(d_shaped, 0)
    d_center = d_shaped * post_gain
    back_sums = butterfly(
        jnp.stack([jnp.sum(d_center, 1), jnp.sum(d_center * centered, 1)]), "heads"
    )
    d_mixed = inv_std * (
        d_center - back_sums[0][:, None] / total_span
        - centered * back_sums[1][:, None] / total_span
    )
    dq, dk, dv, d_rate, dw, db, dg, dsh = ttt_backward(
        joined, rate_t, seg, seg_t, w0, b0, gain_col, shift_col, saved, d_mixed, hd, heads
    )
    dq = d_hidden_y.tie(0, dc_y.tie(0, dq))
    d_inner_weight, d_inner_bias = state_back(dw, db, heads, hd)
    d_rate_pre = d_rate * rate_t * (1.0 - sig)
    d_joined = jnp.concatenate([dq, dk, dv, d_gate_pre], 1)
    d_joined_y, d_rate_y = Along(d_joined, 1), Along(d_rate_pre, 1)
    d_normed = right_product(d_joined, w_joined) + lax.dot_general(
        d_rate_pre, w_rate, (((0,), (1,)), ((), ())), precision=lax.Precision.HIGH,
        preferred_element_type=f32,
    )
    d_gain_one = jnp.sum(d_normed * tokens * r1, 0, keepdims=True)
    weighted = d_normed * gain_one
    d_tokens = r1 * weighted - tokens * (r1 * r1 * r1) * jnp.mean(
        tokens * weighted, -1, keepdims=True
    )
    d_part = scatter_columns(d_tokens, jnp.concatenate([d_gain_one, pad], 0))
    d_stream = d_hidden + d_part[:length]
    d_gain_one = d_part[length]

    def cores(values):
        return [both_cores(value) for value in values]

    (g_gate,) = finish(row_products(cores(da_y.all()), hnorm_y.all()), core, 1)
    (g_up,) = finish(row_products(cores(dc_y.all()), hnorm_y.all()), core, 1)
    (g_out,) = finish(row_products(gathered_y.all(), cores(d_hidden_y.all())), core, 0)
    (g_down,) = finish(sum(other_chips(g_down), g_down), core, 1)
    gain_half = half_of(gain_one, core, 0)
    normed_pairs = [pair * gain_half for pair in unit_y.all()]
    g_query, g_key, g_value, g_gate_attn = finish(
        row_products(normed_pairs, cores(d_joined_y.all())), core, 0, (span,) * 4
    )
    g_rate = None
    for pair, d in zip(normed_pairs, d_rate_y.all()):
        part = product(jnp.concatenate([d, swap(d, "rows", 1)], 1), pair)
        g_rate = part if g_rate is None else g_rate + part
    ends = (g_rate, swap(g_rate, "rows", 1))
    g_rate = jnp.where(core == 0, jnp.concatenate(ends, 1), jnp.concatenate(ends[::-1], 1))

    weights = valid_mask.reshape(-1).astype(f32)[:, None]
    stats = jnp.stack(
        [
            jnp.sum(weights * member * member)
            for member in (stream_cols, attn, hidden, ffn, output)
        ]
        + [jnp.sum(weights) / lax.axis_size("heads")]
    )
    stats = butterfly(butterfly(stats, "rows"), "heads")
    rms_values = jnp.sqrt(stats[:5] / (stats[5] * width))
    small = [
        d_gain_one, jnp.sum(d_rate_pre, 1), d_inner_weight, d_inner_bias, dg, dsh,
        d_post_gain, d_post_shift, d_gain_two,
    ]
    packed = butterfly(jnp.concatenate([item.reshape(-1) for item in small]), "rows")
    parts = []
    at = 0
    for item in small:
        parts.append(packed[at : at + item.size])
        at += item.size
    return (
        output.reshape(1, length, slab),
        d_stream.reshape(1, length, slab),
        parts[0],
        g_query,
        g_key,
        g_value,
        g_rate.T,
        parts[1],
        parts[2].reshape(heads, hd, hd),
        parts[3].reshape(heads, hd),
        parts[4].reshape(heads, hd),
        parts[5].reshape(heads, hd),
        parts[6],
        parts[7],
        g_gate_attn,
        g_out,
        parts[8],
        g_gate.T,
        g_up.T,
        g_down,
        rms_values,
    )


def solution(mesh):
    in_specs = (
        P("rows", None, None),
        P("rows", None),
        P("rows", None),
        P("heads"),
        P(None, "heads"),
        P(None, "heads"),
        P(None, "heads"),
        P(None, "heads"),
        P("heads"),
        P("heads", None, None),
        P("heads", None),
        P("heads", None),
        P("heads", None),
        P("heads"),
        P("heads"),
        P(None, "heads"),
        P(None, "heads"),
        P("heads"),
        P(None, "heads"),
        P(None, "heads"),
        P("heads", None),
        P("rows", None, "heads"),
    )
    out_specs = (
        P("rows", None, "heads"),
        P("rows", None, "heads"),
        P("heads"),
        P(None, "heads"),
        P(None, "heads"),
        P(None, "heads"),
        P(None, "heads"),
        P("heads"),
        P("heads", None, None),
        P("heads", None),
        P("heads", None),
        P("heads", None),
        P("heads"),
        P("heads"),
        P(None, "heads"),
        P(None, "heads"),
        P("heads"),
        P(None, "heads"),
        P(None, "heads"),
        P("heads", None),
        P(),
    )
    return jax.shard_map(
        on_device, mesh=mesh, in_specs=in_specs, out_specs=out_specs, check_vma=False
    )
```

```python
import functools
import jax, jax.numpy as jnp
from jax import lax
from jax.experimental import pallas as pl
from jax.experimental.pallas import tpu as pltpu

from jax.sharding import PartitionSpec as P

MB = 16
CH = 128
epsilon = 1e-06
f32 = jnp.float32
bf16 = jnp.bfloat16
NN = ((1,), (0,))


def split(x):
    hi = x.astype(bf16)
    return hi, (x - hi.astype(f32)).astype(bf16)


def mm(a, b, dims=NN):
    def one(p, q):
        return lax.dot_general(p, q, (dims, ((), ())), preferred_element_type=f32)

    return one(a[0], b[0]) + (one(a[0], b[1]) + one(a[1], b[0]))


def wide(x):
    hi, lo = split(x)
    return jnp.concatenate([hi, lo], axis=1)


def tall_dot(x, pair):
    rows = x.shape[0]
    cols = pair.shape[1] // 2
    hi, lo = split(x)
    out = lax.dot_general(
        jnp.concatenate([hi, lo], axis=0), pair, (NN, ((), ())), preferred_element_type=f32
    )
    top, low = out[:rows], out[rows:]
    return top[:, :cols] + (top[:, cols:] + low[:, :cols])


def iota(shape, dim):
    return lax.broadcasted_iota(jnp.int32, shape, dim)


def head_sum(x, hd):
    rows, cols = x.shape
    parts = [
        jnp.broadcast_to(jnp.sum(x[i : i + hd], axis=0, keepdims=True), (hd, cols))
        for i in range(0, rows, hd)
    ]
    return parts[0] if len(parts) == 1 else jnp.concatenate(parts, axis=0)


def lane_sum(x):
    return jnp.sum(x, axis=1, keepdims=True)


def coefficients(transposed):
    source = iota((CH, CH), 1 if transposed else 0)
    target = iota((CH, CH), 0 if transposed else 1)
    before = (source // MB < target // MB).astype(f32) * (1.0 / MB)
    inside = ((source // MB == target // MB) & (source <= target)).astype(f32)
    return before, before + inside / ((target % MB) + 1).astype(f32)


def forward_body(
    joined, rate, rate_t, seg, seg_t, w0, b0, gain, shift, mixed, z_out, zb_out, w_out, b_out,
    w_s, b_s, z_s, tau_s, a_s, m_s, *, hd, heads,
):
    pairs = heads * hd // CH
    per = CH // hd
    span = heads * hd
    chunks = joined.shape[0] // CH
    n_inv = 1.0 / hd
    row_head = iota((CH, CH), 0) // hd
    lane_head = iota((CH, CH), 1) // hd
    lane_block = iota((hd, CH), 1) // MB
    block_diag = row_head == lane_head
    w_s[...] = jnp.zeros_like(w_s)
    b_s[...] = jnp.zeros_like(b_s)

    def chunk(c, carry):
        ts = pl.multiple_of(c * CH, CH)
        here = pl.ds(ts, CH)
        seg_row = seg_t[:, here]
        seg_col = seg[here, :]
        last_seg = seg_row[:, CH - 1 : CH]
        prev = jnp.max(jnp.where(iota(seg_t.shape, 1) < ts, seg_t[...], 0.0), keepdims=True)
        carried = seg_row == prev
        in_last = (seg_row == last_seg).astype(f32)
        whole = last_seg == prev
        same = seg_col == seg_row
        before, within = coefficients(False)
        before = jnp.where(same, before, 0.0)
        within = jnp.where(same, within, 0.0)
        for p in range(pairs):
            rows = slice(p * CH, (p + 1) * CH)
            kn = joined[here, span + p * CH : span + (p + 1) * CH]
            qn = joined[here, p * CH : (p + 1) * CH]
            vn = joined[here, 2 * span + p * CH : 2 * span + (p + 1) * CH]
            k_t, q_t, v_t = kn.T, qn.T, vn.T
            ks, kts, qts = split(kn), split(k_t), split(q_t)
            ws, w0s = split(w_s[rows]), split(w0[rows])
            bias = jnp.where(carried, b_s[rows], b0[rows])
            z_s[rows] = jnp.where(carried, mm(ws, kts), mm(w0s, kts)) + bias
            zb_out[rows, here] = jnp.where(carried, mm(ws, qts), mm(w0s, qts)) + bias
            w_out[c, rows] = w_s[rows]
            b_out[c, rows] = b_s[rows]
            tau_s[rows] = gain[rows] * (shift[rows] - v_t + k_t)
            for hh in range(per):
                h = p * per + hh
                own = (row_head == hh).astype(bf16)
                r_col = rate[here, h : h + 1]
                score = mm(ks, (kts[0] * own, kts[1] * own))
                a_s[h] = wide((score + 1.0) * (before * r_col))
                score = mm(ks, (qts[0] * own, qts[1] * own))
                m_s[h] = wide((score + 1.0) * (within * r_col))

        gsq = [jnp.broadcast_to(gain[h * hd : (h + 1) * hd] ** 2, (hd, CH)) for h in range(heads)]
        tsum = [
            jnp.sum(tau_s[h * hd : (h + 1) * hd], axis=0, keepdims=True) * n_inv
            for h in range(heads)
        ]

        def inner(h, z):
            tau = tau_s[h * hd : (h + 1) * hd]
            zg = z * gsq[h]
            m2 = jnp.sum(z * z, axis=0, keepdims=True) * n_inv
            a1 = jnp.sum(zg, axis=0, keepdims=True) * n_inv
            a2 = jnp.sum(z * zg, axis=0, keepdims=True) * n_inv
            a3 = jnp.sum(z * tau, axis=0, keepdims=True) * n_inv
            s = lax.rsqrt(m2 + epsilon)
            c_eu = s * (s * a2 + a3)
            e_mean = s * a1 + tsum[h]
            return (s * s) * (zg - c_eu * z) + s * (tau - e_mean)

        def step(t, zs):
            now = lane_block == t
            new = []
            for h in range(heads):
                g = jnp.where(now, inner(h, zs[h]), 0.0)
                new.append(zs[h] - tall_dot(g, a_s[h]))
            return tuple(new)

        zs = tuple(z_s[h * hd : (h + 1) * hd] for h in range(heads))
        zs = lax.fori_loop(0, CH // MB - 1, step, zs)
        for p in range(pairs):
            rows = slice(p * CH, (p + 1) * CH)
            gs = []
            outs = []
            for hh in range(per):
                h = p * per + hh
                hr = slice(h * hd, (h + 1) * hd)
                z_out[hr, here] = zs[h]
                g = inner(h, zs[h])
                zb = zb_out[hr, here] - tall_dot(g, m_s[h])
                zb_out[hr, here] = zb
                sb = lax.rsqrt(jnp.sum(zb * zb, axis=0, keepdims=True) * n_inv + epsilon)
                outs.append(zb * sb * gain[hr] + shift[hr])
                gs.append(g * (rate_t[h : h + 1, here] * in_last * (1.0 / MB)))
            gw = jnp.concatenate(gs, axis=0)
            lanes = slice(p * CH, (p + 1) * CH)
            mixed[here, lanes] = joined[here, lanes] + jnp.concatenate(outs, axis=0).T
            kn = joined[here, span + p * CH : span + (p + 1) * CH]
            upd = mm(split(gw), split(kn))
            w_s[rows] = jnp.where(whole, w_s[rows], w0[rows]) - jnp.where(block_diag, upd, 0.0)
            b_s[rows] = jnp.where(whole, b_s[rows], b0[rows]) - lane_sum(gw)
        return carry

    lax.fori_loop(0, chunks, chunk, 0)


def ttt_forward(joined, rate, rate_t, seg, seg_t, w0, b0, gain, shift, hd, heads):
    length = joined.shape[0]
    span = heads * hd
    chunks = length // CH
    shape = jax.ShapeDtypeStruct
    return pl.pallas_call(
        functools.partial(forward_body, hd=hd, heads=heads),
        out_shape=(
            shape((length, span), f32),
            shape((span, length), f32),
            shape((span, length), f32),
            shape((chunks, span, CH), f32),
            shape((chunks, span, 1), f32),
        ),
        scratch_shapes=[
            pltpu.VMEM((span, CH), f32),
            pltpu.VMEM((span, 1), f32),
            pltpu.VMEM((span, CH), f32),
            pltpu.VMEM((span, CH), f32),
            pltpu.VMEM((heads, CH, 2 * CH), bf16),
            pltpu.VMEM((heads, CH, 2 * CH), bf16),
        ],
        compiler_params=pltpu.CompilerParams(vmem_limit_bytes=48 << 20),
        name="inner_forward",
    )(joined, rate, rate_t, seg, seg_t, w0, b0, gain, shift)


def backward_body(
    joined, rate_t, seg, seg_t, w0, b0, gain, shift, z_in, zb_in, w_in, b_in, dy,
    dq_out, dk_out, dv_out, dr_out, dw_out, db_out, dg_out, dsh_out,
    dw_s, db_s, p_s, u_s, f_s, bb_s, e2_s, u2_s, gt_s, dzb_s, at_s, sc_s,
    *, hd, heads,
):
    pairs = heads * hd // CH
    per = CH // hd
    span = heads * hd
    chunks = joined.shape[0] // CH
    n_inv = 1.0 / hd
    row_head = iota((CH, CH), 0) // hd
    lane_head = iota((CH, CH), 1) // hd
    lane_block = iota((hd, CH), 1) // MB
    block_diag = row_head == lane_head
    for ref in (dw_s, db_s, dw_out, db_out, dg_out, dsh_out):
        ref[...] = jnp.zeros_like(ref)

    def mean(x):
        return head_sum(x, hd) * n_inv

    def chunk(index, carry):
        c = chunks - 1 - index
        ts = pl.multiple_of(c * CH, CH)
        here = pl.ds(ts, CH)
        seg_row = seg_t[:, here]
        seg_col = seg[here, :]
        last_seg = seg_row[:, CH - 1 : CH]
        prev = jnp.max(jnp.where(iota(seg_t.shape, 1) < ts, seg_t[...], 0.0), keepdims=True)
        carried = seg_row == prev
        carried_col = seg_col == prev
        in_last = (seg_row == last_seg).astype(f32)
        whole = last_seg == prev
        same = seg_col == seg_row
        before, within = coefficients(True)
        before = jnp.where(same, before, 0.0)
        within = jnp.where(same, within, 0.0)
        consts = {}
        for p in range(pairs):
            rows = slice(p * CH, (p + 1) * CH)
            lanes = slice(p * CH, (p + 1) * CH)
            qn = joined[here, p * CH : (p + 1) * CH]
            kn = joined[here, span + p * CH : span + (p + 1) * CH]
            vn = joined[here, 2 * span + p * CH : 2 * span + (p + 1) * CH]
            k_t, v_t, dy_t = kn.T, vn.T, dy[here, lanes].T
            qs, ks, kts = split(qn), split(kn), split(k_t)
            g_col = gain[rows]
            gsq = g_col * g_col
            zb = zb_in[rows, here]
            sb = lax.rsqrt(mean(zb * zb) + epsilon)
            ub = zb * sb
            dg_out[rows] += lane_sum(dy_t * ub)
            dsh_out[rows] += lane_sum(dy_t)
            pb = dy_t * g_col
            dzb = sb * (pb - mean(pb) - ub * mean(pb * ub))
            dzb_s[rows] = dzb
            z = z_in[rows, here]
            s = lax.rsqrt(mean(z * z) + epsilon)
            u = z * s
            gu = gsq * u
            e = gu + g_col * (shift[rows] - v_t + k_t)
            c_eu = mean(e * u)
            g_t = s * (e - mean(e) - u * c_eu)
            gt_s[rows] = g_t
            u_s[rows] = u
            f_s[rows] = g_t + s * gu
            bb_s[rows] = (s * s) * (gsq - c_eu)
            e2_s[rows] = (s * s) * (e + gu)
            u2_s[rows] = s * u
            h1 = s * mean(gu)
            h2 = 2.0 * s * c_eu + s * mean(gu * u)
            dzbs = split(dzb)
            gts = split(g_t)
            dzbn = split(dzb.T)
            from_state = mm(split(dw_s[rows]), kts) + db_s[rows]
            pieces = []
            dq = dy[here, lanes]
            dk = jnp.zeros((CH, CH), f32)
            for hh in range(per):
                h = p * per + hh
                hr = slice(hh * hd, (hh + 1) * hd)
                r_row = rate_t[h : h + 1, here]
                consts[h] = (h1[hh * hd : hh * hd + 1], h2[hh * hd : hh * hd + 1])
                own = (row_head == hh).astype(bf16)
                own_lane = (lane_head == hh).astype(bf16)
                kt_h = (kts[0] * own, kts[1] * own)
                sc = (mm(ks, kt_h) + 1.0) * before
                sc_s[h] = sc
                at_s[h] = wide(sc * r_row)
                scq = (mm(qs, kt_h) + 1.0) * within
                pt = mm(dzbn, (gts[0] * own, gts[1] * own))
                dr_out[h : h + 1, here] = -jnp.sum(pt * scq, axis=0, keepdims=True) - (
                    (1.0 / MB) * in_last
                ) * jnp.sum(g_t[hr] * from_state[hr], axis=0, keepdims=True)
                pm = pt * (within * r_row)
                pms = split(pm)
                pmts = split(pm.T)
                kn_h = (ks[0] * own_lane, ks[1] * own_lane)
                qn_h = (qs[0] * own_lane, qs[1] * own_lane)
                dq = dq - mm(pms, kn_h)
                dk = dk - mm(pmts, qn_h)
                pieces.append(
                    -mm((dzbs[0][hr], dzbs[1][hr]), split(scq * r_row))
                    - from_state[hr] * (r_row * in_last * (1.0 / MB))
                )
            p_s[rows] = jnp.concatenate(pieces, axis=0)
            w0s = split(w0[rows])
            wd = split(w_in[c, rows] - w0[rows])
            zero = jnp.zeros((), bf16)
            dzbn_c = (jnp.where(carried_col, dzbn[0], zero), jnp.where(carried_col, dzbn[1], zero))
            dq_out[here, lanes] = dq + mm(dzbn, w0s) + mm(dzbn_c, wd)
            dk_out[here, lanes] = dk

        def upstream(h, pv):
            hr = slice(h * hd, (h + 1) * hd)
            h1, h2 = consts[h]
            pm = jnp.sum(pv, axis=0, keepdims=True) * n_inv
            q = jnp.sum(pv * u_s[hr], axis=0, keepdims=True) * n_inv
            kf = jnp.sum(pv * f_s[hr], axis=0, keepdims=True) * n_inv
            kappa = kf - h1 * pm - h2 * q
            dz = (pv - pm) * bb_s[hr] - q * e2_s[hr] - kappa * u2_s[hr]
            return dz, pm, q

        def step(index, ps):
            now = lane_block == (CH // MB - 1 - index)
            new = []
            for h in range(heads):
                dz = jnp.where(now, upstream(h, ps[h])[0], 0.0)
                new.append(ps[h] - tall_dot(dz, at_s[h]))
            return tuple(new)

        ps = tuple(p_s[h * hd : (h + 1) * hd] for h in range(heads))
        ps = lax.fori_loop(0, CH // MB - 1, step, ps)

        for p in range(pairs):
            rows = slice(p * CH, (p + 1) * CH)
            lanes = slice(p * CH, (p + 1) * CH)
            qn = joined[here, p * CH : (p + 1) * CH]
            kn = joined[here, span + p * CH : span + (p + 1) * CH]
            vn = joined[here, 2 * span + p * CH : 2 * span + (p + 1) * CH]
            qs, ks = split(qn), split(kn)
            g_t = gt_s[rows]
            gts = split(g_t)
            dzs, des = [], []
            for hh in range(per):
                h = p * per + hh
                hr = slice(h * hd, (h + 1) * hd)
                dz, pm, q = upstream(h, ps[h])
                dzs.append(dz - jnp.sum(dz, axis=0, keepdims=True) * n_inv)
                z = z_in[hr, here]
                s = lax.rsqrt(jnp.sum(z * z, axis=0, keepdims=True) * n_inv + epsilon)
                des.append(s * (ps[h] - pm - u_s[hr] * q))
            dz = jnp.concatenate(dzs, axis=0)
            de = jnp.concatenate(des, axis=0)
            g_col = gain[rows]
            gde = g_col * de
            t_t = shift[rows] + (kn - vn).T
            dg_out[rows] += lane_sum((2.0 * g_col * u_s[rows] + t_t) * de)
            dsh_out[rows] += lane_sum(gde)
            gden = gde.T
            dv_out[here, lanes] = -gden
            dzn = split(dz.T)
            dk = dk_out[here, lanes] + gden
            r_rows = []
            for hh in range(per):
                h = p * per + hh
                r_row = rate_t[h : h + 1, here]
                own = (row_head == hh).astype(bf16)
                own_lane = (lane_head == hh).astype(bf16)
                rt = mm(dzn, (gts[0] * own, gts[1] * own))
                dr_out[h : h + 1, here] -= jnp.sum(rt * sc_s[h], axis=0, keepdims=True)
                ra = rt * (before * r_row)
                dk = dk - mm(split(ra + ra.T), (ks[0] * own_lane, ks[1] * own_lane))
                r_rows.append(jnp.broadcast_to(r_row * in_last * (1.0 / MB), (hd, CH)))
            gw = g_t * jnp.concatenate(r_rows, axis=0)
            w0s = split(w0[rows])
            wd = split(w_in[c, rows] - w0[rows])
            zero = jnp.zeros((), bf16)
            dzn_c = (jnp.where(carried_col, dzn[0], zero), jnp.where(carried_col, dzn[1], zero))
            dk = dk + mm(dzn, w0s) + mm(dzn_c, wd) - mm(split(gw.T), split(dw_s[rows]))
            dk_out[here, lanes] = dk
            dzb = dzb_s[rows]
            dzc = jnp.where(carried, dz, 0.0)
            dzbc = jnp.where(carried, dzb, 0.0)
            diag = jnp.where(block_diag, mm(split(dzc), ks) + mm(split(dzbc), qs), 0.0)
            rest = jnp.where(
                block_diag, mm(split(dz - dzc), ks) + mm(split(dzb - dzbc), qs), 0.0
            )
            dw = dw_s[rows]
            db = db_s[rows]
            dw_out[rows] += jnp.where(whole, 0.0, dw) + rest
            db_out[rows] += jnp.where(whole, 0.0, db) + lane_sum(dz - dzc + dzb - dzbc)
            dw_s[rows] = jnp.where(whole, dw, 0.0) + diag
            db_s[rows] = jnp.where(whole, db, 0.0) + lane_sum(dzc + dzbc)
        return carry

    lax.fori_loop(0, chunks, chunk, 0)


def ttt_backward(joined, rate_t, seg, seg_t, w0, b0, gain, shift, saved, dy, hd, heads):
    length = joined.shape[0]
    span = heads * hd
    shape = jax.ShapeDtypeStruct
    return pl.pallas_call(
        functools.partial(backward_body, hd=hd, heads=heads),
        out_shape=(
            shape((length, span), f32),
            shape((length, span), f32),
            shape((length, span), f32),
            shape((heads, length), f32),
            shape((span, CH), f32),
            shape((span, 1), f32),
            shape((span, 1), f32),
            shape((span, 1), f32),
        ),
        scratch_shapes=[
            pltpu.VMEM((span, CH), f32),
            pltpu.VMEM((span, 1), f32),
        ]
        + [pltpu.VMEM((span, CH), f32)] * 8
        + [
            pltpu.VMEM((heads, CH, 2 * CH), bf16),
            pltpu.VMEM((heads, CH, CH), f32),
        ],
        compiler_params=pltpu.CompilerParams(vmem_limit_bytes=48 << 20),
        name="inner_backward",
    )(joined, rate_t, seg, seg_t, w0, b0, gain, shift, *saved, dy)


def state_in(inner_weight, inner_bias):
    heads, hd, _ = inner_weight.shape
    per = CH // hd
    w_t = jnp.swapaxes(inner_weight, 1, 2)
    w_t = w_t - jnp.mean(w_t, axis=1, keepdims=True)
    placed = [
        jnp.pad(w_t[h], ((0, 0), ((h % per) * hd, CH - hd - (h % per) * hd)))
        for h in range(heads)
    ]
    b = inner_bias - jnp.mean(inner_bias, axis=1, keepdims=True)
    return jnp.concatenate(placed, axis=0), b.reshape(heads * hd, 1)


def state_back(dw, db, heads, hd):
    per = CH // hd
    parts = [
        dw[h * hd : (h + 1) * hd, (h % per) * hd : (h % per + 1) * hd] for h in range(heads)
    ]
    d = jnp.stack(parts)
    d = jnp.swapaxes(d - jnp.mean(d, axis=1, keepdims=True), 1, 2)
    b = db.reshape(heads, hd)
    return d, b - jnp.mean(b, axis=1, keepdims=True)


def product(left, right):
    return jnp.dot(left, right, precision=lax.Precision.HIGH, preferred_element_type=f32)


def left_product(left, right):
    return lax.dot_general(
        left, right, (((0,), (0,)), ((), ())), precision=lax.Precision.HIGH,
        preferred_element_type=f32,
    )


def right_product(left, right):
    return lax.dot_general(
        left, right, (((1,), (1,)), ((), ())), precision=lax.Precision.HIGH,
        preferred_element_type=f32,
    )


def heads_grid():
    size = lax.axis_size("heads")
    deep = 4 if size % 4 == 0 else 1
    return deep, size // deep


def heads_place():
    _, across = heads_grid()
    index = lax.axis_index("heads")
    return index // across, index % across


def shift(value, dz, dx):
    deep, across = heads_grid()
    pairs = [
        (h, (h // across + dz) % deep * across + (h % across + dx) % across)
        for h in range(deep * across)
    ]
    return lax.ppermute(value, "heads", pairs)


def swap(value, axis, bit):
    return lax.ppermute(value, axis, [(i, i ^ bit) for i in range(lax.axis_size(axis))])


def row_shift(value, step):
    size = lax.axis_size("rows")
    return lax.ppermute(value, "rows", [(r, (r + 2 * step) % size) for r in range(size)])


def butterfly(value, axis):
    bit = 1
    while bit < lax.axis_size(axis):
        value = value + swap(value, axis, bit)
        bit *= 2
    return value


def small_gather(value):
    size = lax.axis_size("heads")
    place = jnp.arange(size) == lax.axis_index("heads")
    place = place.reshape((size,) + (1,) * value.ndim)
    return butterfly(jnp.where(place, value[None], 0.0), "heads")


class Held:
    def __init__(self, value):
        self.value = value


def meet(values, held=()):
    out = lax.optimization_barrier(tuple(values) + tuple(item.value for item in held))
    for item, value in zip(held, out[len(values) :]):
        item.value = value
    return list(out[: len(values)])


def meet_one(value, *held):
    return meet([value], held)[0]


def turn(hooks, index):
    return hooks[index] if index < len(hooks) else ()


def gather_columns(value, hooks=()):
    deep, across = heads_grid()
    z, x = heads_place()
    rows, cols = value.shape
    out = jnp.zeros((rows, cols * deep * across), value.dtype)
    here = value
    for dz in range(deep):
        moved = [shift(here, 0, dx) for dx in range(1, across)]
        if dz + 1 < deep:
            moved.append(shift(here, 1, 0))
        moved = meet(moved, turn(hooks, dz))
        for dx, side in enumerate([here] + moved[: across - 1]):
            column = ((z - dz) % deep * across + (x - dx) % across) * cols
            out = lax.dynamic_update_slice(out, side, (0, column))
        here = moved[-1]
    return out


def scatter_columns(value, extra=None, hooks=()):
    deep, across = heads_grid()
    z, x = heads_place()
    rows, width = value.shape
    cols = width // (deep * across)

    def piece(dz, dx):
        column = ((z - dz) % deep * across + (x - dx) % across) * cols
        block = lax.dynamic_slice(value, (0, column), (rows, cols))
        if extra is not None:
            tail = lax.dynamic_slice(extra, (0, column), (extra.shape[0], cols))
            block = jnp.concatenate([block, tail], 0)
        return block

    total = None
    for index, dz in enumerate(list(range(1, deep)) + [0]):
        moved = [shift(piece(dz, dx), 0, dx) for dx in range(1, across)]
        if total is not None:
            moved.append(shift(total, 1, 0))
        total = piece(dz, 0)
        for item in meet(moved, turn(hooks, index)):
            total = total + item
    return total


def half_of(value, index, axis):
    size = value.shape[axis] // 2
    return lax.dynamic_slice_in_dim(value, index * size, size, axis)


def both_cores(value):
    return jnp.concatenate([value, swap(value, "rows", 1)], 0)


def tokens_half(value, core):
    return jnp.concatenate(
        [half_of(value, core, 1), swap(half_of(value, 1 - core, 1), "rows", 1)], 0
    )


def chips_along():
    return lax.axis_size("rows") // 2


def other_chips(value):
    return [row_shift(value, step) for step in range(1, chips_along())]


def place_body(core, own, other, *outs, axis, widths):
    first = core[0] == 0
    at = 0
    for out, width in zip(outs, widths):
        mine, its = (own[:, at : at + width], other[:, at : at + width]) if axis == 0 else (own[...], other[...])
        low = jnp.where(first, mine, its)
        high = jnp.where(first, its, mine)
        if axis == 0:
            out[0] = low
            out[1] = high
        else:
            out[:, : low.shape[1]] = low
            out[:, low.shape[1] :] = high
        at += width


def place(own, other, core, axis, widths):
    rows, cols = own.shape
    steps = max(n for n in (1, 2, 4) if rows % (8 * n) == 0)
    size = rows // steps
    part = pl.BlockSpec((size, cols), lambda i: (i, 0))
    if axis == 0:
        shapes = [(2, rows, width) for width in widths]
        specs = [pl.BlockSpec((2, size, width), lambda i: (0, i, 0)) for width in widths]
    else:
        shapes = [(rows, 2 * cols)]
        specs = [pl.BlockSpec((size, 2 * cols), lambda i: (i, 0))]
    out = pl.pallas_call(
        functools.partial(place_body, axis=axis, widths=widths),
        grid=(steps,),
        out_shape=[jax.ShapeDtypeStruct(shape, f32) for shape in shapes],
        in_specs=[pl.BlockSpec(memory_space=pltpu.SMEM), part, part],
        out_specs=specs,
        compiler_params=pltpu.CompilerParams(vmem_limit_bytes=48 << 20),
        name="place",
    )(core.reshape(1).astype(jnp.int32), own, other)
    return [o.reshape(2 * rows, -1) if axis == 0 else o for o in out]


def finish(total, core, axis, widths=None):
    widths = (total.shape[1],) if widths is None else widths
    return place(total, swap(total, "rows", 1), core, axis, widths)


def row_products(lefts, rights):
    total = None
    for left, right in zip(lefts, rights):
        part = left_product(left, right)
        total = part if total is None else total + part
    return total


class Along:
    def __init__(self, value, parts=4):
        size = value.shape[0] // parts
        self.own = value
        self.steps = [
            [Held(row_shift(value[i * size : (i + 1) * size], step)) for i in range(parts)]
            for step in range(1, chips_along())
        ]

    def __getitem__(self, i):
        return [step[i] for step in self.steps]

    def all(self):
        return [self.own] + [
            step[0].value if len(step) == 1
            else jnp.concatenate([item.value for item in step], 0)
            for step in self.steps
        ]


def silu_parts(a):
    sig = jax.nn.sigmoid(a)
    return a * sig, sig * (1.0 + a * (1.0 - sig))


def gelu_parts(v):
    k = 0.7978845608028654
    inner = k * (v + 0.044715 * v * v * v)
    th = jnp.tanh(inner)
    slope = 0.5 * (1.0 + th) + 0.5 * v * (1.0 - th * th) * k * (1.0 + 3 * 0.044715 * v * v)
    return 0.5 * v * (1.0 + th), slope


def on_device(
    stream,
    doc_starts,
    valid_mask,
    first_gain,
    w_query,
    w_key,
    w_value,
    w_rate,
    b_rate,
    inner_weight,
    inner_bias,
    inner_gain,
    inner_shift,
    post_gain,
    post_shift,
    w_gate_attn,
    w_out,
    second_gain,
    w_gate,
    w_up,
    w_down,
    cotangent,
):
    _, length, width = stream.shape
    tokens = stream.reshape(length, width)
    slab = second_gain.shape[0]
    column = lax.axis_index("heads") * slab
    core = lax.axis_index("rows") % 2
    heads, hd = inner_bias.shape
    span = heads * hd
    total_span = span * lax.axis_size("heads")
    gains = small_gather(jnp.stack([first_gain, second_gain]))
    gain_one = gains[:, 0].reshape(width)
    gain_two = gains[:, 1].reshape(width)
    grad_output = cotangent.reshape(length, slab)
    dy_held = Held(gather_columns(grad_output))

    w_joined = jnp.concatenate([w_query, w_key, w_value, w_gate_attn], axis=1)
    r1 = lax.rsqrt(jnp.mean(tokens * tokens, -1, keepdims=True) + epsilon)
    unit = tokens * r1
    unit_y = Along(tokens_half(unit, core))
    normed = unit * gain_one
    joined = product(normed, w_joined)
    rate_pre = lax.dot_general(
        w_rate, normed, (((0,), (1,)), ((), ())), precision=lax.Precision.HIGH,
        preferred_element_type=f32,
    )
    joined = meet_one(joined, *unit_y[0])
    gate_pre = joined[:, 3 * span :]
    sig = jax.nn.sigmoid(rate_pre + b_rate[:, None])
    rate_t = sig / hd
    rate = rate_t.T
    seg = jnp.cumsum(doc_starts.reshape(length)).astype(f32)
    seg, seg_t = seg[:, None], seg[None]
    w0, b0 = state_in(inner_weight, inner_bias)
    gain_col, shift_col = inner_gain.reshape(span, 1), inner_shift.reshape(span, 1)
    mixed, *saved = ttt_forward(
        joined, rate, rate_t, seg, seg_t, w0, b0, gain_col, shift_col, hd, heads
    )
    mixed = meet_one(mixed, *unit_y[1], dy_held)
    row_sums = butterfly(jnp.stack([jnp.sum(mixed, 1), jnp.sum(mixed * mixed, 1)]), "heads")
    row_mean = row_sums[0] / total_span
    inv_std = lax.rsqrt(row_sums[1] / total_span - row_mean * row_mean + epsilon)[:, None]
    centered = (mixed - row_mean[:, None]) * inv_std
    shaped = centered * post_gain + post_shift
    gate_act, gate_slope = gelu_parts(gate_pre)
    gathered = gather_columns(gate_act * shaped, [unit_y[2], (), unit_y[3]])
    gathered_y = Along(tokens_half(gathered, core))
    attn = product(gathered, w_out)
    stream_cols = lax.dynamic_slice_in_dim(tokens, column, slab, 1)
    hidden = stream_cols + attn
    whole = gather_columns(hidden, [(), (), gathered_y[0], gathered_y[1]])
    dy_full = dy_held.value

    r2 = lax.rsqrt(jnp.mean(whole * whole, -1, keepdims=True) + epsilon)
    hnorm = whole * r2 * gain_two
    hnorm_y = Along(tokens_half(hnorm, core))
    a = product(hnorm, w_gate)
    a = meet_one(a, *gathered_y[2])
    c = product(hnorm, w_up)
    act, slope = silu_parts(a)
    m = act * c
    dm = meet_one(right_product(dy_full, w_down), *gathered_y[3])
    da = dm * c * slope
    dc = dm * act
    da_y, dc_y = Along(da, 1), Along(dc, 1)
    dhnorm = right_product(da, w_gate) + right_product(dc, w_up)
    dhnorm = meet_one(dhnorm, *hnorm_y[0])
    d_gain_two = jnp.sum(dhnorm * whole * r2, 0, keepdims=True)
    weighted = dhnorm * gain_two
    d_whole = r2 * weighted - whole * (r2 * r2 * r2) * jnp.mean(
        whole * weighted, -1, keepdims=True
    )
    pad = jnp.zeros((7, width), f32)
    da_pair, dc_pair = both_cores(da), both_cores(dc)
    own_gate = Held(left_product(da_pair, hnorm_y.own))
    own_up = Held(left_product(dc_pair, hnorm_y.own))
    own_down = Held(left_product(both_cores(m), tokens_half(dy_full, core)))
    ffn_part = Held(product(m, w_down))
    d_part = scatter_columns(
        d_whole,
        jnp.concatenate([d_gain_two, pad], 0),
        [[*hnorm_y[1], ffn_part], [*hnorm_y[2], own_gate], [*hnorm_y[3], own_up], [*da_y[0], own_down]],
    )
    d_hidden = grad_output + d_part[:length]
    d_gain_two = d_part[length]
    d_hidden_y = Along(d_hidden, 1)
    own_out = Held(left_product(gathered_y.own, both_cores(d_hidden)))

    d_gated = scatter_columns(
        right_product(d_hidden, w_out),
        None,
        [[], [*dc_y[0], own_out], [*d_hidden_y[0]]],
    )
    d_gated = meet_one(d_gated, ffn_part, own_down)
    down_y = [Held(item) for item in other_chips(own_down.value)]
    deep, across = heads_grid()
    z, x = heads_place()

    def tile_set(dx):
        return jnp.concatenate(
            [
                lax.dynamic_slice_in_dim(
                    ffn_part.value, (i * across + (x - dx) % across) * slab, slab, 1
                )
                for i in range(deep)
            ],
            1,
        )

    ffn_x = [Held(shift(tile_set(dx), 0, dx)) for dx in range(1, across)]
    d_shaped = d_gated * gate_act
    d_gate_pre = d_gated * shaped * gate_slope
    d_post_gain = jnp.sum(d_shaped * centered, 0)
    d_post_shift = jnp.sum(d_shaped, 0)
    d_center = d_shaped * post_gain
    back_sums = butterfly(
        jnp.stack([jnp.sum(d_center, 1), jnp.sum(d_center * centered, 1)]), "heads"
    )
    d_mixed = inv_std * (
        d_center - back_sums[0][:, None] / total_span
        - centered * back_sums[1][:, None] / total_span
    )
    dq, dk, dv, d_rate, dw, db, dg, dsh = ttt_backward(
        joined, rate_t, seg, seg_t, w0, b0, gain_col, shift_col, saved, d_mixed, hd, heads
    )
    dq = meet_one(dq, *ffn_x)
    ffn_sum = tile_set(0)
    for item in ffn_x:
        ffn_sum = ffn_sum + item.value
    ffn = None
    for dz in list(range(1, deep)) + [0]:
        part = lax.dynamic_slice_in_dim(ffn_sum, (z - dz) % deep * slab, slab, 1)
        ffn = part if ffn is None else shift(ffn, 1, 0) + part
    output = hidden + ffn
    d_inner_weight, d_inner_bias = state_back(dw, db, heads, hd)
    d_rate_pre = d_rate * rate_t * (1.0 - sig)
    d_joined = jnp.concatenate([dq, dk, dv, d_gate_pre], 1)
    d_joined_y, d_rate_y = Along(d_joined, 1), Along(d_rate_pre, 1)
    d_normed = right_product(d_joined, w_joined) + lax.dot_general(
        d_rate_pre, w_rate, (((0,), (1,)), ((), ())), precision=lax.Precision.HIGH,
        preferred_element_type=f32,
    )
    d_gain_one = jnp.sum(d_normed * tokens * r1, 0, keepdims=True)
    weighted = d_normed * gain_one
    d_tokens = r1 * weighted - tokens * (r1 * r1 * r1) * jnp.mean(
        tokens * weighted, -1, keepdims=True
    )

    def cores(values):
        return [both_cores(value) for value in values]

    def total(own, lefts, rights):
        for left, right in zip(lefts[1:], rights[1:]):
            own = own + left_product(left, right)
        return Held(own)

    gain_half = half_of(gain_one, core, 0)
    normed_pairs = [pair * gain_half for pair in unit_y.all()]
    own_joined = Held(left_product(normed_pairs[0], both_cores(d_joined)))
    all_gate = total(own_gate.value, cores(da_y.all()), hnorm_y.all())
    all_up = total(own_up.value, cores(dc_y.all()), hnorm_y.all())
    all_out = total(own_out.value, gathered_y.all(), cores(d_hidden_y.all()))
    d_part = scatter_columns(
        d_tokens,
        jnp.concatenate([d_gain_one, pad], 0),
        [[own_joined], [all_gate, *down_y], [all_up, *d_joined_y[0], *d_rate_y[0]], [all_out]],
    )
    d_stream = d_hidden + d_part[:length]
    d_gain_one = d_part[length]

    (g_gate,) = finish(all_gate.value, core, 1)
    (g_up,) = finish(all_up.value, core, 1)
    (g_out,) = finish(all_out.value, core, 0)
    (g_down,) = finish(sum((item.value for item in down_y), own_down.value), core, 1)
    all_joined = total(own_joined.value, normed_pairs, cores(d_joined_y.all()))
    g_query, g_key, g_value, g_gate_attn = finish(all_joined.value, core, 0, (span,) * 4)
    g_rate = None
    for pair, d in zip(normed_pairs, d_rate_y.all()):
        part = product(jnp.concatenate([d, swap(d, "rows", 1)], 1), pair)
        g_rate = part if g_rate is None else g_rate + part
    ends = (g_rate, swap(g_rate, "rows", 1))
    g_rate = jnp.where(core == 0, jnp.concatenate(ends, 1), jnp.concatenate(ends[::-1], 1))

    weights = valid_mask.reshape(-1).astype(f32)[:, None]
    stats = jnp.stack(
        [
            jnp.sum(weights * member * member)
            for member in (stream_cols, attn, hidden, ffn, output)
        ]
        + [jnp.sum(weights) / lax.axis_size("heads")]
    )
    stats = butterfly(stats, "heads")
    small = [
        d_gain_one, jnp.sum(d_rate_pre, 1), d_inner_weight, d_inner_bias, dg, dsh,
        d_post_gain, d_post_shift, d_gain_two, stats,
    ]
    packed = butterfly(jnp.concatenate([item.reshape(-1) for item in small]), "rows")
    parts = []
    at = 0
    for item in small:
        parts.append(packed[at : at + item.size])
        at += item.size
    stats = parts[9]
    rms_values = jnp.sqrt(stats[:5] / (stats[5] * width))
    return (
        output.reshape(1, length, slab),
        d_stream.reshape(1, length, slab),
        parts[0],
        g_query,
        g_key,
        g_value,
        g_rate.T,
        parts[1],
        parts[2].reshape(heads, hd, hd),
        parts[3].reshape(heads, hd),
        parts[4].reshape(heads, hd),
        parts[5].reshape(heads, hd),
        parts[6],
        parts[7],
        g_gate_attn,
        g_out,
        parts[8],
        g_gate.T,
        g_up.T,
        g_down,
        rms_values,
    )


def solution(mesh):
    in_specs = (
        P("rows", None, None),
        P("rows", None),
        P("rows", None),
        P("heads"),
        P(None, "heads"),
        P(None, "heads"),
        P(None, "heads"),
        P(None, "heads"),
        P("heads"),
        P("heads", None, None),
        P("heads", None),
        P("heads", None),
        P("heads", None),
        P("heads"),
        P("heads"),
        P(None, "heads"),
        P(None, "heads"),
        P("heads"),
        P(None, "heads"),
        P(None, "heads"),
        P("heads", None),
        P("rows", None, "heads"),
    )
    out_specs = (
        P("rows", None, "heads"),
        P("rows", None, "heads"),
        P("heads"),
        P(None, "heads"),
        P(None, "heads"),
        P(None, "heads"),
        P(None, "heads"),
        P("heads"),
        P("heads", None, None),
        P("heads", None),
        P("heads", None),
        P("heads", None),
        P("heads"),
        P("heads"),
        P(None, "heads"),
        P(None, "heads"),
        P("heads"),
        P(None, "heads"),
        P(None, "heads"),
        P("heads", None),
        P(),
    )
    return jax.shard_map(
        on_device, mesh=mesh, in_specs=in_specs, out_specs=out_specs, check_vma=False
    )
```

```python
import functools
import jax, jax.numpy as jnp
from jax import lax
from jax.experimental import pallas as pl
from jax.experimental.pallas import tpu as pltpu

from jax.sharding import PartitionSpec as P

MB = 16
CH = 128
epsilon = 1e-06
f32 = jnp.float32
bf16 = jnp.bfloat16
NN = ((1,), (0,))


def split(x):
    hi = x.astype(bf16)
    return hi, (x - hi.astype(f32)).astype(bf16)


def mm(a, b, dims=NN):
    def one(p, q):
        return lax.dot_general(p, q, (dims, ((), ())), preferred_element_type=f32)

    return one(a[0], b[0]) + (one(a[0], b[1]) + one(a[1], b[0]))


def wide(x):
    hi, lo = split(x)
    return jnp.concatenate([hi, lo], axis=1)


def tall_dot(x, pair):
    rows = x.shape[0]
    cols = pair.shape[1] // 2
    hi, lo = split(x)
    out = lax.dot_general(
        jnp.concatenate([hi, lo], axis=0), pair, (NN, ((), ())), preferred_element_type=f32
    )
    top, low = out[:rows], out[rows:]
    return top[:, :cols] + (top[:, cols:] + low[:, :cols])


def iota(shape, dim):
    return lax.broadcasted_iota(jnp.int32, shape, dim)


def head_sum(x, hd):
    rows, cols = x.shape
    parts = [
        jnp.broadcast_to(jnp.sum(x[i : i + hd], axis=0, keepdims=True), (hd, cols))
        for i in range(0, rows, hd)
    ]
    return parts[0] if len(parts) == 1 else jnp.concatenate(parts, axis=0)


def lane_sum(x):
    return jnp.sum(x, axis=1, keepdims=True)


def coefficients(transposed):
    source = iota((CH, CH), 1 if transposed else 0)
    target = iota((CH, CH), 0 if transposed else 1)
    before = (source // MB < target // MB).astype(f32) * (1.0 / MB)
    inside = ((source // MB == target // MB) & (source <= target)).astype(f32)
    return before, before + inside / ((target % MB) + 1).astype(f32)


def forward_body(
    joined, rate, rate_t, seg, seg_t, w0, b0, gain, shift, mixed, z_out, zb_out, w_out, b_out,
    w_s, b_s, z_s, tau_s, a_s, m_s, *, hd, heads,
):
    pairs = heads * hd // CH
    per = CH // hd
    span = heads * hd
    chunks = joined.shape[0] // CH
    n_inv = 1.0 / hd
    row_head = iota((CH, CH), 0) // hd
    lane_head = iota((CH, CH), 1) // hd
    lane_block = iota((hd, CH), 1) // MB
    block_diag = row_head == lane_head
    w_s[...] = jnp.zeros_like(w_s)
    b_s[...] = jnp.zeros_like(b_s)

    def chunk(c, carry):
        ts = pl.multiple_of(c * CH, CH)
        here = pl.ds(ts, CH)
        seg_row = seg_t[:, here]
        seg_col = seg[here, :]
        last_seg = seg_row[:, CH - 1 : CH]
        prev = jnp.max(jnp.where(iota(seg_t.shape, 1) < ts, seg_t[...], 0.0), keepdims=True)
        carried = seg_row == prev
        in_last = (seg_row == last_seg).astype(f32)
        whole = last_seg == prev
        same = seg_col == seg_row
        before, within = coefficients(False)
        before = jnp.where(same, before, 0.0)
        within = jnp.where(same, within, 0.0)
        for p in range(pairs):
            rows = slice(p * CH, (p + 1) * CH)
            kn = joined[here, span + p * CH : span + (p + 1) * CH]
            qn = joined[here, p * CH : (p + 1) * CH]
            vn = joined[here, 2 * span + p * CH : 2 * span + (p + 1) * CH]
            k_t, q_t, v_t = kn.T, qn.T, vn.T
            ks, kts, qts = split(kn), split(k_t), split(q_t)
            ws, w0s = split(w_s[rows]), split(w0[rows])
            bias = jnp.where(carried, b_s[rows], b0[rows])
            z_s[rows] = jnp.where(carried, mm(ws, kts), mm(w0s, kts)) + bias
            zb_out[rows, here] = jnp.where(carried, mm(ws, qts), mm(w0s, qts)) + bias
            w_out[c, rows] = w_s[rows]
            b_out[c, rows] = b_s[rows]
            tau_s[rows] = gain[rows] * (shift[rows] - v_t + k_t)
            for hh in range(per):
                h = p * per + hh
                own = (row_head == hh).astype(bf16)
                r_col = rate[here, h : h + 1]
                score = mm(ks, (kts[0] * own, kts[1] * own))
                a_s[h] = wide((score + 1.0) * (before * r_col))
                score = mm(ks, (qts[0] * own, qts[1] * own))
                m_s[h] = wide((score + 1.0) * (within * r_col))

        gsq = [jnp.broadcast_to(gain[h * hd : (h + 1) * hd] ** 2, (hd, CH)) for h in range(heads)]
        tsum = [
            jnp.sum(tau_s[h * hd : (h + 1) * hd], axis=0, keepdims=True) * n_inv
            for h in range(heads)
        ]

        def inner(h, z):
            tau = tau_s[h * hd : (h + 1) * hd]
            zg = z * gsq[h]
            m2 = jnp.sum(z * z, axis=0, keepdims=True) * n_inv
            a1 = jnp.sum(zg, axis=0, keepdims=True) * n_inv
            a2 = jnp.sum(z * zg, axis=0, keepdims=True) * n_inv
            a3 = jnp.sum(z * tau, axis=0, keepdims=True) * n_inv
            s = lax.rsqrt(m2 + epsilon)
            c_eu = s * (s * a2 + a3)
            e_mean = s * a1 + tsum[h]
            return (s * s) * (zg - c_eu * z) + s * (tau - e_mean)

        def step(t, zs):
            now = lane_block == t
            new = []
            for h in range(heads):
                g = jnp.where(now, inner(h, zs[h]), 0.0)
                new.append(zs[h] - tall_dot(g, a_s[h]))
            return tuple(new)

        zs = tuple(z_s[h * hd : (h + 1) * hd] for h in range(heads))
        zs = lax.fori_loop(0, CH // MB - 1, step, zs)
        for p in range(pairs):
            rows = slice(p * CH, (p + 1) * CH)
            gs = []
            outs = []
            for hh in range(per):
                h = p * per + hh
                hr = slice(h * hd, (h + 1) * hd)
                z_out[hr, here] = zs[h]
                g = inner(h, zs[h])
                zb = zb_out[hr, here] - tall_dot(g, m_s[h])
                zb_out[hr, here] = zb
                sb = lax.rsqrt(jnp.sum(zb * zb, axis=0, keepdims=True) * n_inv + epsilon)
                outs.append(zb * sb * gain[hr] + shift[hr])
                gs.append(g * (rate_t[h : h + 1, here] * in_last * (1.0 / MB)))
            gw = jnp.concatenate(gs, axis=0)
            lanes = slice(p * CH, (p + 1) * CH)
            mixed[here, lanes] = joined[here, lanes] + jnp.concatenate(outs, axis=0).T
            kn = joined[here, span + p * CH : span + (p + 1) * CH]
            upd = mm(split(gw), split(kn))
            w_s[rows] = jnp.where(whole, w_s[rows], w0[rows]) - jnp.where(block_diag, upd, 0.0)
            b_s[rows] = jnp.where(whole, b_s[rows], b0[rows]) - lane_sum(gw)
        return carry

    lax.fori_loop(0, chunks, chunk, 0)


def ttt_forward(joined, rate, rate_t, seg, seg_t, w0, b0, gain, shift, hd, heads):
    length = joined.shape[0]
    span = heads * hd
    chunks = length // CH
    shape = jax.ShapeDtypeStruct
    return pl.pallas_call(
        functools.partial(forward_body, hd=hd, heads=heads),
        out_shape=(
            shape((length, span), f32),
            shape((span, length), f32),
            shape((span, length), f32),
            shape((chunks, span, CH), f32),
            shape((chunks, span, 1), f32),
        ),
        scratch_shapes=[
            pltpu.VMEM((span, CH), f32),
            pltpu.VMEM((span, 1), f32),
            pltpu.VMEM((span, CH), f32),
            pltpu.VMEM((span, CH), f32),
            pltpu.VMEM((heads, CH, 2 * CH), bf16),
            pltpu.VMEM((heads, CH, 2 * CH), bf16),
        ],
        compiler_params=pltpu.CompilerParams(vmem_limit_bytes=48 << 20),
        name="inner_forward",
    )(joined, rate, rate_t, seg, seg_t, w0, b0, gain, shift)


def backward_body(
    joined, rate_t, seg, seg_t, w0, b0, gain, shift, z_in, zb_in, w_in, b_in, dy,
    dq_out, dk_out, dv_out, dr_out, dw_out, db_out, dg_out, dsh_out,
    dw_s, db_s, p_s, u_s, f_s, bb_s, e2_s, u2_s, gt_s, dzb_s, at_s, sc_s,
    *, hd, heads,
):
    pairs = heads * hd // CH
    per = CH // hd
    span = heads * hd
    chunks = joined.shape[0] // CH
    n_inv = 1.0 / hd
    row_head = iota((CH, CH), 0) // hd
    lane_head = iota((CH, CH), 1) // hd
    lane_block = iota((hd, CH), 1) // MB
    block_diag = row_head == lane_head
    for ref in (dw_s, db_s, dw_out, db_out, dg_out, dsh_out):
        ref[...] = jnp.zeros_like(ref)

    def mean(x):
        return head_sum(x, hd) * n_inv

    def chunk(index, carry):
        c = chunks - 1 - index
        ts = pl.multiple_of(c * CH, CH)
        here = pl.ds(ts, CH)
        seg_row = seg_t[:, here]
        seg_col = seg[here, :]
        last_seg = seg_row[:, CH - 1 : CH]
        prev = jnp.max(jnp.where(iota(seg_t.shape, 1) < ts, seg_t[...], 0.0), keepdims=True)
        carried = seg_row == prev
        carried_col = seg_col == prev
        in_last = (seg_row == last_seg).astype(f32)
        whole = last_seg == prev
        same = seg_col == seg_row
        before, within = coefficients(True)
        before = jnp.where(same, before, 0.0)
        within = jnp.where(same, within, 0.0)
        consts = {}
        for p in range(pairs):
            rows = slice(p * CH, (p + 1) * CH)
            lanes = slice(p * CH, (p + 1) * CH)
            qn = joined[here, p * CH : (p + 1) * CH]
            kn = joined[here, span + p * CH : span + (p + 1) * CH]
            vn = joined[here, 2 * span + p * CH : 2 * span + (p + 1) * CH]
            k_t, v_t, dy_t = kn.T, vn.T, dy[here, lanes].T
            qs, ks, kts = split(qn), split(kn), split(k_t)
            g_col = gain[rows]
            gsq = g_col * g_col
            zb = zb_in[rows, here]
            sb = lax.rsqrt(mean(zb * zb) + epsilon)
            ub = zb * sb
            dg_out[rows] += lane_sum(dy_t * ub)
            dsh_out[rows] += lane_sum(dy_t)
            pb = dy_t * g_col
            dzb = sb * (pb - mean(pb) - ub * mean(pb * ub))
            dzb_s[rows] = dzb
            z = z_in[rows, here]
            s = lax.rsqrt(mean(z * z) + epsilon)
            u = z * s
            gu = gsq * u
            e = gu + g_col * (shift[rows] - v_t + k_t)
            c_eu = mean(e * u)
            g_t = s * (e - mean(e) - u * c_eu)
            gt_s[rows] = g_t
            u_s[rows] = u
            f_s[rows] = g_t + s * gu
            bb_s[rows] = (s * s) * (gsq - c_eu)
            e2_s[rows] = (s * s) * (e + gu)
            u2_s[rows] = s * u
            h1 = s * mean(gu)
            h2 = 2.0 * s * c_eu + s * mean(gu * u)
            dzbs = split(dzb)
            gts = split(g_t)
            dzbn = split(dzb.T)
            from_state = mm(split(dw_s[rows]), kts) + db_s[rows]
            pieces = []
            dq = dy[here, lanes]
            dk = jnp.zeros((CH, CH), f32)
            for hh in range(per):
                h = p * per + hh
                hr = slice(hh * hd, (hh + 1) * hd)
                r_row = rate_t[h : h + 1, here]
                consts[h] = (h1[hh * hd : hh * hd + 1], h2[hh * hd : hh * hd + 1])
                own = (row_head == hh).astype(bf16)
                own_lane = (lane_head == hh).astype(bf16)
                kt_h = (kts[0] * own, kts[1] * own)
                sc = (mm(ks, kt_h) + 1.0) * before
                sc_s[h] = sc
                at_s[h] = wide(sc * r_row)
                scq = (mm(qs, kt_h) + 1.0) * within
                pt = mm(dzbn, (gts[0] * own, gts[1] * own))
                dr_out[h : h + 1, here] = -jnp.sum(pt * scq, axis=0, keepdims=True) - (
                    (1.0 / MB) * in_last
                ) * jnp.sum(g_t[hr] * from_state[hr], axis=0, keepdims=True)
                pm = pt * (within * r_row)
                pms = split(pm)
                pmts = split(pm.T)
                kn_h = (ks[0] * own_lane, ks[1] * own_lane)
                qn_h = (qs[0] * own_lane, qs[1] * own_lane)
                dq = dq - mm(pms, kn_h)
                dk = dk - mm(pmts, qn_h)
                pieces.append(
                    -mm((dzbs[0][hr], dzbs[1][hr]), split(scq * r_row))
                    - from_state[hr] * (r_row * in_last * (1.0 / MB))
                )
            p_s[rows] = jnp.concatenate(pieces, axis=0)
            w0s = split(w0[rows])
            wd = split(w_in[c, rows] - w0[rows])
            zero = jnp.zeros((), bf16)
            dzbn_c = (jnp.where(carried_col, dzbn[0], zero), jnp.where(carried_col, dzbn[1], zero))
            dq_out[here, lanes] = dq + mm(dzbn, w0s) + mm(dzbn_c, wd)
            dk_out[here, lanes] = dk

        def upstream(h, pv):
            hr = slice(h * hd, (h + 1) * hd)
            h1, h2 = consts[h]
            pm = jnp.sum(pv, axis=0, keepdims=True) * n_inv
            q = jnp.sum(pv * u_s[hr], axis=0, keepdims=True) * n_inv
            kf = jnp.sum(pv * f_s[hr], axis=0, keepdims=True) * n_inv
            kappa = kf - h1 * pm - h2 * q
            dz = (pv - pm) * bb_s[hr] - q * e2_s[hr] - kappa * u2_s[hr]
            return dz, pm, q

        def step(index, ps):
            now = lane_block == (CH // MB - 1 - index)
            new = []
            for h in range(heads):
                dz = jnp.where(now, upstream(h, ps[h])[0], 0.0)
                new.append(ps[h] - tall_dot(dz, at_s[h]))
            return tuple(new)

        ps = tuple(p_s[h * hd : (h + 1) * hd] for h in range(heads))
        ps = lax.fori_loop(0, CH // MB - 1, step, ps)

        for p in range(pairs):
            rows = slice(p * CH, (p + 1) * CH)
            lanes = slice(p * CH, (p + 1) * CH)
            qn = joined[here, p * CH : (p + 1) * CH]
            kn = joined[here, span + p * CH : span + (p + 1) * CH]
            vn = joined[here, 2 * span + p * CH : 2 * span + (p + 1) * CH]
            qs, ks = split(qn), split(kn)
            g_t = gt_s[rows]
            gts = split(g_t)
            dzs, des = [], []
            for hh in range(per):
                h = p * per + hh
                hr = slice(h * hd, (h + 1) * hd)
                dz, pm, q = upstream(h, ps[h])
                dzs.append(dz - jnp.sum(dz, axis=0, keepdims=True) * n_inv)
                z = z_in[hr, here]
                s = lax.rsqrt(jnp.sum(z * z, axis=0, keepdims=True) * n_inv + epsilon)
                des.append(s * (ps[h] - pm - u_s[hr] * q))
            dz = jnp.concatenate(dzs, axis=0)
            de = jnp.concatenate(des, axis=0)
            g_col = gain[rows]
            gde = g_col * de
            t_t = shift[rows] + (kn - vn).T
            dg_out[rows] += lane_sum((2.0 * g_col * u_s[rows] + t_t) * de)
            dsh_out[rows] += lane_sum(gde)
            gden = gde.T
            dv_out[here, lanes] = -gden
            dzn = split(dz.T)
            dk = dk_out[here, lanes] + gden
            r_rows = []
            for hh in range(per):
                h = p * per + hh
                r_row = rate_t[h : h + 1, here]
                own = (row_head == hh).astype(bf16)
                own_lane = (lane_head == hh).astype(bf16)
                rt = mm(dzn, (gts[0] * own, gts[1] * own))
                dr_out[h : h + 1, here] -= jnp.sum(rt * sc_s[h], axis=0, keepdims=True)
                ra = rt * (before * r_row)
                dk = dk - mm(split(ra + ra.T), (ks[0] * own_lane, ks[1] * own_lane))
                r_rows.append(jnp.broadcast_to(r_row * in_last * (1.0 / MB), (hd, CH)))
            gw = g_t * jnp.concatenate(r_rows, axis=0)
            w0s = split(w0[rows])
            wd = split(w_in[c, rows] - w0[rows])
            zero = jnp.zeros((), bf16)
            dzn_c = (jnp.where(carried_col, dzn[0], zero), jnp.where(carried_col, dzn[1], zero))
            dk = dk + mm(dzn, w0s) + mm(dzn_c, wd) - mm(split(gw.T), split(dw_s[rows]))
            dk_out[here, lanes] = dk
            dzb = dzb_s[rows]
            dzc = jnp.where(carried, dz, 0.0)
            dzbc = jnp.where(carried, dzb, 0.0)
            diag = jnp.where(block_diag, mm(split(dzc), ks) + mm(split(dzbc), qs), 0.0)
            rest = jnp.where(
                block_diag, mm(split(dz - dzc), ks) + mm(split(dzb - dzbc), qs), 0.0
            )
            dw = dw_s[rows]
            db = db_s[rows]
            dw_out[rows] += jnp.where(whole, 0.0, dw) + rest
            db_out[rows] += jnp.where(whole, 0.0, db) + lane_sum(dz - dzc + dzb - dzbc)
            dw_s[rows] = jnp.where(whole, dw, 0.0) + diag
            db_s[rows] = jnp.where(whole, db, 0.0) + lane_sum(dzc + dzbc)
        return carry

    lax.fori_loop(0, chunks, chunk, 0)


def ttt_backward(joined, rate_t, seg, seg_t, w0, b0, gain, shift, saved, dy, hd, heads):
    length = joined.shape[0]
    span = heads * hd
    shape = jax.ShapeDtypeStruct
    return pl.pallas_call(
        functools.partial(backward_body, hd=hd, heads=heads),
        out_shape=(
            shape((length, span), f32),
            shape((length, span), f32),
            shape((length, span), f32),
            shape((heads, length), f32),
            shape((span, CH), f32),
            shape((span, 1), f32),
            shape((span, 1), f32),
            shape((span, 1), f32),
        ),
        scratch_shapes=[
            pltpu.VMEM((span, CH), f32),
            pltpu.VMEM((span, 1), f32),
        ]
        + [pltpu.VMEM((span, CH), f32)] * 8
        + [
            pltpu.VMEM((heads, CH, 2 * CH), bf16),
            pltpu.VMEM((heads, CH, CH), f32),
        ],
        compiler_params=pltpu.CompilerParams(vmem_limit_bytes=48 << 20),
        name="inner_backward",
    )(joined, rate_t, seg, seg_t, w0, b0, gain, shift, *saved, dy)


def state_in(inner_weight, inner_bias):
    heads, hd, _ = inner_weight.shape
    per = CH // hd
    w_t = jnp.swapaxes(inner_weight, 1, 2)
    w_t = w_t - jnp.mean(w_t, axis=1, keepdims=True)
    placed = [
        jnp.pad(w_t[h], ((0, 0), ((h % per) * hd, CH - hd - (h % per) * hd)))
        for h in range(heads)
    ]
    b = inner_bias - jnp.mean(inner_bias, axis=1, keepdims=True)
    return jnp.concatenate(placed, axis=0), b.reshape(heads * hd, 1)


def state_back(dw, db, heads, hd):
    per = CH // hd
    parts = [
        dw[h * hd : (h + 1) * hd, (h % per) * hd : (h % per + 1) * hd] for h in range(heads)
    ]
    d = jnp.stack(parts)
    d = jnp.swapaxes(d - jnp.mean(d, axis=1, keepdims=True), 1, 2)
    b = db.reshape(heads, hd)
    return d, b - jnp.mean(b, axis=1, keepdims=True)


def product(left, right):
    return jnp.dot(left, right, precision=lax.Precision.HIGH, preferred_element_type=f32)


def left_product(left, right):
    return lax.dot_general(
        left, right, (((0,), (0,)), ((), ())), precision=lax.Precision.HIGH,
        preferred_element_type=f32,
    )


def right_product(left, right):
    return lax.dot_general(
        left, right, (((1,), (1,)), ((), ())), precision=lax.Precision.HIGH,
        preferred_element_type=f32,
    )


def heads_grid():
    size = lax.axis_size("heads")
    deep = 4 if size % 4 == 0 else 1
    return deep, size // deep


def heads_place():
    _, across = heads_grid()
    index = lax.axis_index("heads")
    return index // across, index % across


def shift(value, dz, dx):
    deep, across = heads_grid()
    pairs = [
        (h, (h // across + dz) % deep * across + (h % across + dx) % across)
        for h in range(deep * across)
    ]
    return lax.ppermute(value, "heads", pairs)


def swap(value, axis, bit):
    return lax.ppermute(value, axis, [(i, i ^ bit) for i in range(lax.axis_size(axis))])


def row_shift(value, step):
    size = lax.axis_size("rows")
    return lax.ppermute(value, "rows", [(r, (r + 2 * step) % size) for r in range(size)])


def butterfly(value, axis):
    bit = 1
    while bit < lax.axis_size(axis):
        value = value + swap(value, axis, bit)
        bit *= 2
    return value


def small_gather(value):
    size = lax.axis_size("heads")
    place = jnp.arange(size) == lax.axis_index("heads")
    place = place.reshape((size,) + (1,) * value.ndim)
    return butterfly(jnp.where(place, value[None], 0.0), "heads")


class Held:
    def __init__(self, value):
        self.value = value


def meet(values, held=()):
    out = lax.optimization_barrier(tuple(values) + tuple(item.value for item in held))
    for item, value in zip(held, out[len(values) :]):
        item.value = value
    return list(out[: len(values)])


def meet_one(value, *held):
    return meet([value], held)[0]


def turn(hooks, index):
    hook = hooks[index] if index < len(hooks) else ()
    return hook() if callable(hook) else hook


def gather_columns(value, hooks=()):
    deep, across = heads_grid()
    z, x = heads_place()
    rows, cols = value.shape
    out = jnp.zeros((rows, cols * deep * across), value.dtype)
    here, ready = value, [(0, 0, value)]
    for dz in range(deep):
        moved = [shift(here, 0, dx) for dx in range(1, across)]
        if dz + 1 < deep:
            moved.append(shift(here, 1, 0))
        for oz, ox, item in ready:
            column = ((z - oz) % deep * across + (x - ox) % across) * cols
            out = lax.dynamic_update_slice(out, item, (0, column))
        *moved, out = meet(moved + [out], turn(hooks, dz))
        ready = [(dz, dx, moved[dx - 1]) for dx in range(1, across)]
        if dz + 1 < deep:
            here = moved[-1]
            ready.append((dz + 1, 0, here))
    for oz, ox, item in ready:
        column = ((z - oz) % deep * across + (x - ox) % across) * cols
        out = lax.dynamic_update_slice(out, item, (0, column))
    return out


def scatter_columns(value, extra=None, hooks=()):
    deep, across = heads_grid()
    z, x = heads_place()
    rows, width = value.shape
    cols = width // (deep * across)

    def piece(dz, dx):
        column = ((z - dz) % deep * across + (x - dx) % across) * cols
        block = lax.dynamic_slice(value, (0, column), (rows, cols))
        if extra is not None:
            tail = lax.dynamic_slice(extra, (0, column), (extra.shape[0], cols))
            block = jnp.concatenate([block, tail], 0)
        return block

    total = None
    for index, dz in enumerate(list(range(1, deep)) + [0]):
        moved = [shift(piece(dz, dx), 0, dx) for dx in range(1, across)]
        if total is not None:
            moved.append(shift(total, 1, 0))
        total = piece(dz, 0)
        for item in meet(moved, turn(hooks, index)):
            total = total + item
    return total


def half_of(value, index, axis):
    size = value.shape[axis] // 2
    return lax.dynamic_slice_in_dim(value, index * size, size, axis)


def both_cores(value):
    return jnp.concatenate([value, swap(value, "rows", 1)], 0)


def tokens_half(value, core):
    return jnp.concatenate(
        [half_of(value, core, 1), swap(half_of(value, 1 - core, 1), "rows", 1)], 0
    )


def chips_along():
    return lax.axis_size("rows") // 2


def other_chips(value):
    return [row_shift(value, step) for step in range(1, chips_along())]


def place_body(core, own, other, *outs, axis, widths):
    first = core[0] == 0
    at = 0
    for out, width in zip(outs, widths):
        mine, its = (own[:, at : at + width], other[:, at : at + width]) if axis == 0 else (own[...], other[...])
        low = jnp.where(first, mine, its)
        high = jnp.where(first, its, mine)
        if axis == 0:
            out[0] = low
            out[1] = high
        else:
            out[:, : low.shape[1]] = low
            out[:, low.shape[1] :] = high
        at += width


def place(own, other, core, axis, widths):
    rows, cols = own.shape
    steps = max(n for n in (1, 2, 4) if rows % (8 * n) == 0)
    size = rows // steps
    part = pl.BlockSpec((size, cols), lambda i: (i, 0))
    if axis == 0:
        shapes = [(2, rows, width) for width in widths]
        specs = [pl.BlockSpec((2, size, width), lambda i: (0, i, 0)) for width in widths]
    else:
        shapes = [(rows, 2 * cols)]
        specs = [pl.BlockSpec((size, 2 * cols), lambda i: (i, 0))]
    out = pl.pallas_call(
        functools.partial(place_body, axis=axis, widths=widths),
        grid=(steps,),
        out_shape=[jax.ShapeDtypeStruct(shape, f32) for shape in shapes],
        in_specs=[pl.BlockSpec(memory_space=pltpu.SMEM), part, part],
        out_specs=specs,
        compiler_params=pltpu.CompilerParams(vmem_limit_bytes=48 << 20),
        name="place",
    )(core.reshape(1).astype(jnp.int32), own, other)
    return [o.reshape(2 * rows, -1) if axis == 0 else o for o in out]


def finish(total, core, axis, widths=None):
    widths = (total.shape[1],) if widths is None else widths
    return place(total, swap(total, "rows", 1), core, axis, widths)


def row_products(lefts, rights):
    total = None
    for left, right in zip(lefts, rights):
        part = left_product(left, right)
        total = part if total is None else total + part
    return total


class Along:
    def __init__(self, value, parts=4):
        size = value.shape[0] // parts
        self.own = value
        self.steps = [
            [Held(row_shift(value[i * size : (i + 1) * size], step)) for i in range(parts)]
            for step in range(1, chips_along())
        ]

    def __getitem__(self, i):
        return [step[i] for step in self.steps]

    def all(self):
        return [self.own] + [
            step[0].value if len(step) == 1
            else jnp.concatenate([item.value for item in step], 0)
            for step in self.steps
        ]


def silu_parts(a):
    sig = jax.nn.sigmoid(a)
    return a * sig, sig * (1.0 + a * (1.0 - sig))


def gelu_parts(v):
    k = 0.7978845608028654
    inner = k * (v + 0.044715 * v * v * v)
    th = jnp.tanh(inner)
    slope = 0.5 * (1.0 + th) + 0.5 * v * (1.0 - th * th) * k * (1.0 + 3 * 0.044715 * v * v)
    return 0.5 * v * (1.0 + th), slope


def on_device(
    stream,
    doc_starts,
    valid_mask,
    first_gain,
    w_query,
    w_key,
    w_value,
    w_rate,
    b_rate,
    inner_weight,
    inner_bias,
    inner_gain,
    inner_shift,
    post_gain,
    post_shift,
    w_gate_attn,
    w_out,
    second_gain,
    w_gate,
    w_up,
    w_down,
    cotangent,
):
    _, length, width = stream.shape
    tokens = stream.reshape(length, width)
    slab = second_gain.shape[0]
    column = lax.axis_index("heads") * slab
    core = lax.axis_index("rows") % 2
    heads, hd = inner_bias.shape
    span = heads * hd
    total_span = span * lax.axis_size("heads")
    gains = small_gather(jnp.stack([first_gain, second_gain]))
    gain_one = gains[:, 0].reshape(width)
    gain_two = gains[:, 1].reshape(width)
    grad_output = cotangent.reshape(length, slab)
    dy_held = Held(gather_columns(grad_output))

    w_joined = jnp.concatenate([w_query, w_key, w_value, w_gate_attn], axis=1)
    r1 = lax.rsqrt(jnp.mean(tokens * tokens, -1, keepdims=True) + epsilon)
    unit = tokens * r1
    unit_y = Along(tokens_half(unit, core))
    normed = unit * gain_one
    joined = product(normed, w_joined)
    rate_pre = lax.dot_general(
        w_rate, normed, (((0,), (1,)), ((), ())), precision=lax.Precision.HIGH,
        preferred_element_type=f32,
    )
    joined = meet_one(joined, *unit_y[0])
    gate_pre = joined[:, 3 * span :]
    sig = jax.nn.sigmoid(rate_pre + b_rate[:, None])
    rate_t = sig / hd
    rate = rate_t.T
    seg = jnp.cumsum(doc_starts.reshape(length)).astype(f32)
    seg, seg_t = seg[:, None], seg[None]
    w0, b0 = state_in(inner_weight, inner_bias)
    gain_col, shift_col = inner_gain.reshape(span, 1), inner_shift.reshape(span, 1)
    mixed, *saved = ttt_forward(
        joined, rate, rate_t, seg, seg_t, w0, b0, gain_col, shift_col, hd, heads
    )
    mixed = meet_one(mixed, *unit_y[1])
    row_sums = butterfly(jnp.stack([jnp.sum(mixed, 1), jnp.sum(mixed * mixed, 1)]), "heads")
    row_sums = meet_one(row_sums, *unit_y[2], dy_held)
    row_mean = row_sums[0] / total_span
    inv_std = lax.rsqrt(row_sums[1] / total_span - row_mean * row_mean + epsilon)[:, None]
    centered = (mixed - row_mean[:, None]) * inv_std
    shaped = centered * post_gain + post_shift
    gate_act, gate_slope = gelu_parts(gate_pre)
    gathered = gather_columns(gate_act * shaped, [(), unit_y[3]])
    gathered_y = Along(tokens_half(gathered, core))
    attn = product(gathered, w_out)
    stream_cols = lax.dynamic_slice_in_dim(tokens, column, slab, 1)
    hidden = stream_cols + attn
    whole = gather_columns(hidden, [(), gathered_y[0], gathered_y[1]])
    dy_full = dy_held.value

    r2 = lax.rsqrt(jnp.mean(whole * whole, -1, keepdims=True) + epsilon)
    hnorm = whole * r2 * gain_two
    hnorm_y = Along(tokens_half(hnorm, core))
    a = product(hnorm, w_gate)
    c = product(hnorm, w_up)
    act, slope = silu_parts(a)
    m = act * c
    ffn_part = product(m, w_down)
    deep, across = heads_grid()
    z, x = heads_place()

    def tile_set(dx):
        return jnp.concatenate(
            [
                lax.dynamic_slice_in_dim(
                    ffn_part, (i * across + (x - dx) % across) * slab, slab, 1
                )
                for i in range(deep)
            ],
            1,
        )

    ffn_x = [Held(shift(tile_set(dx), 0, dx)) for dx in range(1, across)]
    dm = meet_one(right_product(dy_full, w_down), *gathered_y[2])
    da = dm * c * slope
    dc = dm * act
    da_y, dc_y = Along(da, 1), Along(dc, 1)
    dhnorm = right_product(da, w_gate) + right_product(dc, w_up)
    dhnorm = meet_one(dhnorm, *gathered_y[3], *ffn_x)
    ffn_sum = tile_set(0)
    for item in ffn_x:
        ffn_sum = ffn_sum + item.value

    def ffn_tile(dz):
        return lax.dynamic_slice_in_dim(ffn_sum, (z - dz) % deep * slab, slab, 1)

    d_gain_two = jnp.sum(dhnorm * whole * r2, 0, keepdims=True)
    weighted = dhnorm * gain_two
    d_whole = r2 * weighted - whole * (r2 * r2 * r2) * jnp.mean(
        whole * weighted, -1, keepdims=True
    )
    pad = jnp.zeros((7, width), f32)
    da_pair, dc_pair = both_cores(da), both_cores(dc)
    own_gate = Held(left_product(da_pair, hnorm_y.own))
    own_up = Held(left_product(dc_pair, hnorm_y.own))
    own_down = Held(left_product(both_cores(m), tokens_half(dy_full, core)))
    ffn_step = Held(shift(ffn_tile(1), 1, 0))
    d_part = scatter_columns(
        d_whole,
        jnp.concatenate([d_gain_two, pad], 0),
        [[ffn_step], [*hnorm_y[0], *hnorm_y[1]], [*hnorm_y[2], own_gate], [own_up]],
    )
    d_hidden = grad_output + d_part[:length]
    d_gain_two = d_part[length]
    d_hidden_y = Along(d_hidden, 1)
    own_out = Held(left_product(gathered_y.own, both_cores(d_hidden)))
    ffn_step = Held(shift(ffn_step.value + ffn_tile(2 % deep), 1, 0) if deep > 2 else ffn_step.value)

    d_gated = scatter_columns(
        right_product(d_hidden, w_out),
        None,
        [[*hnorm_y[3], own_down], [*da_y[0], ffn_step], [*dc_y[0], own_out], [*d_hidden_y[0]]],
    )
    d_gated = meet_one(d_gated, own_down)
    down_y = [Held(item) for item in other_chips(own_down.value)]
    ffn = ffn_step.value
    for dz in range(3, deep):
        ffn = shift(ffn + ffn_tile(dz), 1, 0)
    ffn = Held(ffn + ffn_tile(0))
    d_shaped = d_gated * gate_act
    d_gate_pre = d_gated * shaped * gate_slope
    d_post_gain = jnp.sum(d_shaped * centered, 0)
    d_post_shift = jnp.sum(d_shaped, 0)
    d_center = d_shaped * post_gain
    gain_half = half_of(gain_one, core, 0)
    normed_pairs = [pair * gain_half for pair in unit_y.all()]
    d_gate_y = Along(d_gate_pre, 1)
    own_attn = Held(left_product(normed_pairs[0], both_cores(d_gate_pre)))
    back_sums = butterfly(
        jnp.stack([jnp.sum(d_center, 1), jnp.sum(d_center * centered, 1)]), "heads"
    )
    d_mixed = inv_std * (
        d_center - back_sums[0][:, None] / total_span
        - centered * back_sums[1][:, None] / total_span
    )
    dq, dk, dv, d_rate, dw, db, dg, dsh = ttt_backward(
        joined, rate_t, seg, seg_t, w0, b0, gain_col, shift_col, saved, d_mixed, hd, heads
    )
    dq = meet_one(dq, *down_y, *d_gate_y[0], own_attn, ffn)
    output = hidden + ffn.value
    ffn = ffn.value
    d_inner_weight, d_inner_bias = state_back(dw, db, heads, hd)
    d_rate_pre = d_rate * rate_t * (1.0 - sig)
    d_three = jnp.concatenate([dq, dk, dv], 1)
    d_three_y, d_rate_y = Along(d_three, 1), Along(d_rate_pre, 1)
    d_joined = jnp.concatenate([d_three, d_gate_pre], 1)
    d_normed = right_product(d_joined, w_joined) + lax.dot_general(
        d_rate_pre, w_rate, (((0,), (1,)), ((), ())), precision=lax.Precision.HIGH,
        preferred_element_type=f32,
    )
    d_gain_one = jnp.sum(d_normed * tokens * r1, 0, keepdims=True)
    weighted = d_normed * gain_one
    d_tokens = r1 * weighted - tokens * (r1 * r1 * r1) * jnp.mean(
        tokens * weighted, -1, keepdims=True
    )

    def cores(values):
        return [both_cores(value) for value in values]

    def total(own, lefts, rights):
        for left, right in zip(lefts[1:], rights[1:]):
            own = own + left_product(left, right)
        return Held(own)

    own_three = Held(left_product(normed_pairs[0], both_cores(d_three)))
    all_attn = total(own_attn.value, normed_pairs, cores(d_gate_y.all()))
    all_gate = total(own_gate.value, cores(da_y.all()), hnorm_y.all())
    all_up = total(own_up.value, cores(dc_y.all()), hnorm_y.all())
    all_out = total(own_out.value, gathered_y.all(), cores(d_hidden_y.all()))
    weights = valid_mask.reshape(-1).astype(f32)[:, None]
    stats = jnp.stack(
        [
            jnp.sum(weights * member * member)
            for member in (stream_cols, attn, hidden, ffn, output)
        ]
        + [jnp.sum(weights) / lax.axis_size("heads")]
    )
    late = []

    def last_hook():
        late.append(total(own_three.value, normed_pairs, cores(d_three_y.all())))
        return [late[0], *d_rate_y[0]]

    across_slabs = jnp.tile(jnp.pad(stats, (0, slab - stats.size)), width // slab)[None]
    d_part = scatter_columns(
        d_tokens,
        jnp.concatenate([d_gain_one, across_slabs, pad[1:]], 0),
        [[own_three], [all_gate, all_attn], [all_up, all_out, *d_three_y[0]], last_hook],
    )
    d_stream = d_hidden + d_part[:length]
    d_gain_one = d_part[length]
    stats = d_part[length + 1, : stats.size]

    (g_gate,) = finish(all_gate.value, core, 1)
    (g_up,) = finish(all_up.value, core, 1)
    (g_out,) = finish(all_out.value, core, 0)
    (g_down,) = finish(sum((item.value for item in down_y), own_down.value), core, 1)
    (g_gate_attn,) = finish(all_attn.value, core, 0)
    g_query, g_key, g_value = finish(late[0].value, core, 0, (span,) * 3)
    g_rate = None
    for pair, d in zip(normed_pairs, d_rate_y.all()):
        part = product(jnp.concatenate([d, swap(d, "rows", 1)], 1), pair)
        g_rate = part if g_rate is None else g_rate + part
    ends = (g_rate, swap(g_rate, "rows", 1))
    g_rate = jnp.where(core == 0, jnp.concatenate(ends, 1), jnp.concatenate(ends[::-1], 1))

    small = [
        d_gain_one, jnp.sum(d_rate_pre, 1), d_inner_weight, d_inner_bias, dg, dsh,
        d_post_gain, d_post_shift, d_gain_two, stats,
    ]
    packed = butterfly(jnp.concatenate([item.reshape(-1) for item in small]), "rows")
    parts = []
    at = 0
    for item in small:
        parts.append(packed[at : at + item.size])
        at += item.size
    stats = parts[9]
    rms_values = jnp.sqrt(stats[:5] / (stats[5] * width))
    return (
        output.reshape(1, length, slab),
        d_stream.reshape(1, length, slab),
        parts[0],
        g_query,
        g_key,
        g_value,
        g_rate.T,
        parts[1],
        parts[2].reshape(heads, hd, hd),
        parts[3].reshape(heads, hd),
        parts[4].reshape(heads, hd),
        parts[5].reshape(heads, hd),
        parts[6],
        parts[7],
        g_gate_attn,
        g_out,
        parts[8],
        g_gate.T,
        g_up.T,
        g_down,
        rms_values,
    )


def solution(mesh):
    in_specs = (
        P("rows", None, None),
        P("rows", None),
        P("rows", None),
        P("heads"),
        P(None, "heads"),
        P(None, "heads"),
        P(None, "heads"),
        P(None, "heads"),
        P("heads"),
        P("heads", None, None),
        P("heads", None),
        P("heads", None),
        P("heads", None),
        P("heads"),
        P("heads"),
        P(None, "heads"),
        P(None, "heads"),
        P("heads"),
        P(None, "heads"),
        P(None, "heads"),
        P("heads", None),
        P("rows", None, "heads"),
    )
    out_specs = (
        P("rows", None, "heads"),
        P("rows", None, "heads"),
        P("heads"),
        P(None, "heads"),
        P(None, "heads"),
        P(None, "heads"),
        P(None, "heads"),
        P("heads"),
        P("heads", None, None),
        P("heads", None),
        P("heads", None),
        P("heads", None),
        P("heads"),
        P("heads"),
        P(None, "heads"),
        P(None, "heads"),
        P("heads"),
        P(None, "heads"),
        P(None, "heads"),
        P("heads", None),
        P(),
    )
    return jax.shard_map(
        on_device, mesh=mesh, in_specs=in_specs, out_specs=out_specs, check_vma=False
    )
```

```python
import functools
import jax, jax.numpy as jnp
from jax import lax
from jax.experimental import pallas as pl
from jax.experimental.pallas import tpu as pltpu

from jax.sharding import PartitionSpec as P

MB = 16
CH = 128
epsilon = 1e-06
f32 = jnp.float32
bf16 = jnp.bfloat16
NN = ((1,), (0,))


def split(x):
    hi = x.astype(bf16)
    return hi, (x - hi.astype(f32)).astype(bf16)


def mm(a, b, dims=NN):
    def one(p, q):
        return lax.dot_general(p, q, (dims, ((), ())), preferred_element_type=f32)

    return one(a[0], b[0]) + (one(a[0], b[1]) + one(a[1], b[0]))


def wide(x):
    hi, lo = split(x)
    return jnp.concatenate([hi, lo], axis=1)


def tall_dot(x, pair):
    rows = x.shape[0]
    cols = pair.shape[1] // 2
    hi, lo = split(x)
    out = lax.dot_general(
        jnp.concatenate([hi, lo], axis=0), pair, (NN, ((), ())), preferred_element_type=f32
    )
    top, low = out[:rows], out[rows:]
    return top[:, :cols] + (top[:, cols:] + low[:, :cols])


def iota(shape, dim):
    return lax.broadcasted_iota(jnp.int32, shape, dim)


def head_sum(x, hd):
    rows, cols = x.shape
    parts = [
        jnp.broadcast_to(jnp.sum(x[i : i + hd], axis=0, keepdims=True), (hd, cols))
        for i in range(0, rows, hd)
    ]
    return parts[0] if len(parts) == 1 else jnp.concatenate(parts, axis=0)


def lane_sum(x):
    return jnp.sum(x, axis=1, keepdims=True)


def coefficients(transposed):
    source = iota((CH, CH), 1 if transposed else 0)
    target = iota((CH, CH), 0 if transposed else 1)
    before = (source // MB < target // MB).astype(f32) * (1.0 / MB)
    inside = ((source // MB == target // MB) & (source <= target)).astype(f32)
    return before, before + inside / ((target % MB) + 1).astype(f32)


def forward_body(
    joined, rate, rate_t, seg, seg_t, w0, b0, gain, shift, mixed, z_out, zb_out, w_out, b_out,
    w_s, b_s, z_s, tau_s, a_s, m_s, *, hd, heads,
):
    pairs = heads * hd // CH
    per = CH // hd
    span = heads * hd
    chunks = joined.shape[0] // CH
    n_inv = 1.0 / hd
    row_head = iota((CH, CH), 0) // hd
    lane_head = iota((CH, CH), 1) // hd
    lane_block = iota((hd, CH), 1) // MB
    block_diag = row_head == lane_head
    w_s[...] = jnp.zeros_like(w_s)
    b_s[...] = jnp.zeros_like(b_s)

    def chunk(c, carry):
        ts = pl.multiple_of(c * CH, CH)
        here = pl.ds(ts, CH)
        seg_row = seg_t[:, here]
        seg_col = seg[here, :]
        last_seg = seg_row[:, CH - 1 : CH]
        prev = jnp.max(jnp.where(iota(seg_t.shape, 1) < ts, seg_t[...], 0.0), keepdims=True)
        carried = seg_row == prev
        in_last = (seg_row == last_seg).astype(f32)
        whole = last_seg == prev
        same = seg_col == seg_row
        before, within = coefficients(False)
        before = jnp.where(same, before, 0.0)
        within = jnp.where(same, within, 0.0)
        for p in range(pairs):
            rows = slice(p * CH, (p + 1) * CH)
            kn = joined[here, span + p * CH : span + (p + 1) * CH]
            qn = joined[here, p * CH : (p + 1) * CH]
            vn = joined[here, 2 * span + p * CH : 2 * span + (p + 1) * CH]
            k_t, q_t, v_t = kn.T, qn.T, vn.T
            ks, kts, qts = split(kn), split(k_t), split(q_t)
            ws, w0s = split(w_s[rows]), split(w0[rows])
            bias = jnp.where(carried, b_s[rows], b0[rows])
            z_s[rows] = jnp.where(carried, mm(ws, kts), mm(w0s, kts)) + bias
            zb_out[rows, here] = jnp.where(carried, mm(ws, qts), mm(w0s, qts)) + bias
            w_out[c, rows] = w_s[rows]
            b_out[c, rows] = b_s[rows]
            tau_s[rows] = gain[rows] * (shift[rows] - v_t + k_t)
            for hh in range(per):
                h = p * per + hh
                own = (row_head == hh).astype(bf16)
                r_col = rate[here, h : h + 1]
                score = mm(ks, (kts[0] * own, kts[1] * own))
                a_s[h] = wide((score + 1.0) * (before * r_col))
                score = mm(ks, (qts[0] * own, qts[1] * own))
                m_s[h] = wide((score + 1.0) * (within * r_col))

        gsq = [jnp.broadcast_to(gain[h * hd : (h + 1) * hd] ** 2, (hd, CH)) for h in range(heads)]
        tsum = [
            jnp.sum(tau_s[h * hd : (h + 1) * hd], axis=0, keepdims=True) * n_inv
            for h in range(heads)
        ]

        def inner(h, z):
            tau = tau_s[h * hd : (h + 1) * hd]
            zg = z * gsq[h]
            m2 = jnp.sum(z * z, axis=0, keepdims=True) * n_inv
            a1 = jnp.sum(zg, axis=0, keepdims=True) * n_inv
            a2 = jnp.sum(z * zg, axis=0, keepdims=True) * n_inv
            a3 = jnp.sum(z * tau, axis=0, keepdims=True) * n_inv
            s = lax.rsqrt(m2 + epsilon)
            c_eu = s * (s * a2 + a3)
            e_mean = s * a1 + tsum[h]
            return (s * s) * (zg - c_eu * z) + s * (tau - e_mean)

        def step(t, zs):
            now = lane_block == t
            new = []
            for h in range(heads):
                g = jnp.where(now, inner(h, zs[h]), 0.0)
                new.append(zs[h] - tall_dot(g, a_s[h]))
            return tuple(new)

        zs = tuple(z_s[h * hd : (h + 1) * hd] for h in range(heads))
        zs = lax.fori_loop(0, CH // MB - 1, step, zs)
        for p in range(pairs):
            rows = slice(p * CH, (p + 1) * CH)
            gs = []
            outs = []
            for hh in range(per):
                h = p * per + hh
                hr = slice(h * hd, (h + 1) * hd)
                z_out[hr, here] = zs[h]
                g = inner(h, zs[h])
                zb = zb_out[hr, here] - tall_dot(g, m_s[h])
                zb_out[hr, here] = zb
                sb = lax.rsqrt(jnp.sum(zb * zb, axis=0, keepdims=True) * n_inv + epsilon)
                outs.append(zb * sb * gain[hr] + shift[hr])
                gs.append(g * (rate_t[h : h + 1, here] * in_last * (1.0 / MB)))
            gw = jnp.concatenate(gs, axis=0)
            lanes = slice(p * CH, (p + 1) * CH)
            mixed[here, lanes] = joined[here, lanes] + jnp.concatenate(outs, axis=0).T
            kn = joined[here, span + p * CH : span + (p + 1) * CH]
            upd = mm(split(gw), split(kn))
            w_s[rows] = jnp.where(whole, w_s[rows], w0[rows]) - jnp.where(block_diag, upd, 0.0)
            b_s[rows] = jnp.where(whole, b_s[rows], b0[rows]) - lane_sum(gw)
        return carry

    lax.fori_loop(0, chunks, chunk, 0)


def ttt_forward(joined, rate, rate_t, seg, seg_t, w0, b0, gain, shift, hd, heads):
    length = joined.shape[0]
    span = heads * hd
    chunks = length // CH
    shape = jax.ShapeDtypeStruct
    return pl.pallas_call(
        functools.partial(forward_body, hd=hd, heads=heads),
        out_shape=(
            shape((length, span), f32),
            shape((span, length), f32),
            shape((span, length), f32),
            shape((chunks, span, CH), f32),
            shape((chunks, span, 1), f32),
        ),
        scratch_shapes=[
            pltpu.VMEM((span, CH), f32),
            pltpu.VMEM((span, 1), f32),
            pltpu.VMEM((span, CH), f32),
            pltpu.VMEM((span, CH), f32),
            pltpu.VMEM((heads, CH, 2 * CH), bf16),
            pltpu.VMEM((heads, CH, 2 * CH), bf16),
        ],
        compiler_params=pltpu.CompilerParams(vmem_limit_bytes=48 << 20),
        name="inner_forward",
    )(joined, rate, rate_t, seg, seg_t, w0, b0, gain, shift)


def backward_body(
    joined, rate_t, seg, seg_t, w0, b0, gain, shift, z_in, zb_in, w_in, b_in, dy,
    dq_out, dk_out, dv_out, dr_out, dw_out, db_out, dg_out, dsh_out,
    dw_s, db_s, p_s, u_s, f_s, bb_s, e2_s, u2_s, gt_s, dzb_s, at_s, sc_s,
    *, hd, heads,
):
    pairs = heads * hd // CH
    per = CH // hd
    span = heads * hd
    chunks = joined.shape[0] // CH
    n_inv = 1.0 / hd
    row_head = iota((CH, CH), 0) // hd
    lane_head = iota((CH, CH), 1) // hd
    lane_block = iota((hd, CH), 1) // MB
    block_diag = row_head == lane_head
    for ref in (dw_s, db_s, dw_out, db_out, dg_out, dsh_out):
        ref[...] = jnp.zeros_like(ref)

    def mean(x):
        return head_sum(x, hd) * n_inv

    def chunk(index, carry):
        c = chunks - 1 - index
        ts = pl.multiple_of(c * CH, CH)
        here = pl.ds(ts, CH)
        seg_row = seg_t[:, here]
        seg_col = seg[here, :]
        last_seg = seg_row[:, CH - 1 : CH]
        prev = jnp.max(jnp.where(iota(seg_t.shape, 1) < ts, seg_t[...], 0.0), keepdims=True)
        carried = seg_row == prev
        carried_col = seg_col == prev
        in_last = (seg_row == last_seg).astype(f32)
        whole = last_seg == prev
        same = seg_col == seg_row
        before, within = coefficients(True)
        before = jnp.where(same, before, 0.0)
        within = jnp.where(same, within, 0.0)
        consts = {}
        for p in range(pairs):
            rows = slice(p * CH, (p + 1) * CH)
            lanes = slice(p * CH, (p + 1) * CH)
            qn = joined[here, p * CH : (p + 1) * CH]
            kn = joined[here, span + p * CH : span + (p + 1) * CH]
            vn = joined[here, 2 * span + p * CH : 2 * span + (p + 1) * CH]
            k_t, v_t, dy_t = kn.T, vn.T, dy[here, lanes].T
            qs, ks, kts = split(qn), split(kn), split(k_t)
            g_col = gain[rows]
            gsq = g_col * g_col
            zb = zb_in[rows, here]
            sb = lax.rsqrt(mean(zb * zb) + epsilon)
            ub = zb * sb
            dg_out[rows] += lane_sum(dy_t * ub)
            dsh_out[rows] += lane_sum(dy_t)
            pb = dy_t * g_col
            dzb = sb * (pb - mean(pb) - ub * mean(pb * ub))
            dzb_s[rows] = dzb
            z = z_in[rows, here]
            s = lax.rsqrt(mean(z * z) + epsilon)
            u = z * s
            gu = gsq * u
            e = gu + g_col * (shift[rows] - v_t + k_t)
            c_eu = mean(e * u)
            g_t = s * (e - mean(e) - u * c_eu)
            gt_s[rows] = g_t
            u_s[rows] = u
            f_s[rows] = g_t + s * gu
            bb_s[rows] = (s * s) * (gsq - c_eu)
            e2_s[rows] = (s * s) * (e + gu)
            u2_s[rows] = s * u
            h1 = s * mean(gu)
            h2 = 2.0 * s * c_eu + s * mean(gu * u)
            dzbs = split(dzb)
            gts = split(g_t)
            dzbn = split(dzb.T)
            from_state = mm(split(dw_s[rows]), kts) + db_s[rows]
            pieces = []
            dq = dy[here, lanes]
            dk = jnp.zeros((CH, CH), f32)
            for hh in range(per):
                h = p * per + hh
                hr = slice(hh * hd, (hh + 1) * hd)
                r_row = rate_t[h : h + 1, here]
                consts[h] = (h1[hh * hd : hh * hd + 1], h2[hh * hd : hh * hd + 1])
                own = (row_head == hh).astype(bf16)
                own_lane = (lane_head == hh).astype(bf16)
                kt_h = (kts[0] * own, kts[1] * own)
                sc = (mm(ks, kt_h) + 1.0) * before
                sc_s[h] = sc
                at_s[h] = wide(sc * r_row)
                scq = (mm(qs, kt_h) + 1.0) * within
                pt = mm(dzbn, (gts[0] * own, gts[1] * own))
                dr_out[h : h + 1, here] = -jnp.sum(pt * scq, axis=0, keepdims=True) - (
                    (1.0 / MB) * in_last
                ) * jnp.sum(g_t[hr] * from_state[hr], axis=0, keepdims=True)
                pm = pt * (within * r_row)
                pms = split(pm)
                pmts = split(pm.T)
                kn_h = (ks[0] * own_lane, ks[1] * own_lane)
                qn_h = (qs[0] * own_lane, qs[1] * own_lane)
                dq = dq - mm(pms, kn_h)
                dk = dk - mm(pmts, qn_h)
                pieces.append(
                    -mm((dzbs[0][hr], dzbs[1][hr]), split(scq * r_row))
                    - from_state[hr] * (r_row * in_last * (1.0 / MB))
                )
            p_s[rows] = jnp.concatenate(pieces, axis=0)
            w0s = split(w0[rows])
            wd = split(w_in[c, rows] - w0[rows])
            zero = jnp.zeros((), bf16)
            dzbn_c = (jnp.where(carried_col, dzbn[0], zero), jnp.where(carried_col, dzbn[1], zero))
            dq_out[here, lanes] = dq + mm(dzbn, w0s) + mm(dzbn_c, wd)
            dk_out[here, lanes] = dk

        def upstream(h, pv):
            hr = slice(h * hd, (h + 1) * hd)
            h1, h2 = consts[h]
            pm = jnp.sum(pv, axis=0, keepdims=True) * n_inv
            q = jnp.sum(pv * u_s[hr], axis=0, keepdims=True) * n_inv
            kf = jnp.sum(pv * f_s[hr], axis=0, keepdims=True) * n_inv
            kappa = kf - h1 * pm - h2 * q
            dz = (pv - pm) * bb_s[hr] - q * e2_s[hr] - kappa * u2_s[hr]
            return dz, pm, q

        def step(index, ps):
            now = lane_block == (CH // MB - 1 - index)
            new = []
            for h in range(heads):
                dz = jnp.where(now, upstream(h, ps[h])[0], 0.0)
                new.append(ps[h] - tall_dot(dz, at_s[h]))
            return tuple(new)

        ps = tuple(p_s[h * hd : (h + 1) * hd] for h in range(heads))
        ps = lax.fori_loop(0, CH // MB - 1, step, ps)

        for p in range(pairs):
            rows = slice(p * CH, (p + 1) * CH)
            lanes = slice(p * CH, (p + 1) * CH)
            qn = joined[here, p * CH : (p + 1) * CH]
            kn = joined[here, span + p * CH : span + (p + 1) * CH]
            vn = joined[here, 2 * span + p * CH : 2 * span + (p + 1) * CH]
            qs, ks = split(qn), split(kn)
            g_t = gt_s[rows]
            gts = split(g_t)
            dzs, des = [], []
            for hh in range(per):
                h = p * per + hh
                hr = slice(h * hd, (h + 1) * hd)
                dz, pm, q = upstream(h, ps[h])
                dzs.append(dz - jnp.sum(dz, axis=0, keepdims=True) * n_inv)
                z = z_in[hr, here]
                s = lax.rsqrt(jnp.sum(z * z, axis=0, keepdims=True) * n_inv + epsilon)
                des.append(s * (ps[h] - pm - u_s[hr] * q))
            dz = jnp.concatenate(dzs, axis=0)
            de = jnp.concatenate(des, axis=0)
            g_col = gain[rows]
            gde = g_col * de
            t_t = shift[rows] + (kn - vn).T
            dg_out[rows] += lane_sum((2.0 * g_col * u_s[rows] + t_t) * de)
            dsh_out[rows] += lane_sum(gde)
            gden = gde.T
            dv_out[here, lanes] = -gden
            dzn = split(dz.T)
            dk = dk_out[here, lanes] + gden
            r_rows = []
            for hh in range(per):
                h = p * per + hh
                r_row = rate_t[h : h + 1, here]
                own = (row_head == hh).astype(bf16)
                own_lane = (lane_head == hh).astype(bf16)
                rt = mm(dzn, (gts[0] * own, gts[1] * own))
                dr_out[h : h + 1, here] -= jnp.sum(rt * sc_s[h], axis=0, keepdims=True)
                ra = rt * (before * r_row)
                dk = dk - mm(split(ra + ra.T), (ks[0] * own_lane, ks[1] * own_lane))
                r_rows.append(jnp.broadcast_to(r_row * in_last * (1.0 / MB), (hd, CH)))
            gw = g_t * jnp.concatenate(r_rows, axis=0)
            w0s = split(w0[rows])
            wd = split(w_in[c, rows] - w0[rows])
            zero = jnp.zeros((), bf16)
            dzn_c = (jnp.where(carried_col, dzn[0], zero), jnp.where(carried_col, dzn[1], zero))
            dk = dk + mm(dzn, w0s) + mm(dzn_c, wd) - mm(split(gw.T), split(dw_s[rows]))
            dk_out[here, lanes] = dk
            dzb = dzb_s[rows]
            dzc = jnp.where(carried, dz, 0.0)
            dzbc = jnp.where(carried, dzb, 0.0)
            diag = jnp.where(block_diag, mm(split(dzc), ks) + mm(split(dzbc), qs), 0.0)
            rest = jnp.where(
                block_diag, mm(split(dz - dzc), ks) + mm(split(dzb - dzbc), qs), 0.0
            )
            dw = dw_s[rows]
            db = db_s[rows]
            dw_out[rows] += jnp.where(whole, 0.0, dw) + rest
            db_out[rows] += jnp.where(whole, 0.0, db) + lane_sum(dz - dzc + dzb - dzbc)
            dw_s[rows] = jnp.where(whole, dw, 0.0) + diag
            db_s[rows] = jnp.where(whole, db, 0.0) + lane_sum(dzc + dzbc)
        return carry

    lax.fori_loop(0, chunks, chunk, 0)


def ttt_backward(joined, rate_t, seg, seg_t, w0, b0, gain, shift, saved, dy, hd, heads):
    length = joined.shape[0]
    span = heads * hd
    shape = jax.ShapeDtypeStruct
    return pl.pallas_call(
        functools.partial(backward_body, hd=hd, heads=heads),
        out_shape=(
            shape((length, span), f32),
            shape((length, span), f32),
            shape((length, span), f32),
            shape((heads, length), f32),
            shape((span, CH), f32),
            shape((span, 1), f32),
            shape((span, 1), f32),
            shape((span, 1), f32),
        ),
        scratch_shapes=[
            pltpu.VMEM((span, CH), f32),
            pltpu.VMEM((span, 1), f32),
        ]
        + [pltpu.VMEM((span, CH), f32)] * 8
        + [
            pltpu.VMEM((heads, CH, 2 * CH), bf16),
            pltpu.VMEM((heads, CH, CH), f32),
        ],
        compiler_params=pltpu.CompilerParams(vmem_limit_bytes=48 << 20),
        name="inner_backward",
    )(joined, rate_t, seg, seg_t, w0, b0, gain, shift, *saved, dy)


def state_in(inner_weight, inner_bias):
    heads, hd, _ = inner_weight.shape
    per = CH // hd
    w_t = jnp.swapaxes(inner_weight, 1, 2)
    w_t = w_t - jnp.mean(w_t, axis=1, keepdims=True)
    placed = [
        jnp.pad(w_t[h], ((0, 0), ((h % per) * hd, CH - hd - (h % per) * hd)))
        for h in range(heads)
    ]
    b = inner_bias - jnp.mean(inner_bias, axis=1, keepdims=True)
    return jnp.concatenate(placed, axis=0), b.reshape(heads * hd, 1)


def state_back(dw, db, heads, hd):
    per = CH // hd
    parts = [
        dw[h * hd : (h + 1) * hd, (h % per) * hd : (h % per + 1) * hd] for h in range(heads)
    ]
    d = jnp.stack(parts)
    d = jnp.swapaxes(d - jnp.mean(d, axis=1, keepdims=True), 1, 2)
    b = db.reshape(heads, hd)
    return d, b - jnp.mean(b, axis=1, keepdims=True)


def product(left, right):
    return jnp.dot(left, right, precision=lax.Precision.HIGH, preferred_element_type=f32)


def left_product(left, right):
    return lax.dot_general(
        left, right, (((0,), (0,)), ((), ())), precision=lax.Precision.HIGH,
        preferred_element_type=f32,
    )


def right_product(left, right):
    return lax.dot_general(
        left, right, (((1,), (1,)), ((), ())), precision=lax.Precision.HIGH,
        preferred_element_type=f32,
    )


def heads_grid():
    size = lax.axis_size("heads")
    deep = 4 if size % 4 == 0 else 1
    return deep, size // deep


def heads_place():
    _, across = heads_grid()
    index = lax.axis_index("heads")
    return index // across, index % across


def shift(value, dz, dx):
    deep, across = heads_grid()
    pairs = [
        (h, (h // across + dz) % deep * across + (h % across + dx) % across)
        for h in range(deep * across)
    ]
    return lax.ppermute(value, "heads", pairs)


def swap(value, axis, bit):
    return lax.ppermute(value, axis, [(i, i ^ bit) for i in range(lax.axis_size(axis))])


def row_shift(value, step):
    size = lax.axis_size("rows")
    return lax.ppermute(value, "rows", [(r, (r + 2 * step) % size) for r in range(size)])


def butterfly(value, axis):
    bit = 1
    while bit < lax.axis_size(axis):
        value = value + swap(value, axis, bit)
        bit *= 2
    return value


def small_gather(value):
    size = lax.axis_size("heads")
    place = jnp.arange(size) == lax.axis_index("heads")
    place = place.reshape((size,) + (1,) * value.ndim)
    return butterfly(jnp.where(place, value[None], 0.0), "heads")


class Held:
    def __init__(self, value):
        self.value = value


def meet(values, held=()):
    out = lax.optimization_barrier(tuple(values) + tuple(item.value for item in held))
    for item, value in zip(held, out[len(values) :]):
        item.value = value
    return list(out[: len(values)])


def meet_one(value, *held):
    return meet([value], held)[0]


def turn(hooks, index):
    hook = hooks[index] if index < len(hooks) else ()
    return hook() if callable(hook) else hook


def gather_columns(value, hooks=()):
    deep, across = heads_grid()
    z, x = heads_place()
    rows, cols = value.shape
    out = jnp.zeros((rows, cols * deep * across), value.dtype)
    here, ready = value, [(0, 0, value)]
    for dz in range(deep):
        moved = [shift(here, 0, dx) for dx in range(1, across)]
        if dz + 1 < deep:
            moved.append(shift(here, 1, 0))
        for oz, ox, item in ready:
            column = ((z - oz) % deep * across + (x - ox) % across) * cols
            out = lax.dynamic_update_slice(out, item, (0, column))
        *moved, out = meet(moved + [out], turn(hooks, dz))
        ready = [(dz, dx, moved[dx - 1]) for dx in range(1, across)]
        if dz + 1 < deep:
            here = moved[-1]
            ready.append((dz + 1, 0, here))
    for oz, ox, item in ready:
        column = ((z - oz) % deep * across + (x - ox) % across) * cols
        out = lax.dynamic_update_slice(out, item, (0, column))
    return out


def scatter_columns(value, extra=None, hooks=()):
    deep, across = heads_grid()
    z, x = heads_place()
    rows, width = value.shape
    cols = width // (deep * across)

    def piece(dz, dx):
        column = ((z - dz) % deep * across + (x - dx) % across) * cols
        block = lax.dynamic_slice(value, (0, column), (rows, cols))
        if extra is not None:
            tail = lax.dynamic_slice(extra, (0, column), (extra.shape[0], cols))
            block = jnp.concatenate([block, tail], 0)
        return block

    total = None
    for index, dz in enumerate(list(range(1, deep)) + [0]):
        moved = [shift(piece(dz, dx), 0, dx) for dx in range(1, across)]
        if total is not None:
            moved.append(shift(total, 1, 0))
        total = piece(dz, 0)
        for item in meet(moved, turn(hooks, index)):
            total = total + item
    return total


def half_of(value, index, axis):
    size = value.shape[axis] // 2
    return lax.dynamic_slice_in_dim(value, index * size, size, axis)


def both_cores(value):
    return jnp.concatenate([value, swap(value, "rows", 1)], 0)


def tokens_half(value, core):
    return jnp.concatenate(
        [half_of(value, core, 1), swap(half_of(value, 1 - core, 1), "rows", 1)], 0
    )


def chips_along():
    return lax.axis_size("rows") // 2


def other_chips(value):
    return [row_shift(value, step) for step in range(1, chips_along())]


def place_body(core, own, other, *outs, axis, widths):
    first = core[0] == 0
    at = 0
    for out, width in zip(outs, widths):
        mine, its = (own[:, at : at + width], other[:, at : at + width]) if axis == 0 else (own[...], other[...])
        low = jnp.where(first, mine, its)
        high = jnp.where(first, its, mine)
        if axis == 0:
            out[0] = low
            out[1] = high
        else:
            out[:, : low.shape[1]] = low
            out[:, low.shape[1] :] = high
        at += width


def place(own, other, core, axis, widths):
    rows, cols = own.shape
    steps = max(n for n in (1, 2, 4) if rows % (8 * n) == 0)
    size = rows // steps
    part = pl.BlockSpec((size, cols), lambda i: (i, 0))
    if axis == 0:
        shapes = [(2, rows, width) for width in widths]
        specs = [pl.BlockSpec((2, size, width), lambda i: (0, i, 0)) for width in widths]
    else:
        shapes = [(rows, 2 * cols)]
        specs = [pl.BlockSpec((size, 2 * cols), lambda i: (i, 0))]
    out = pl.pallas_call(
        functools.partial(place_body, axis=axis, widths=widths),
        grid=(steps,),
        out_shape=[jax.ShapeDtypeStruct(shape, f32) for shape in shapes],
        in_specs=[pl.BlockSpec(memory_space=pltpu.SMEM), part, part],
        out_specs=specs,
        compiler_params=pltpu.CompilerParams(vmem_limit_bytes=48 << 20),
        name="place",
    )(core.reshape(1).astype(jnp.int32), own, other)
    return [o.reshape(2 * rows, -1) if axis == 0 else o for o in out]


def finish(total, core, axis, widths=None):
    widths = (total.shape[1],) if widths is None else widths
    return place(total, swap(total, "rows", 1), core, axis, widths)


def row_products(lefts, rights):
    total = None
    for left, right in zip(lefts, rights):
        part = left_product(left, right)
        total = part if total is None else total + part
    return total


class Along:
    def __init__(self, value, parts=4, axis=0):
        self.own = value
        self.axis = axis
        pieces = jnp.split(value, parts, axis)
        self.steps = [
            [Held(row_shift(piece, step)) for piece in pieces] for step in range(1, chips_along())
        ]

    def __getitem__(self, i):
        return [step[i] for step in self.steps]

    def all(self):
        return [self.own] + [
            step[0].value if len(step) == 1
            else jnp.concatenate([item.value for item in step], self.axis)
            for step in self.steps
        ]


def silu_parts(a):
    sig = jax.nn.sigmoid(a)
    return a * sig, sig * (1.0 + a * (1.0 - sig))


def gelu_parts(v):
    k = 0.7978845608028654
    inner = k * (v + 0.044715 * v * v * v)
    th = jnp.tanh(inner)
    slope = 0.5 * (1.0 + th) + 0.5 * v * (1.0 - th * th) * k * (1.0 + 3 * 0.044715 * v * v)
    return 0.5 * v * (1.0 + th), slope


def on_device(
    stream,
    doc_starts,
    valid_mask,
    first_gain,
    w_query,
    w_key,
    w_value,
    w_rate,
    b_rate,
    inner_weight,
    inner_bias,
    inner_gain,
    inner_shift,
    post_gain,
    post_shift,
    w_gate_attn,
    w_out,
    second_gain,
    w_gate,
    w_up,
    w_down,
    cotangent,
):
    _, length, width = stream.shape
    tokens = stream.reshape(length, width)
    slab = second_gain.shape[0]
    column = lax.axis_index("heads") * slab
    core = lax.axis_index("rows") % 2
    heads, hd = inner_bias.shape
    span = heads * hd
    total_span = span * lax.axis_size("heads")
    gains = small_gather(jnp.stack([first_gain, second_gain]))
    gain_one = gains[:, 0].reshape(width)
    gain_two = gains[:, 1].reshape(width)
    grad_output = cotangent.reshape(length, slab)
    dy_held = Held(gather_columns(grad_output))

    w_joined = jnp.concatenate([w_query, w_key, w_value, w_gate_attn], axis=1)
    r1 = lax.rsqrt(jnp.mean(tokens * tokens, -1, keepdims=True) + epsilon)
    unit = tokens * r1
    unit_y = Along(tokens_half(unit, core))
    normed = unit * gain_one
    joined = product(normed, w_joined)
    rate_pre = lax.dot_general(
        w_rate, normed, (((0,), (1,)), ((), ())), precision=lax.Precision.HIGH,
        preferred_element_type=f32,
    )
    joined = meet_one(joined, *unit_y[0])
    gate_pre = joined[:, 3 * span :]
    sig = jax.nn.sigmoid(rate_pre + b_rate[:, None])
    rate_t = sig / hd
    rate = rate_t.T
    seg = jnp.cumsum(doc_starts.reshape(length)).astype(f32)
    seg, seg_t = seg[:, None], seg[None]
    w0, b0 = state_in(inner_weight, inner_bias)
    gain_col, shift_col = inner_gain.reshape(span, 1), inner_shift.reshape(span, 1)
    mixed, *saved = ttt_forward(
        joined, rate, rate_t, seg, seg_t, w0, b0, gain_col, shift_col, hd, heads
    )
    mixed = meet_one(mixed, *unit_y[1])
    row_sums = butterfly(jnp.stack([jnp.sum(mixed, 1), jnp.sum(mixed * mixed, 1)]), "heads")
    row_sums = meet_one(row_sums, *unit_y[2], dy_held)
    row_mean = row_sums[0] / total_span
    inv_std = lax.rsqrt(row_sums[1] / total_span - row_mean * row_mean + epsilon)[:, None]
    centered = (mixed - row_mean[:, None]) * inv_std
    shaped = centered * post_gain + post_shift
    gate_act, gate_slope = gelu_parts(gate_pre)
    gathered = gather_columns(gate_act * shaped, [(), unit_y[3]])
    gathered_pair = tokens_half(gathered, core)
    attn = product(gathered, w_out)
    stream_cols = lax.dynamic_slice_in_dim(tokens, column, slab, 1)
    hidden = stream_cols + attn
    whole = gather_columns(hidden)
    dy_full = dy_held.value

    r2 = lax.rsqrt(jnp.mean(whole * whole, -1, keepdims=True) + epsilon)
    hnorm = whole * r2 * gain_two
    hnorm_y = Along(tokens_half(hnorm, core), 8)
    a = product(hnorm, w_gate)
    c = product(hnorm, w_up)
    act, slope = silu_parts(a)
    m = act * c
    ffn_part = product(m, w_down)
    deep, across = heads_grid()
    z, x = heads_place()

    def ffn_piece(dz, dx):
        place_of = (z - dz) % deep * across + (x - dx) % across
        return lax.dynamic_slice_in_dim(ffn_part, place_of * slab, slab, 1)

    ffn_x = [
        [Held(shift(ffn_piece(dz, dx), 0, dx)) for dx in range(1, across)] for dz in range(deep)
    ]
    dm = right_product(dy_full, w_down)
    da = meet_one(dm * c * slope, *ffn_x[1 % deep])
    dc = dm * act
    da_y, dc_y = Along(da, 2), Along(dc, 2)
    dhnorm = meet_one(right_product(da, w_gate), *ffn_x[2 % deep], *hnorm_y[0])
    dhnorm = dhnorm + right_product(dc, w_up)
    dhnorm = meet_one(dhnorm, *hnorm_y[1], *ffn_x[3 % deep])

    def ffn_tile(dz):
        out = ffn_piece(dz, 0)
        for item in ffn_x[dz]:
            out = out + item.value
        return out

    ffn_steps = []

    def ffn_step(dz):
        ffn_steps.append(Held(shift(ffn_steps[-1].value + ffn_tile(dz) if ffn_steps else ffn_tile(dz), 1, 0)))
        return ffn_steps[-1]

    d_gain_two = jnp.sum(dhnorm * whole * r2, 0, keepdims=True)
    weighted = dhnorm * gain_two
    d_whole = r2 * weighted - whole * (r2 * r2 * r2) * jnp.mean(
        whole * weighted, -1, keepdims=True
    )
    pad = jnp.zeros((7, width), f32)
    da_pair, dc_pair = both_cores(da), both_cores(dc)
    own_gate = Held(left_product(da_pair, hnorm_y.own))
    own_up = Held(left_product(dc_pair, hnorm_y.own))
    own_down = Held(left_product(both_cores(m), tokens_half(dy_full, core)))
    d_part = scatter_columns(
        d_whole,
        jnp.concatenate([d_gain_two, pad], 0),
        [
            [*ffn_x[0], *hnorm_y[2], *hnorm_y[3]],
            [*hnorm_y[4], *hnorm_y[5], own_down],
            lambda: [*hnorm_y[6], own_gate, ffn_step(1)],
            [*hnorm_y[7], *da_y[0], own_up],
        ],
    )
    d_hidden = grad_output + d_part[:length]
    d_gain_two = d_part[length]
    own_out = Held(left_product(gathered_pair, both_cores(d_hidden)))
    down_y = Along(own_down.value, 4, 1)
    late = {}

    def cores(values):
        return [both_cores(value) for value in values]

    def total(name, own, lefts, rights):
        for left, right in zip(lefts[1:], rights[1:]):
            own = own + left_product(left, right)
        late[name] = Held(own)
        return late[name]

    def placed(name, value, axis, widths=None):
        late[name] = [Held(item) for item in finish(value, core, axis, widths)]
        return late[name]

    d_gated = scatter_columns(
        right_product(d_hidden, w_out),
        None,
        [
            lambda: [*da_y[1], *down_y[0], *([ffn_step(2)] if deep > 2 else [])],
            [*dc_y[0], *down_y[1], own_out],
            lambda: [
                *dc_y[1], *down_y[2],
                total("gate", own_gate.value, cores(da_y.all()), hnorm_y.all()),
            ],
            lambda: [
                *down_y[3],
                total("up", own_up.value, cores(dc_y.all()), hnorm_y.all()),
            ],
        ],
    )
    out_y = Along(own_out.value, 1)
    for dz in range(3, deep):
        ffn_step(dz)
    ffn = Held(ffn_steps[-1].value + ffn_tile(0))
    d_shaped = d_gated * gate_act
    d_gate_pre = d_gated * shaped * gate_slope
    d_post_gain = jnp.sum(d_shaped * centered, 0)
    d_post_shift = jnp.sum(d_shaped, 0)
    d_center = d_shaped * post_gain
    gain_half = half_of(gain_one, core, 0)
    normed_pairs = [pair * gain_half for pair in unit_y.all()]
    d_gate_y = Along(d_gate_pre, 1)
    own_attn = Held(left_product(normed_pairs[0], both_cores(d_gate_pre)))
    back_sums = butterfly(
        jnp.stack([jnp.sum(d_center, 1), jnp.sum(d_center * centered, 1)]), "heads"
    )
    d_mixed = inv_std * (
        d_center - back_sums[0][:, None] / total_span
        - centered * back_sums[1][:, None] / total_span
    )
    dq, dk, dv, d_rate, dw, db, dg, dsh = ttt_backward(
        joined, rate_t, seg, seg_t, w0, b0, gain_col, shift_col, saved, d_mixed, hd, heads
    )
    dq = meet_one(dq, *out_y[0], *d_gate_y[0], own_attn, ffn)
    output = hidden + ffn.value
    ffn = ffn.value
    d_inner_weight, d_inner_bias = state_back(dw, db, heads, hd)
    d_rate_pre = d_rate * rate_t * (1.0 - sig)
    d_three = jnp.concatenate([dq, dk, dv], 1)
    d_three_y, d_rate_y = Along(d_three, 1), Along(d_rate_pre, 1)
    d_joined = jnp.concatenate([d_three, d_gate_pre], 1)
    d_normed = right_product(d_joined, w_joined) + lax.dot_general(
        d_rate_pre, w_rate, (((0,), (1,)), ((), ())), precision=lax.Precision.HIGH,
        preferred_element_type=f32,
    )
    d_gain_one = jnp.sum(d_normed * tokens * r1, 0, keepdims=True)
    weighted = d_normed * gain_one
    d_tokens = r1 * weighted - tokens * (r1 * r1 * r1) * jnp.mean(
        tokens * weighted, -1, keepdims=True
    )

    own_three = Held(left_product(normed_pairs[0], both_cores(d_three)))
    weights = valid_mask.reshape(-1).astype(f32)[:, None]
    stats = jnp.stack(
        [
            jnp.sum(weights * member * member)
            for member in (stream_cols, attn, hidden, ffn, output)
        ]
        + [jnp.sum(weights) / lax.axis_size("heads")]
    )
    def rate_total():
        out = None
        for pair, d in zip(normed_pairs, d_rate_y.all()):
            part = product(jnp.concatenate([d, swap(d, "rows", 1)], 1), pair)
            out = part if out is None else out + part
        late["rate"] = Held(out)
        return late["rate"]

    hooks = [
        lambda: [own_three, *placed("g_gate", late["gate"].value, 1)],
        lambda: [
            total("attn", own_attn.value, normed_pairs, cores(d_gate_y.all())),
            *placed("g_up", late["up"].value, 1),
        ],
        lambda: [
            *d_three_y[0], *d_rate_y[0],
            *placed("g_down", sum(down_y.all()), 1),
            *placed("g_out", sum(out_y.all()), 0),
        ],
        lambda: [
            total("three", own_three.value, normed_pairs, cores(d_three_y.all())),
            *placed("g_attn", late["attn"].value, 0),
            rate_total(),
        ],
    ]
    across_slabs = jnp.tile(jnp.pad(stats, (0, slab - stats.size)), width // slab)[None]
    d_part = scatter_columns(
        d_tokens,
        jnp.concatenate([d_gain_one, across_slabs, pad[1:]], 0),
        hooks,
    )
    d_stream = d_hidden + d_part[:length]
    d_gain_one = d_part[length]
    stats = d_part[length + 1, : stats.size]

    ((g_gate,), (g_up,), (g_down,), (g_out,), (g_gate_attn,)) = (
        [item.value for item in late[name]]
        for name in ("g_gate", "g_up", "g_down", "g_out", "g_attn")
    )
    g_query, g_key, g_value = finish(late["three"].value, core, 0, (span,) * 3)
    g_rate = late["rate"].value
    ends = (g_rate, swap(g_rate, "rows", 1))
    g_rate = jnp.where(core == 0, jnp.concatenate(ends, 1), jnp.concatenate(ends[::-1], 1))

    small = [
        d_gain_one, jnp.sum(d_rate_pre, 1), d_inner_weight, d_inner_bias, dg, dsh,
        d_post_gain, d_post_shift, d_gain_two, stats,
    ]
    packed = butterfly(jnp.concatenate([item.reshape(-1) for item in small]), "rows")
    parts = []
    at = 0
    for item in small:
        parts.append(packed[at : at + item.size])
        at += item.size
    stats = parts[9]
    rms_values = jnp.sqrt(stats[:5] / (stats[5] * width))
    return (
        output.reshape(1, length, slab),
        d_stream.reshape(1, length, slab),
        parts[0],
        g_query,
        g_key,
        g_value,
        g_rate.T,
        parts[1],
        parts[2].reshape(heads, hd, hd),
        parts[3].reshape(heads, hd),
        parts[4].reshape(heads, hd),
        parts[5].reshape(heads, hd),
        parts[6],
        parts[7],
        g_gate_attn,
        g_out,
        parts[8],
        g_gate.T,
        g_up.T,
        g_down,
        rms_values,
    )


def solution(mesh):
    in_specs = (
        P("rows", None, None),
        P("rows", None),
        P("rows", None),
        P("heads"),
        P(None, "heads"),
        P(None, "heads"),
        P(None, "heads"),
        P(None, "heads"),
        P("heads"),
        P("heads", None, None),
        P("heads", None),
        P("heads", None),
        P("heads", None),
        P("heads"),
        P("heads"),
        P(None, "heads"),
        P(None, "heads"),
        P("heads"),
        P(None, "heads"),
        P(None, "heads"),
        P("heads", None),
        P("rows", None, "heads"),
    )
    out_specs = (
        P("rows", None, "heads"),
        P("rows", None, "heads"),
        P("heads"),
        P(None, "heads"),
        P(None, "heads"),
        P(None, "heads"),
        P(None, "heads"),
        P("heads"),
        P("heads", None, None),
        P("heads", None),
        P("heads", None),
        P("heads", None),
        P("heads"),
        P("heads"),
        P(None, "heads"),
        P(None, "heads"),
        P("heads"),
        P(None, "heads"),
        P(None, "heads"),
        P("heads", None),
        P(),
    )
    return jax.shard_map(
        on_device, mesh=mesh, in_specs=in_specs, out_specs=out_specs, check_vma=False
    )
```

```python
import functools
import jax, jax.numpy as jnp
from jax import lax
from jax.experimental import pallas as pl
from jax.experimental.pallas import tpu as pltpu

from jax.sharding import PartitionSpec as P

MB = 16
CH = 128
epsilon = 1e-06
f32 = jnp.float32
bf16 = jnp.bfloat16
NN = ((1,), (0,))


def split(x):
    hi = x.astype(bf16)
    return hi, (x - hi.astype(f32)).astype(bf16)


def mm(a, b, dims=NN):
    def one(p, q):
        return lax.dot_general(p, q, (dims, ((), ())), preferred_element_type=f32)

    return one(a[0], b[0]) + (one(a[0], b[1]) + one(a[1], b[0]))


def wide(x):
    hi, lo = split(x)
    return jnp.concatenate([hi, lo], axis=1)


def tall_dot(x, pair):
    rows = x.shape[0]
    cols = pair.shape[1] // 2
    hi, lo = split(x)
    out = lax.dot_general(
        jnp.concatenate([hi, lo], axis=0), pair, (NN, ((), ())), preferred_element_type=f32
    )
    top, low = out[:rows], out[rows:]
    return top[:, :cols] + (top[:, cols:] + low[:, :cols])


def iota(shape, dim):
    return lax.broadcasted_iota(jnp.int32, shape, dim)


def head_sum(x, hd):
    rows, cols = x.shape
    parts = [
        jnp.broadcast_to(jnp.sum(x[i : i + hd], axis=0, keepdims=True), (hd, cols))
        for i in range(0, rows, hd)
    ]
    return parts[0] if len(parts) == 1 else jnp.concatenate(parts, axis=0)


def lane_sum(x):
    return jnp.sum(x, axis=1, keepdims=True)


def coefficients(transposed):
    source = iota((CH, CH), 1 if transposed else 0)
    target = iota((CH, CH), 0 if transposed else 1)
    before = (source // MB < target // MB).astype(f32) * (1.0 / MB)
    inside = ((source // MB == target // MB) & (source <= target)).astype(f32)
    return before, before + inside / ((target % MB) + 1).astype(f32)


def forward_body(
    joined, rate, rate_t, seg, seg_t, w0, b0, gain, shift, mixed, z_out, zb_out, w_out, b_out,
    w_s, b_s, z_s, tau_s, a_s, m_s, *, hd, heads,
):
    pairs = heads * hd // CH
    per = CH // hd
    span = heads * hd
    chunks = joined.shape[0] // CH
    n_inv = 1.0 / hd
    row_head = iota((CH, CH), 0) // hd
    lane_head = iota((CH, CH), 1) // hd
    lane_block = iota((hd, CH), 1) // MB
    block_diag = row_head == lane_head
    w_s[...] = jnp.zeros_like(w_s)
    b_s[...] = jnp.zeros_like(b_s)

    def chunk(c, carry):
        ts = pl.multiple_of(c * CH, CH)
        here = pl.ds(ts, CH)
        seg_row = seg_t[:, here]
        seg_col = seg[here, :]
        last_seg = seg_row[:, CH - 1 : CH]
        prev = jnp.max(jnp.where(iota(seg_t.shape, 1) < ts, seg_t[...], 0.0), keepdims=True)
        carried = seg_row == prev
        in_last = (seg_row == last_seg).astype(f32)
        whole = last_seg == prev
        same = seg_col == seg_row
        before, within = coefficients(False)
        before = jnp.where(same, before, 0.0)
        within = jnp.where(same, within, 0.0)
        for p in range(pairs):
            rows = slice(p * CH, (p + 1) * CH)
            kn = joined[here, span + p * CH : span + (p + 1) * CH]
            qn = joined[here, p * CH : (p + 1) * CH]
            vn = joined[here, 2 * span + p * CH : 2 * span + (p + 1) * CH]
            k_t, q_t, v_t = kn.T, qn.T, vn.T
            ks, kts, qts = split(kn), split(k_t), split(q_t)
            ws, w0s = split(w_s[rows]), split(w0[rows])
            bias = jnp.where(carried, b_s[rows], b0[rows])
            z_s[rows] = jnp.where(carried, mm(ws, kts), mm(w0s, kts)) + bias
            zb_out[rows, here] = jnp.where(carried, mm(ws, qts), mm(w0s, qts)) + bias
            w_out[c, rows] = w_s[rows]
            b_out[c, rows] = b_s[rows]
            tau_s[rows] = gain[rows] * (shift[rows] - v_t + k_t)
            for hh in range(per):
                h = p * per + hh
                own = (row_head == hh).astype(bf16)
                r_col = rate[here, h : h + 1]
                score = mm(ks, (kts[0] * own, kts[1] * own))
                a_s[h] = wide((score + 1.0) * (before * r_col))
                score = mm(ks, (qts[0] * own, qts[1] * own))
                m_s[h] = wide((score + 1.0) * (within * r_col))

        gsq = [jnp.broadcast_to(gain[h * hd : (h + 1) * hd] ** 2, (hd, CH)) for h in range(heads)]
        tsum = [
            jnp.sum(tau_s[h * hd : (h + 1) * hd], axis=0, keepdims=True) * n_inv
            for h in range(heads)
        ]

        def inner(h, z):
            tau = tau_s[h * hd : (h + 1) * hd]
            zg = z * gsq[h]
            m2 = jnp.sum(z * z, axis=0, keepdims=True) * n_inv
            a1 = jnp.sum(zg, axis=0, keepdims=True) * n_inv
            a2 = jnp.sum(z * zg, axis=0, keepdims=True) * n_inv
            a3 = jnp.sum(z * tau, axis=0, keepdims=True) * n_inv
            s = lax.rsqrt(m2 + epsilon)
            c_eu = s * (s * a2 + a3)
            e_mean = s * a1 + tsum[h]
            return (s * s) * (zg - c_eu * z) + s * (tau - e_mean)

        def step(t, zs):
            now = lane_block == t
            new = []
            for h in range(heads):
                g = jnp.where(now, inner(h, zs[h]), 0.0)
                new.append(zs[h] - tall_dot(g, a_s[h]))
            return tuple(new)

        zs = tuple(z_s[h * hd : (h + 1) * hd] for h in range(heads))
        zs = lax.fori_loop(0, CH // MB - 1, step, zs)
        for p in range(pairs):
            rows = slice(p * CH, (p + 1) * CH)
            gs = []
            outs = []
            for hh in range(per):
                h = p * per + hh
                hr = slice(h * hd, (h + 1) * hd)
                z_out[hr, here] = zs[h]
                g = inner(h, zs[h])
                zb = zb_out[hr, here] - tall_dot(g, m_s[h])
                zb_out[hr, here] = zb
                sb = lax.rsqrt(jnp.sum(zb * zb, axis=0, keepdims=True) * n_inv + epsilon)
                outs.append(zb * sb * gain[hr] + shift[hr])
                gs.append(g * (rate_t[h : h + 1, here] * in_last * (1.0 / MB)))
            gw = jnp.concatenate(gs, axis=0)
            lanes = slice(p * CH, (p + 1) * CH)
            mixed[here, lanes] = joined[here, lanes] + jnp.concatenate(outs, axis=0).T
            kn = joined[here, span + p * CH : span + (p + 1) * CH]
            upd = mm(split(gw), split(kn))
            w_s[rows] = jnp.where(whole, w_s[rows], w0[rows]) - jnp.where(block_diag, upd, 0.0)
            b_s[rows] = jnp.where(whole, b_s[rows], b0[rows]) - lane_sum(gw)
        return carry

    lax.fori_loop(0, chunks, chunk, 0)


def ttt_forward(joined, rate, rate_t, seg, seg_t, w0, b0, gain, shift, hd, heads):
    length = joined.shape[0]
    span = heads * hd
    chunks = length // CH
    shape = jax.ShapeDtypeStruct
    return pl.pallas_call(
        functools.partial(forward_body, hd=hd, heads=heads),
        out_shape=(
            shape((length, span), f32),
            shape((span, length), f32),
            shape((span, length), f32),
            shape((chunks, span, CH), f32),
            shape((chunks, span, 1), f32),
        ),
        scratch_shapes=[
            pltpu.VMEM((span, CH), f32),
            pltpu.VMEM((span, 1), f32),
            pltpu.VMEM((span, CH), f32),
            pltpu.VMEM((span, CH), f32),
            pltpu.VMEM((heads, CH, 2 * CH), bf16),
            pltpu.VMEM((heads, CH, 2 * CH), bf16),
        ],
        compiler_params=pltpu.CompilerParams(vmem_limit_bytes=48 << 20),
        name="inner_forward",
    )(joined, rate, rate_t, seg, seg_t, w0, b0, gain, shift)


def backward_body(
    joined, rate_t, seg, seg_t, w0, b0, gain, shift, z_in, zb_in, w_in, b_in, dy,
    dq_out, dk_out, dv_out, dr_out, dw_out, db_out, dg_out, dsh_out,
    dw_s, db_s, p_s, u_s, f_s, bb_s, e2_s, u2_s, gt_s, dzb_s, at_s, sc_s,
    *, hd, heads,
):
    pairs = heads * hd // CH
    per = CH // hd
    span = heads * hd
    chunks = joined.shape[0] // CH
    n_inv = 1.0 / hd
    row_head = iota((CH, CH), 0) // hd
    lane_head = iota((CH, CH), 1) // hd
    lane_block = iota((hd, CH), 1) // MB
    block_diag = row_head == lane_head
    for ref in (dw_s, db_s, dw_out, db_out, dg_out, dsh_out):
        ref[...] = jnp.zeros_like(ref)

    def mean(x):
        return head_sum(x, hd) * n_inv

    def chunk(index, carry):
        c = chunks - 1 - index
        ts = pl.multiple_of(c * CH, CH)
        here = pl.ds(ts, CH)
        seg_row = seg_t[:, here]
        seg_col = seg[here, :]
        last_seg = seg_row[:, CH - 1 : CH]
        prev = jnp.max(jnp.where(iota(seg_t.shape, 1) < ts, seg_t[...], 0.0), keepdims=True)
        carried = seg_row == prev
        carried_col = seg_col == prev
        in_last = (seg_row == last_seg).astype(f32)
        whole = last_seg == prev
        same = seg_col == seg_row
        before, within = coefficients(True)
        before = jnp.where(same, before, 0.0)
        within = jnp.where(same, within, 0.0)
        consts = {}
        for p in range(pairs):
            rows = slice(p * CH, (p + 1) * CH)
            lanes = slice(p * CH, (p + 1) * CH)
            qn = joined[here, p * CH : (p + 1) * CH]
            kn = joined[here, span + p * CH : span + (p + 1) * CH]
            vn = joined[here, 2 * span + p * CH : 2 * span + (p + 1) * CH]
            k_t, v_t, dy_t = kn.T, vn.T, dy[here, lanes].T
            qs, ks, kts = split(qn), split(kn), split(k_t)
            g_col = gain[rows]
            gsq = g_col * g_col
            zb = zb_in[rows, here]
            sb = lax.rsqrt(mean(zb * zb) + epsilon)
            ub = zb * sb
            dg_out[rows] += lane_sum(dy_t * ub)
            dsh_out[rows] += lane_sum(dy_t)
            pb = dy_t * g_col
            dzb = sb * (pb - mean(pb) - ub * mean(pb * ub))
            dzb_s[rows] = dzb
            z = z_in[rows, here]
            s = lax.rsqrt(mean(z * z) + epsilon)
            u = z * s
            gu = gsq * u
            e = gu + g_col * (shift[rows] - v_t + k_t)
            c_eu = mean(e * u)
            g_t = s * (e - mean(e) - u * c_eu)
            gt_s[rows] = g_t
            u_s[rows] = u
            f_s[rows] = g_t + s * gu
            bb_s[rows] = (s * s) * (gsq - c_eu)
            e2_s[rows] = (s * s) * (e + gu)
            u2_s[rows] = s * u
            h1 = s * mean(gu)
            h2 = 2.0 * s * c_eu + s * mean(gu * u)
            dzbs = split(dzb)
            gts = split(g_t)
            dzbn = split(dzb.T)
            from_state = mm(split(dw_s[rows]), kts) + db_s[rows]
            pieces = []
            dq = dy[here, lanes]
            dk = jnp.zeros((CH, CH), f32)
            for hh in range(per):
                h = p * per + hh
                hr = slice(hh * hd, (hh + 1) * hd)
                r_row = rate_t[h : h + 1, here]
                consts[h] = (h1[hh * hd : hh * hd + 1], h2[hh * hd : hh * hd + 1])
                own = (row_head == hh).astype(bf16)
                own_lane = (lane_head == hh).astype(bf16)
                kt_h = (kts[0] * own, kts[1] * own)
                sc = (mm(ks, kt_h) + 1.0) * before
                sc_s[h] = sc
                at_s[h] = wide(sc * r_row)
                scq = (mm(qs, kt_h) + 1.0) * within
                pt = mm(dzbn, (gts[0] * own, gts[1] * own))
                dr_out[h : h + 1, here] = -jnp.sum(pt * scq, axis=0, keepdims=True) - (
                    (1.0 / MB) * in_last
                ) * jnp.sum(g_t[hr] * from_state[hr], axis=0, keepdims=True)
                pm = pt * (within * r_row)
                pms = split(pm)
                pmts = split(pm.T)
                kn_h = (ks[0] * own_lane, ks[1] * own_lane)
                qn_h = (qs[0] * own_lane, qs[1] * own_lane)
                dq = dq - mm(pms, kn_h)
                dk = dk - mm(pmts, qn_h)
                pieces.append(
                    -mm((dzbs[0][hr], dzbs[1][hr]), split(scq * r_row))
                    - from_state[hr] * (r_row * in_last * (1.0 / MB))
                )
            p_s[rows] = jnp.concatenate(pieces, axis=0)
            w0s = split(w0[rows])
            wd = split(w_in[c, rows] - w0[rows])
            zero = jnp.zeros((), bf16)
            dzbn_c = (jnp.where(carried_col, dzbn[0], zero), jnp.where(carried_col, dzbn[1], zero))
            dq_out[here, lanes] = dq + mm(dzbn, w0s) + mm(dzbn_c, wd)
            dk_out[here, lanes] = dk

        def upstream(h, pv):
            hr = slice(h * hd, (h + 1) * hd)
            h1, h2 = consts[h]
            pm = jnp.sum(pv, axis=0, keepdims=True) * n_inv
            q = jnp.sum(pv * u_s[hr], axis=0, keepdims=True) * n_inv
            kf = jnp.sum(pv * f_s[hr], axis=0, keepdims=True) * n_inv
            kappa = kf - h1 * pm - h2 * q
            dz = (pv - pm) * bb_s[hr] - q * e2_s[hr] - kappa * u2_s[hr]
            return dz, pm, q

        def step(index, ps):
            now = lane_block == (CH // MB - 1 - index)
            new = []
            for h in range(heads):
                dz = jnp.where(now, upstream(h, ps[h])[0], 0.0)
                new.append(ps[h] - tall_dot(dz, at_s[h]))
            return tuple(new)

        ps = tuple(p_s[h * hd : (h + 1) * hd] for h in range(heads))
        ps = lax.fori_loop(0, CH // MB - 1, step, ps)

        for p in range(pairs):
            rows = slice(p * CH, (p + 1) * CH)
            lanes = slice(p * CH, (p + 1) * CH)
            qn = joined[here, p * CH : (p + 1) * CH]
            kn = joined[here, span + p * CH : span + (p + 1) * CH]
            vn = joined[here, 2 * span + p * CH : 2 * span + (p + 1) * CH]
            qs, ks = split(qn), split(kn)
            g_t = gt_s[rows]
            gts = split(g_t)
            dzs, des = [], []
            for hh in range(per):
                h = p * per + hh
                hr = slice(h * hd, (h + 1) * hd)
                dz, pm, q = upstream(h, ps[h])
                dzs.append(dz - jnp.sum(dz, axis=0, keepdims=True) * n_inv)
                z = z_in[hr, here]
                s = lax.rsqrt(jnp.sum(z * z, axis=0, keepdims=True) * n_inv + epsilon)
                des.append(s * (ps[h] - pm - u_s[hr] * q))
            dz = jnp.concatenate(dzs, axis=0)
            de = jnp.concatenate(des, axis=0)
            g_col = gain[rows]
            gde = g_col * de
            t_t = shift[rows] + (kn - vn).T
            dg_out[rows] += lane_sum((2.0 * g_col * u_s[rows] + t_t) * de)
            dsh_out[rows] += lane_sum(gde)
            gden = gde.T
            dv_out[here, lanes] = -gden
            dzn = split(dz.T)
            dk = dk_out[here, lanes] + gden
            r_rows = []
            for hh in range(per):
                h = p * per + hh
                r_row = rate_t[h : h + 1, here]
                own = (row_head == hh).astype(bf16)
                own_lane = (lane_head == hh).astype(bf16)
                rt = mm(dzn, (gts[0] * own, gts[1] * own))
                dr_out[h : h + 1, here] -= jnp.sum(rt * sc_s[h], axis=0, keepdims=True)
                ra = rt * (before * r_row)
                dk = dk - mm(split(ra + ra.T), (ks[0] * own_lane, ks[1] * own_lane))
                r_rows.append(jnp.broadcast_to(r_row * in_last * (1.0 / MB), (hd, CH)))
            gw = g_t * jnp.concatenate(r_rows, axis=0)
            w0s = split(w0[rows])
            wd = split(w_in[c, rows] - w0[rows])
            zero = jnp.zeros((), bf16)
            dzn_c = (jnp.where(carried_col, dzn[0], zero), jnp.where(carried_col, dzn[1], zero))
            dk = dk + mm(dzn, w0s) + mm(dzn_c, wd) - mm(split(gw.T), split(dw_s[rows]))
            dk_out[here, lanes] = dk
            dzb = dzb_s[rows]
            dzc = jnp.where(carried, dz, 0.0)
            dzbc = jnp.where(carried, dzb, 0.0)
            diag = jnp.where(block_diag, mm(split(dzc), ks) + mm(split(dzbc), qs), 0.0)
            rest = jnp.where(
                block_diag, mm(split(dz - dzc), ks) + mm(split(dzb - dzbc), qs), 0.0
            )
            dw = dw_s[rows]
            db = db_s[rows]
            dw_out[rows] += jnp.where(whole, 0.0, dw) + rest
            db_out[rows] += jnp.where(whole, 0.0, db) + lane_sum(dz - dzc + dzb - dzbc)
            dw_s[rows] = jnp.where(whole, dw, 0.0) + diag
            db_s[rows] = jnp.where(whole, db, 0.0) + lane_sum(dzc + dzbc)
        return carry

    lax.fori_loop(0, chunks, chunk, 0)


def ttt_backward(joined, rate_t, seg, seg_t, w0, b0, gain, shift, saved, dy, hd, heads):
    length = joined.shape[0]
    span = heads * hd
    shape = jax.ShapeDtypeStruct
    return pl.pallas_call(
        functools.partial(backward_body, hd=hd, heads=heads),
        out_shape=(
            shape((length, span), f32),
            shape((length, span), f32),
            shape((length, span), f32),
            shape((heads, length), f32),
            shape((span, CH), f32),
            shape((span, 1), f32),
            shape((span, 1), f32),
            shape((span, 1), f32),
        ),
        scratch_shapes=[
            pltpu.VMEM((span, CH), f32),
            pltpu.VMEM((span, 1), f32),
        ]
        + [pltpu.VMEM((span, CH), f32)] * 8
        + [
            pltpu.VMEM((heads, CH, 2 * CH), bf16),
            pltpu.VMEM((heads, CH, CH), f32),
        ],
        compiler_params=pltpu.CompilerParams(vmem_limit_bytes=48 << 20),
        name="inner_backward",
    )(joined, rate_t, seg, seg_t, w0, b0, gain, shift, *saved, dy)


def state_in(inner_weight, inner_bias):
    heads, hd, _ = inner_weight.shape
    per = CH // hd
    w_t = jnp.swapaxes(inner_weight, 1, 2)
    w_t = w_t - jnp.mean(w_t, axis=1, keepdims=True)
    placed = [
        jnp.pad(w_t[h], ((0, 0), ((h % per) * hd, CH - hd - (h % per) * hd)))
        for h in range(heads)
    ]
    b = inner_bias - jnp.mean(inner_bias, axis=1, keepdims=True)
    return jnp.concatenate(placed, axis=0), b.reshape(heads * hd, 1)


def state_back(dw, db, heads, hd):
    per = CH // hd
    parts = [
        dw[h * hd : (h + 1) * hd, (h % per) * hd : (h % per + 1) * hd] for h in range(heads)
    ]
    d = jnp.stack(parts)
    d = jnp.swapaxes(d - jnp.mean(d, axis=1, keepdims=True), 1, 2)
    b = db.reshape(heads, hd)
    return d, b - jnp.mean(b, axis=1, keepdims=True)


def product(left, right):
    return jnp.dot(left, right, precision=lax.Precision.HIGH, preferred_element_type=f32)


def left_product(left, right):
    return lax.dot_general(
        left, right, (((0,), (0,)), ((), ())), precision=lax.Precision.HIGH,
        preferred_element_type=f32,
    )


def right_product(left, right):
    return lax.dot_general(
        left, right, (((1,), (1,)), ((), ())), precision=lax.Precision.HIGH,
        preferred_element_type=f32,
    )


def heads_grid():
    size = lax.axis_size("heads")
    deep = 4 if size % 4 == 0 else 1
    return deep, size // deep


def heads_place():
    _, across = heads_grid()
    index = lax.axis_index("heads")
    return index // across, index % across


def shift(value, dz, dx):
    deep, across = heads_grid()
    pairs = [
        (h, (h // across + dz) % deep * across + (h % across + dx) % across)
        for h in range(deep * across)
    ]
    return lax.ppermute(value, "heads", pairs)


def swap(value, axis, bit):
    return lax.ppermute(value, axis, [(i, i ^ bit) for i in range(lax.axis_size(axis))])


def row_shift(value, step):
    size = lax.axis_size("rows")
    return lax.ppermute(value, "rows", [(r, (r + 2 * step) % size) for r in range(size)])


def butterfly(value, axis, hooks=()):
    size = lax.axis_size(axis)
    bits = [1 << i for i in range(size.bit_length() - 1)][::-1]
    for index, bit in enumerate(bits):
        (other,) = meet([swap(value, axis, bit)], turn(hooks, index))
        value = value + other
    return value


def small_gather(value, hooks=()):
    size = lax.axis_size("heads")
    place = jnp.arange(size) == lax.axis_index("heads")
    place = place.reshape((size,) + (1,) * value.ndim)
    return butterfly(jnp.where(place, value[None], 0.0), "heads", hooks)


class Held:
    def __init__(self, value):
        self.value = value


def meet(values, held=()):
    out = lax.optimization_barrier(tuple(values) + tuple(item.value for item in held))
    for item, value in zip(held, out[len(values) :]):
        item.value = value
    return list(out[: len(values)])


def meet_one(value, *held):
    return meet([value], held)[0]


def turn(hooks, index):
    hook = hooks[index] if index < len(hooks) else ()
    return hook() if callable(hook) else hook


def gather_columns(value, hooks=()):
    deep, across = heads_grid()
    z, x = heads_place()
    rows, cols = value.shape
    out = jnp.zeros((rows, cols * deep * across), value.dtype)
    here, ready = value, [(0, 0, value)]
    for dz in range(deep):
        moved = [shift(here, 0, dx) for dx in range(1, across)]
        if dz + 1 < deep:
            moved.append(shift(here, 1, 0))
        for oz, ox, item in ready:
            column = ((z - oz) % deep * across + (x - ox) % across) * cols
            out = lax.dynamic_update_slice(out, item, (0, column))
        *moved, out = meet(moved + [out], turn(hooks, dz))
        ready = [(dz, dx, moved[dx - 1]) for dx in range(1, across)]
        if dz + 1 < deep:
            here = moved[-1]
            ready.append((dz + 1, 0, here))
    for oz, ox, item in ready:
        column = ((z - oz) % deep * across + (x - ox) % across) * cols
        out = lax.dynamic_update_slice(out, item, (0, column))
    return out


def scatter_columns(value, extra=None, hooks=()):
    deep, across = heads_grid()
    z, x = heads_place()
    rows, width = value.shape
    cols = width // (deep * across)

    def piece(dz, dx):
        column = ((z - dz) % deep * across + (x - dx) % across) * cols
        block = lax.dynamic_slice(value, (0, column), (rows, cols))
        if extra is not None:
            tail = lax.dynamic_slice(extra, (0, column), (extra.shape[0], cols))
            block = jnp.concatenate([block, tail], 0)
        return block

    total = None
    for index, dz in enumerate(list(range(1, deep)) + [0]):
        moved = [shift(piece(dz, dx), 0, dx) for dx in range(1, across)]
        if total is not None:
            moved.append(shift(total, 1, 0))
        total = piece(dz, 0)
        for item in meet(moved, turn(hooks, index)):
            total = total + item
    return total


def half_of(value, index, axis):
    size = value.shape[axis] // 2
    return lax.dynamic_slice_in_dim(value, index * size, size, axis)


def both_cores(value):
    return jnp.concatenate([value, swap(value, "rows", 1)], 0)


def tokens_half(value, core):
    return jnp.concatenate(
        [half_of(value, core, 1), swap(half_of(value, 1 - core, 1), "rows", 1)], 0
    )


def chips_along():
    return lax.axis_size("rows") // 2


def other_chips(value):
    return [row_shift(value, step) for step in range(1, chips_along())]


def place_body(core, own, other, *outs, axis, widths):
    first = core[0] == 0
    at = 0
    for out, width in zip(outs, widths):
        mine, its = (own[:, at : at + width], other[:, at : at + width]) if axis == 0 else (own[...], other[...])
        low = jnp.where(first, mine, its)
        high = jnp.where(first, its, mine)
        if axis == 0:
            out[0] = low
            out[1] = high
        else:
            out[:, : low.shape[1]] = low
            out[:, low.shape[1] :] = high
        at += width


def place(own, other, core, axis, widths):
    rows, cols = own.shape
    steps = max(n for n in (1, 2, 4) if rows % (8 * n) == 0)
    size = rows // steps
    part = pl.BlockSpec((size, cols), lambda i: (i, 0))
    if axis == 0:
        shapes = [(2, rows, width) for width in widths]
        specs = [pl.BlockSpec((2, size, width), lambda i: (0, i, 0)) for width in widths]
    else:
        shapes = [(rows, 2 * cols)]
        specs = [pl.BlockSpec((size, 2 * cols), lambda i: (i, 0))]
    out = pl.pallas_call(
        functools.partial(place_body, axis=axis, widths=widths),
        grid=(steps,),
        out_shape=[jax.ShapeDtypeStruct(shape, f32) for shape in shapes],
        in_specs=[pl.BlockSpec(memory_space=pltpu.SMEM), part, part],
        out_specs=specs,
        compiler_params=pltpu.CompilerParams(vmem_limit_bytes=48 << 20),
        name="place",
    )(core.reshape(1).astype(jnp.int32), own, other)
    return [o.reshape(2 * rows, -1) if axis == 0 else o for o in out]


def finish(total, core, axis, widths=None):
    widths = (total.shape[1],) if widths is None else widths
    return place(total, swap(total, "rows", 1), core, axis, widths)


def row_products(lefts, rights):
    total = None
    for left, right in zip(lefts, rights):
        part = left_product(left, right)
        total = part if total is None else total + part
    return total


class Along:
    def __init__(self, value, parts=4, axis=0):
        self.own = value
        self.axis = axis
        pieces = jnp.split(value, parts, axis)
        self.steps = [
            [Held(row_shift(piece, step)) for piece in pieces] for step in range(1, chips_along())
        ]

    def __getitem__(self, i):
        return [step[i] for step in self.steps]

    def all(self):
        return [self.own] + [
            step[0].value if len(step) == 1
            else jnp.concatenate([item.value for item in step], self.axis)
            for step in self.steps
        ]


def silu_parts(a):
    sig = jax.nn.sigmoid(a)
    return a * sig, sig * (1.0 + a * (1.0 - sig))


def gelu_parts(v):
    k = 0.7978845608028654
    inner = k * (v + 0.044715 * v * v * v)
    th = jnp.tanh(inner)
    slope = 0.5 * (1.0 + th) + 0.5 * v * (1.0 - th * th) * k * (1.0 + 3 * 0.044715 * v * v)
    return 0.5 * v * (1.0 + th), slope


def on_device(
    stream,
    doc_starts,
    valid_mask,
    first_gain,
    w_query,
    w_key,
    w_value,
    w_rate,
    b_rate,
    inner_weight,
    inner_bias,
    inner_gain,
    inner_shift,
    post_gain,
    post_shift,
    w_gate_attn,
    w_out,
    second_gain,
    w_gate,
    w_up,
    w_down,
    cotangent,
):
    _, length, width = stream.shape
    tokens = stream.reshape(length, width)
    slab = second_gain.shape[0]
    column = lax.axis_index("heads") * slab
    core = lax.axis_index("rows") % 2
    heads, hd = inner_bias.shape
    span = heads * hd
    total_span = span * lax.axis_size("heads")
    grad_output = cotangent.reshape(length, slab)
    early = {}

    def first():
        early["r1"] = Held(lax.rsqrt(jnp.mean(tokens * tokens, -1, keepdims=True) + epsilon))
        return [early["r1"]]

    def second():
        early["unit"] = Held(tokens * early["r1"].value)
        return [early["unit"]]

    def third():
        early["pair"] = Held(half_of(early["unit"].value, core, 1))
        return [early["pair"]]

    gains = small_gather(jnp.stack([first_gain, second_gain]), [first, second, third])
    gain_one = gains[:, 0].reshape(width)
    gain_two = gains[:, 1].reshape(width)
    r1, unit = early["r1"].value, early["unit"].value
    dy_in, gain_one = lax.optimization_barrier((grad_output, gain_one))
    unit_y = Along(
        jnp.concatenate(
            [early["pair"].value, swap(half_of(unit, 1 - core, 1), "rows", 1)], 0
        )
    )
    w_joined = jnp.concatenate([w_query, w_key, w_value, w_gate_attn], axis=1)
    normed = unit * gain_one
    joined = product(normed, w_joined)
    rate_pre = lax.dot_general(
        w_rate, normed, (((0,), (1,)), ((), ())), precision=lax.Precision.HIGH,
        preferred_element_type=f32,
    )
    joined = Held(joined)
    after = {}

    def run_inner():
        after["mixed"] = [
            Held(item) for item in ttt_forward(
                joined.value, rate, rate_t, seg, seg_t, w0, b0, gain_col, shift_col, hd, heads
            )
        ]
        return [*after["mixed"], *unit_y[1]]

    sig = jax.nn.sigmoid(rate_pre + b_rate[:, None])
    rate_t = sig / hd
    rate = rate_t.T
    seg = jnp.cumsum(doc_starts.reshape(length)).astype(f32)
    seg, seg_t = seg[:, None], seg[None]
    w0, b0 = state_in(inner_weight, inner_bias)
    gain_col, shift_col = inner_gain.reshape(span, 1), inner_shift.reshape(span, 1)
    dy_held = Held(gather_columns(dy_in, [[], [joined, *unit_y[0]], run_inner]))
    joined = joined.value
    gate_pre = joined[:, 3 * span :]
    mixed, *saved = [item.value for item in after["mixed"]]
    row_sums = butterfly(jnp.stack([jnp.sum(mixed, 1), jnp.sum(mixed * mixed, 1)]), "heads")
    row_sums = meet_one(row_sums, *unit_y[2], dy_held)
    row_mean = row_sums[0] / total_span
    inv_std = lax.rsqrt(row_sums[1] / total_span - row_mean * row_mean + epsilon)[:, None]
    centered = (mixed - row_mean[:, None]) * inv_std
    shaped = centered * post_gain + post_shift
    gate_act, gate_slope = gelu_parts(gate_pre)
    gathered = gather_columns(gate_act * shaped, [(), unit_y[3]])
    gathered_pair = tokens_half(gathered, core)
    attn = product(gathered, w_out)
    stream_cols = lax.dynamic_slice_in_dim(tokens, column, slab, 1)
    hidden = stream_cols + attn
    whole = gather_columns(hidden)
    dy_full = dy_held.value

    r2 = lax.rsqrt(jnp.mean(whole * whole, -1, keepdims=True) + epsilon)
    hnorm = whole * r2 * gain_two
    hnorm_y = Along(tokens_half(hnorm, core), 8)
    a = product(hnorm, w_gate)
    c = product(hnorm, w_up)
    act, slope = silu_parts(a)
    m = act * c
    ffn_part = product(m, w_down)
    deep, across = heads_grid()
    z, x = heads_place()

    dy_full, ffn_part = lax.optimization_barrier((dy_full, ffn_part))

    def ffn_piece(dz, dx):
        place_of = (z - dz) % deep * across + (x - dx) % across
        return lax.dynamic_slice_in_dim(ffn_part, place_of * slab, slab, 1)

    ffn_x = [
        [Held(shift(ffn_piece(dz, dx), 0, dx)) for dx in range(1, across)] for dz in range(deep)
    ]
    dm = right_product(dy_full, w_down)
    da = meet_one(dm * c * slope, *ffn_x[1 % deep])
    dc = dm * act
    da_y, dc_y = Along(da, 2), Along(dc, 2)
    dhnorm = meet_one(right_product(da, w_gate), *ffn_x[2 % deep], *ffn_x[3 % deep], *hnorm_y[0])
    dhnorm = dhnorm + right_product(dc, w_up)
    dhnorm = meet_one(dhnorm, *hnorm_y[1])

    def ffn_tile(dz):
        out = ffn_piece(dz, 0)
        for item in ffn_x[dz]:
            out = out + item.value
        return out

    ffn_steps = []

    def ffn_step(dz):
        ffn_steps.append(Held(shift(ffn_steps[-1].value + ffn_tile(dz) if ffn_steps else ffn_tile(dz), 1, 0)))
        return ffn_steps[-1]

    d_gain_two = jnp.sum(dhnorm * whole * r2, 0, keepdims=True)
    weighted = dhnorm * gain_two
    d_whole = r2 * weighted - whole * (r2 * r2 * r2) * jnp.mean(
        whole * weighted, -1, keepdims=True
    )
    pad = jnp.zeros((7, width), f32)
    da_pair, dc_pair = both_cores(da), both_cores(dc)
    own_gate = Held(left_product(da_pair, hnorm_y.own))
    own_up = Held(left_product(dc_pair, hnorm_y.own))
    own_down = Held(left_product(both_cores(m), tokens_half(dy_full, core)))
    d_part = scatter_columns(
        d_whole,
        jnp.concatenate([d_gain_two, pad], 0),
        [
            [*ffn_x[0], *hnorm_y[2], *hnorm_y[3]],
            [*hnorm_y[4], *hnorm_y[5], own_down],
            lambda: [*hnorm_y[6], own_gate, ffn_step(1)],
            [*hnorm_y[7], *da_y[0], own_up],
        ],
    )
    d_hidden = grad_output + d_part[:length]
    d_gain_two = d_part[length]
    own_out = Held(left_product(gathered_pair, both_cores(d_hidden)))
    down_y = Along(own_down.value, 4, 1)
    late = {}

    def cores(values):
        return [both_cores(value) for value in values]

    def total(name, own, lefts, rights):
        for left, right in zip(lefts[1:], rights[1:]):
            own = own + left_product(left, right)
        late[name] = Held(own)
        return late[name]

    def placed(name, value, axis, widths=None):
        late[name] = [Held(item) for item in finish(value, core, axis, widths)]
        return late[name]

    d_gated = scatter_columns(
        right_product(d_hidden, w_out),
        None,
        [
            lambda: [*da_y[1], *([ffn_step(2)] if deep > 2 else [])],
            [*dc_y[0], own_out],
            lambda: [
                *dc_y[1],
                total("gate", own_gate.value, cores(da_y.all()), hnorm_y.all()),
            ],
            lambda: [
                *down_y[0],
                total("up", own_up.value, cores(dc_y.all()), hnorm_y.all()),
            ],
        ],
    )
    out_y = Along(own_out.value, 1)
    d_shaped = d_gated * gate_act
    d_gate_pre = d_gated * shaped * gate_slope
    d_post_gain = jnp.sum(d_shaped * centered, 0)
    d_post_shift = jnp.sum(d_shaped, 0)
    d_center = d_shaped * post_gain
    gain_half = half_of(gain_one, core, 0)
    normed_pairs = [pair * gain_half for pair in unit_y.all()]
    d_gate_y = Along(d_gate_pre, 1)
    own_attn = Held(left_product(normed_pairs[0], both_cores(d_gate_pre)))
    back_sums = butterfly(
        jnp.stack([jnp.sum(d_center, 1), jnp.sum(d_center * centered, 1)]), "heads"
    )
    back_sums = meet_one(back_sums, ffn_steps[-1])
    for dz in range(3, deep):
        ffn_step(dz)
    ffn = Held(ffn_steps[-1].value + ffn_tile(0))
    d_mixed = inv_std * (
        d_center - back_sums[0][:, None] / total_span
        - centered * back_sums[1][:, None] / total_span
    )
    dq, dk, dv, d_rate, dw, db, dg, dsh = ttt_backward(
        joined, rate_t, seg, seg_t, w0, b0, gain_col, shift_col, saved, d_mixed, hd, heads
    )
    dq = meet_one(dq, *down_y[1], *down_y[2], *down_y[3], own_attn, ffn)
    output = hidden + ffn.value
    ffn = ffn.value
    d_inner_weight, d_inner_bias = state_back(dw, db, heads, hd)
    d_rate_pre = d_rate * rate_t * (1.0 - sig)
    d_three = jnp.concatenate([dq, dk, dv], 1)
    d_three_y, d_rate_y = Along(d_three, 1), Along(d_rate_pre, 1)
    d_joined = jnp.concatenate([d_three, d_gate_pre], 1)
    d_normed = right_product(d_joined, w_joined) + lax.dot_general(
        d_rate_pre, w_rate, (((0,), (1,)), ((), ())), precision=lax.Precision.HIGH,
        preferred_element_type=f32,
    )
    d_normed = meet_one(d_normed, *d_gate_y[0], *out_y[0])
    d_gain_one = jnp.sum(d_normed * tokens * r1, 0, keepdims=True)
    weighted = d_normed * gain_one
    d_tokens = r1 * weighted - tokens * (r1 * r1 * r1) * jnp.mean(
        tokens * weighted, -1, keepdims=True
    )

    own_three = Held(left_product(normed_pairs[0], both_cores(d_three)))
    weights = valid_mask.reshape(-1).astype(f32)[:, None]
    stats = jnp.stack(
        [
            jnp.sum(weights * member * member)
            for member in (stream_cols, attn, hidden, ffn, output)
        ]
        + [jnp.sum(weights) / lax.axis_size("heads")]
    )
    def rate_total():
        out = None
        for pair, d in zip(normed_pairs, d_rate_y.all()):
            part = product(jnp.concatenate([d, swap(d, "rows", 1)], 1), pair)
            out = part if out is None else out + part
        late["rate"] = Held(out)
        return late["rate"]

    hooks = [
        lambda: [own_three, *placed("g_gate", late["gate"].value, 1)],
        lambda: [
            total("attn", own_attn.value, normed_pairs, cores(d_gate_y.all())),
            *placed("g_up", late["up"].value, 1),
        ],
        lambda: [
            *d_three_y[0], *d_rate_y[0],
            *placed("g_down", sum(down_y.all()), 1),
        ],
        lambda: [
            total("three", own_three.value, normed_pairs, cores(d_three_y.all())),
            *placed("g_attn", late["attn"].value, 0),
            rate_total(),
        ],
    ]
    across_slabs = jnp.tile(jnp.pad(stats, (0, slab - stats.size)), width // slab)[None]
    d_part = scatter_columns(
        d_tokens,
        jnp.concatenate([d_gain_one, across_slabs, pad[1:]], 0),
        hooks,
    )
    d_stream = d_hidden + d_part[:length]
    d_gain_one = d_part[length]
    stats = d_part[length + 1, : stats.size]

    placed("g_out", sum(out_y.all()), 0)
    g_query, g_key, g_value = finish(late["three"].value, core, 0, (span,) * 3)
    ((g_gate,), (g_up,), (g_down,), (g_out,), (g_gate_attn,)) = (
        [item.value for item in late[name]]
        for name in ("g_gate", "g_up", "g_down", "g_out", "g_attn")
    )
    g_rate = late["rate"].value
    ends = (g_rate, swap(g_rate, "rows", 1))
    g_rate = jnp.where(core == 0, jnp.concatenate(ends, 1), jnp.concatenate(ends[::-1], 1))

    small = [
        d_gain_one, jnp.sum(d_rate_pre, 1), d_inner_weight, d_inner_bias, dg, dsh,
        d_post_gain, d_post_shift, d_gain_two, stats,
    ]
    packed = butterfly(jnp.concatenate([item.reshape(-1) for item in small]), "rows")
    parts = []
    at = 0
    for item in small:
        parts.append(packed[at : at + item.size])
        at += item.size
    stats = parts[9]
    rms_values = jnp.sqrt(stats[:5] / (stats[5] * width))
    return (
        output.reshape(1, length, slab),
        d_stream.reshape(1, length, slab),
        parts[0],
        g_query,
        g_key,
        g_value,
        g_rate.T,
        parts[1],
        parts[2].reshape(heads, hd, hd),
        parts[3].reshape(heads, hd),
        parts[4].reshape(heads, hd),
        parts[5].reshape(heads, hd),
        parts[6],
        parts[7],
        g_gate_attn,
        g_out,
        parts[8],
        g_gate.T,
        g_up.T,
        g_down,
        rms_values,
    )


def solution(mesh):
    in_specs = (
        P("rows", None, None),
        P("rows", None),
        P("rows", None),
        P("heads"),
        P(None, "heads"),
        P(None, "heads"),
        P(None, "heads"),
        P(None, "heads"),
        P("heads"),
        P("heads", None, None),
        P("heads", None),
        P("heads", None),
        P("heads", None),
        P("heads"),
        P("heads"),
        P(None, "heads"),
        P(None, "heads"),
        P("heads"),
        P(None, "heads"),
        P(None, "heads"),
        P("heads", None),
        P("rows", None, "heads"),
    )
    out_specs = (
        P("rows", None, "heads"),
        P("rows", None, "heads"),
        P("heads"),
        P(None, "heads"),
        P(None, "heads"),
        P(None, "heads"),
        P(None, "heads"),
        P("heads"),
        P("heads", None, None),
        P("heads", None),
        P("heads", None),
        P("heads", None),
        P("heads"),
        P("heads"),
        P(None, "heads"),
        P(None, "heads"),
        P("heads"),
        P(None, "heads"),
        P(None, "heads"),
        P("heads", None),
        P(),
    )
    return jax.shard_map(
        on_device, mesh=mesh, in_specs=in_specs, out_specs=out_specs, check_vma=False
    )
```

```python
import functools
import jax, jax.numpy as jnp
from jax import lax
from jax.experimental import pallas as pl
from jax.experimental.pallas import tpu as pltpu

from jax.sharding import PartitionSpec as P

MB = 16
CH = 128
epsilon = 1e-06
f32 = jnp.float32
bf16 = jnp.bfloat16
NN = ((1,), (0,))


def split(x):
    hi = x.astype(bf16)
    return hi, (x - hi.astype(f32)).astype(bf16)


def mm(a, b, dims=NN):
    def one(p, q):
        return lax.dot_general(p, q, (dims, ((), ())), preferred_element_type=f32)

    return one(a[0], b[0]) + (one(a[0], b[1]) + one(a[1], b[0]))


def wide(x):
    hi, lo = split(x)
    return jnp.concatenate([hi, lo], axis=1)


def tall_dot(x, pair):
    rows = x.shape[0]
    cols = pair.shape[1] // 2
    hi, lo = split(x)
    out = lax.dot_general(
        jnp.concatenate([hi, lo], axis=0), pair, (NN, ((), ())), preferred_element_type=f32
    )
    top, low = out[:rows], out[rows:]
    return top[:, :cols] + (top[:, cols:] + low[:, :cols])


def iota(shape, dim):
    return lax.broadcasted_iota(jnp.int32, shape, dim)


def head_sum(x, hd):
    rows, cols = x.shape
    parts = [
        jnp.broadcast_to(jnp.sum(x[i : i + hd], axis=0, keepdims=True), (hd, cols))
        for i in range(0, rows, hd)
    ]
    return parts[0] if len(parts) == 1 else jnp.concatenate(parts, axis=0)


def lane_sum(x):
    return jnp.sum(x, axis=1, keepdims=True)


def coefficients(transposed):
    source = iota((CH, CH), 1 if transposed else 0)
    target = iota((CH, CH), 0 if transposed else 1)
    before = (source // MB < target // MB).astype(f32) * (1.0 / MB)
    inside = ((source // MB == target // MB) & (source <= target)).astype(f32)
    return before, before + inside / ((target % MB) + 1).astype(f32)


def forward_body(
    joined, rate, rate_t, seg, seg_t, w0, b0, gain, shift, mixed, z_out, zb_out, w_out, b_out,
    w_s, b_s, z_s, tau_s, a_s, m_s, *, hd, heads,
):
    pairs = heads * hd // CH
    per = CH // hd
    span = heads * hd
    chunks = joined.shape[0] // CH
    n_inv = 1.0 / hd
    row_head = iota((CH, CH), 0) // hd
    lane_head = iota((CH, CH), 1) // hd
    lane_block = iota((hd, CH), 1) // MB
    block_diag = row_head == lane_head
    w_s[...] = jnp.zeros_like(w_s)
    b_s[...] = jnp.zeros_like(b_s)

    def chunk(c, carry):
        ts = pl.multiple_of(c * CH, CH)
        here = pl.ds(ts, CH)
        seg_row = seg_t[:, here]
        seg_col = seg[here, :]
        last_seg = seg_row[:, CH - 1 : CH]
        prev = jnp.max(jnp.where(iota(seg_t.shape, 1) < ts, seg_t[...], 0.0), keepdims=True)
        carried = seg_row == prev
        in_last = (seg_row == last_seg).astype(f32)
        whole = last_seg == prev
        same = seg_col == seg_row
        before, within = coefficients(False)
        before = jnp.where(same, before, 0.0)
        within = jnp.where(same, within, 0.0)
        for p in range(pairs):
            rows = slice(p * CH, (p + 1) * CH)
            kn = joined[here, span + p * CH : span + (p + 1) * CH]
            qn = joined[here, p * CH : (p + 1) * CH]
            vn = joined[here, 2 * span + p * CH : 2 * span + (p + 1) * CH]
            k_t, q_t, v_t = kn.T, qn.T, vn.T
            ks, kts, qts = split(kn), split(k_t), split(q_t)
            ws, w0s = split(w_s[rows]), split(w0[rows])
            bias = jnp.where(carried, b_s[rows], b0[rows])
            z_s[rows] = jnp.where(carried, mm(ws, kts), mm(w0s, kts)) + bias
            zb_out[rows, here] = jnp.where(carried, mm(ws, qts), mm(w0s, qts)) + bias
            w_out[c, rows] = w_s[rows]
            b_out[c, rows] = b_s[rows]
            tau_s[rows] = gain[rows] * (shift[rows] - v_t + k_t)
            for hh in range(per):
                h = p * per + hh
                own = (row_head == hh).astype(bf16)
                r_col = rate[here, h : h + 1]
                score = mm(ks, (kts[0] * own, kts[1] * own))
                a_s[h] = wide((score + 1.0) * (before * r_col))
                score = mm(ks, (qts[0] * own, qts[1] * own))
                m_s[h] = wide((score + 1.0) * (within * r_col))

        gsq = [jnp.broadcast_to(gain[h * hd : (h + 1) * hd] ** 2, (hd, CH)) for h in range(heads)]
        tsum = [
            jnp.sum(tau_s[h * hd : (h + 1) * hd], axis=0, keepdims=True) * n_inv
            for h in range(heads)
        ]

        def inner(h, z):
            tau = tau_s[h * hd : (h + 1) * hd]
            zg = z * gsq[h]
            m2 = jnp.sum(z * z, axis=0, keepdims=True) * n_inv
            a1 = jnp.sum(zg, axis=0, keepdims=True) * n_inv
            a2 = jnp.sum(z * zg, axis=0, keepdims=True) * n_inv
            a3 = jnp.sum(z * tau, axis=0, keepdims=True) * n_inv
            s = lax.rsqrt(m2 + epsilon)
            c_eu = s * (s * a2 + a3)
            e_mean = s * a1 + tsum[h]
            return (s * s) * (zg - c_eu * z) + s * (tau - e_mean)

        def step(t, zs):
            now = lane_block == t
            new = []
            for h in range(heads):
                g = jnp.where(now, inner(h, zs[h]), 0.0)
                new.append(zs[h] - tall_dot(g, a_s[h]))
            return tuple(new)

        zs = tuple(z_s[h * hd : (h + 1) * hd] for h in range(heads))
        zs = lax.fori_loop(0, CH // MB - 1, step, zs)
        for p in range(pairs):
            rows = slice(p * CH, (p + 1) * CH)
            gs = []
            outs = []
            for hh in range(per):
                h = p * per + hh
                hr = slice(h * hd, (h + 1) * hd)
                z_out[hr, here] = zs[h]
                g = inner(h, zs[h])
                zb = zb_out[hr, here] - tall_dot(g, m_s[h])
                zb_out[hr, here] = zb
                sb = lax.rsqrt(jnp.sum(zb * zb, axis=0, keepdims=True) * n_inv + epsilon)
                outs.append(zb * sb * gain[hr] + shift[hr])
                gs.append(g * (rate_t[h : h + 1, here] * in_last * (1.0 / MB)))
            gw = jnp.concatenate(gs, axis=0)
            lanes = slice(p * CH, (p + 1) * CH)
            mixed[here, lanes] = joined[here, lanes] + jnp.concatenate(outs, axis=0).T
            kn = joined[here, span + p * CH : span + (p + 1) * CH]
            upd = mm(split(gw), split(kn))
            w_s[rows] = jnp.where(whole, w_s[rows], w0[rows]) - jnp.where(block_diag, upd, 0.0)
            b_s[rows] = jnp.where(whole, b_s[rows], b0[rows]) - lane_sum(gw)
        return carry

    lax.fori_loop(0, chunks, chunk, 0)


def ttt_forward(joined, rate, rate_t, seg, seg_t, w0, b0, gain, shift, hd, heads):
    length = joined.shape[0]
    span = heads * hd
    chunks = length // CH
    shape = jax.ShapeDtypeStruct
    return pl.pallas_call(
        functools.partial(forward_body, hd=hd, heads=heads),
        out_shape=(
            shape((length, span), f32),
            shape((span, length), f32),
            shape((span, length), f32),
            shape((chunks, span, CH), f32),
            shape((chunks, span, 1), f32),
        ),
        scratch_shapes=[
            pltpu.VMEM((span, CH), f32),
            pltpu.VMEM((span, 1), f32),
            pltpu.VMEM((span, CH), f32),
            pltpu.VMEM((span, CH), f32),
            pltpu.VMEM((heads, CH, 2 * CH), bf16),
            pltpu.VMEM((heads, CH, 2 * CH), bf16),
        ],
        compiler_params=pltpu.CompilerParams(vmem_limit_bytes=48 << 20),
        name="inner_forward",
    )(joined, rate, rate_t, seg, seg_t, w0, b0, gain, shift)


def backward_body(
    joined, rate_t, seg, seg_t, w0, b0, gain, shift, z_in, zb_in, w_in, b_in, dy,
    dq_out, dk_out, dv_out, dr_out, dw_out, db_out, dg_out, dsh_out,
    dw_s, db_s, p_s, u_s, f_s, bb_s, e2_s, u2_s, gt_s, dzb_s, at_s, sc_s,
    *, hd, heads,
):
    pairs = heads * hd // CH
    per = CH // hd
    span = heads * hd
    chunks = joined.shape[0] // CH
    n_inv = 1.0 / hd
    row_head = iota((CH, CH), 0) // hd
    lane_head = iota((CH, CH), 1) // hd
    lane_block = iota((hd, CH), 1) // MB
    block_diag = row_head == lane_head
    for ref in (dw_s, db_s, dw_out, db_out, dg_out, dsh_out):
        ref[...] = jnp.zeros_like(ref)

    def mean(x):
        return head_sum(x, hd) * n_inv

    def chunk(index, carry):
        c = chunks - 1 - index
        ts = pl.multiple_of(c * CH, CH)
        here = pl.ds(ts, CH)
        seg_row = seg_t[:, here]
        seg_col = seg[here, :]
        last_seg = seg_row[:, CH - 1 : CH]
        prev = jnp.max(jnp.where(iota(seg_t.shape, 1) < ts, seg_t[...], 0.0), keepdims=True)
        carried = seg_row == prev
        carried_col = seg_col == prev
        in_last = (seg_row == last_seg).astype(f32)
        whole = last_seg == prev
        same = seg_col == seg_row
        before, within = coefficients(True)
        before = jnp.where(same, before, 0.0)
        within = jnp.where(same, within, 0.0)
        consts = {}
        for p in range(pairs):
            rows = slice(p * CH, (p + 1) * CH)
            lanes = slice(p * CH, (p + 1) * CH)
            qn = joined[here, p * CH : (p + 1) * CH]
            kn = joined[here, span + p * CH : span + (p + 1) * CH]
            vn = joined[here, 2 * span + p * CH : 2 * span + (p + 1) * CH]
            k_t, v_t, dy_t = kn.T, vn.T, dy[here, lanes].T
            qs, ks, kts = split(qn), split(kn), split(k_t)
            g_col = gain[rows]
            gsq = g_col * g_col
            zb = zb_in[rows, here]
            sb = lax.rsqrt(mean(zb * zb) + epsilon)
            ub = zb * sb
            dg_out[rows] += lane_sum(dy_t * ub)
            dsh_out[rows] += lane_sum(dy_t)
            pb = dy_t * g_col
            dzb = sb * (pb - mean(pb) - ub * mean(pb * ub))
            dzb_s[rows] = dzb
            z = z_in[rows, here]
            s = lax.rsqrt(mean(z * z) + epsilon)
            u = z * s
            gu = gsq * u
            e = gu + g_col * (shift[rows] - v_t + k_t)
            c_eu = mean(e * u)
            g_t = s * (e - mean(e) - u * c_eu)
            gt_s[rows] = g_t
            u_s[rows] = u
            f_s[rows] = g_t + s * gu
            bb_s[rows] = (s * s) * (gsq - c_eu)
            e2_s[rows] = (s * s) * (e + gu)
            u2_s[rows] = s * u
            h1 = s * mean(gu)
            h2 = 2.0 * s * c_eu + s * mean(gu * u)
            dzbs = split(dzb)
            gts = split(g_t)
            dzbn = split(dzb.T)
            from_state = mm(split(dw_s[rows]), kts) + db_s[rows]
            pieces = []
            dq = dy[here, lanes]
            dk = jnp.zeros((CH, CH), f32)
            for hh in range(per):
                h = p * per + hh
                hr = slice(hh * hd, (hh + 1) * hd)
                r_row = rate_t[h : h + 1, here]
                consts[h] = (h1[hh * hd : hh * hd + 1], h2[hh * hd : hh * hd + 1])
                own = (row_head == hh).astype(bf16)
                own_lane = (lane_head == hh).astype(bf16)
                kt_h = (kts[0] * own, kts[1] * own)
                sc = (mm(ks, kt_h) + 1.0) * before
                sc_s[h] = sc
                at_s[h] = wide(sc * r_row)
                scq = (mm(qs, kt_h) + 1.0) * within
                pt = mm(dzbn, (gts[0] * own, gts[1] * own))
                dr_out[h : h + 1, here] = -jnp.sum(pt * scq, axis=0, keepdims=True) - (
                    (1.0 / MB) * in_last
                ) * jnp.sum(g_t[hr] * from_state[hr], axis=0, keepdims=True)
                pm = pt * (within * r_row)
                pms = split(pm)
                pmts = split(pm.T)
                kn_h = (ks[0] * own_lane, ks[1] * own_lane)
                qn_h = (qs[0] * own_lane, qs[1] * own_lane)
                dq = dq - mm(pms, kn_h)
                dk = dk - mm(pmts, qn_h)
                pieces.append(
                    -mm((dzbs[0][hr], dzbs[1][hr]), split(scq * r_row))
                    - from_state[hr] * (r_row * in_last * (1.0 / MB))
                )
            p_s[rows] = jnp.concatenate(pieces, axis=0)
            w0s = split(w0[rows])
            wd = split(w_in[c, rows] - w0[rows])
            zero = jnp.zeros((), bf16)
            dzbn_c = (jnp.where(carried_col, dzbn[0], zero), jnp.where(carried_col, dzbn[1], zero))
            dq_out[here, lanes] = dq + mm(dzbn, w0s) + mm(dzbn_c, wd)
            dk_out[here, lanes] = dk

        def upstream(h, pv):
            hr = slice(h * hd, (h + 1) * hd)
            h1, h2 = consts[h]
            pm = jnp.sum(pv, axis=0, keepdims=True) * n_inv
            q = jnp.sum(pv * u_s[hr], axis=0, keepdims=True) * n_inv
            kf = jnp.sum(pv * f_s[hr], axis=0, keepdims=True) * n_inv
            kappa = kf - h1 * pm - h2 * q
            dz = (pv - pm) * bb_s[hr] - q * e2_s[hr] - kappa * u2_s[hr]
            return dz, pm, q

        def step(index, ps):
            now = lane_block == (CH // MB - 1 - index)
            new = []
            for h in range(heads):
                dz = jnp.where(now, upstream(h, ps[h])[0], 0.0)
                new.append(ps[h] - tall_dot(dz, at_s[h]))
            return tuple(new)

        ps = tuple(p_s[h * hd : (h + 1) * hd] for h in range(heads))
        ps = lax.fori_loop(0, CH // MB - 1, step, ps)

        for p in range(pairs):
            rows = slice(p * CH, (p + 1) * CH)
            lanes = slice(p * CH, (p + 1) * CH)
            qn = joined[here, p * CH : (p + 1) * CH]
            kn = joined[here, span + p * CH : span + (p + 1) * CH]
            vn = joined[here, 2 * span + p * CH : 2 * span + (p + 1) * CH]
            qs, ks = split(qn), split(kn)
            g_t = gt_s[rows]
            gts = split(g_t)
            dzs, des = [], []
            for hh in range(per):
                h = p * per + hh
                hr = slice(h * hd, (h + 1) * hd)
                dz, pm, q = upstream(h, ps[h])
                dzs.append(dz - jnp.sum(dz, axis=0, keepdims=True) * n_inv)
                z = z_in[hr, here]
                s = lax.rsqrt(jnp.sum(z * z, axis=0, keepdims=True) * n_inv + epsilon)
                des.append(s * (ps[h] - pm - u_s[hr] * q))
            dz = jnp.concatenate(dzs, axis=0)
            de = jnp.concatenate(des, axis=0)
            g_col = gain[rows]
            gde = g_col * de
            t_t = shift[rows] + (kn - vn).T
            dg_out[rows] += lane_sum((2.0 * g_col * u_s[rows] + t_t) * de)
            dsh_out[rows] += lane_sum(gde)
            gden = gde.T
            dv_out[here, lanes] = -gden
            dzn = split(dz.T)
            dk = dk_out[here, lanes] + gden
            r_rows = []
            for hh in range(per):
                h = p * per + hh
                r_row = rate_t[h : h + 1, here]
                own = (row_head == hh).astype(bf16)
                own_lane = (lane_head == hh).astype(bf16)
                rt = mm(dzn, (gts[0] * own, gts[1] * own))
                dr_out[h : h + 1, here] -= jnp.sum(rt * sc_s[h], axis=0, keepdims=True)
                ra = rt * (before * r_row)
                dk = dk - mm(split(ra + ra.T), (ks[0] * own_lane, ks[1] * own_lane))
                r_rows.append(jnp.broadcast_to(r_row * in_last * (1.0 / MB), (hd, CH)))
            gw = g_t * jnp.concatenate(r_rows, axis=0)
            w0s = split(w0[rows])
            wd = split(w_in[c, rows] - w0[rows])
            zero = jnp.zeros((), bf16)
            dzn_c = (jnp.where(carried_col, dzn[0], zero), jnp.where(carried_col, dzn[1], zero))
            dk = dk + mm(dzn, w0s) + mm(dzn_c, wd) - mm(split(gw.T), split(dw_s[rows]))
            dk_out[here, lanes] = dk
            dzb = dzb_s[rows]
            dzc = jnp.where(carried, dz, 0.0)
            dzbc = jnp.where(carried, dzb, 0.0)
            diag = jnp.where(block_diag, mm(split(dzc), ks) + mm(split(dzbc), qs), 0.0)
            rest = jnp.where(
                block_diag, mm(split(dz - dzc), ks) + mm(split(dzb - dzbc), qs), 0.0
            )
            dw = dw_s[rows]
            db = db_s[rows]
            dw_out[rows] += jnp.where(whole, 0.0, dw) + rest
            db_out[rows] += jnp.where(whole, 0.0, db) + lane_sum(dz - dzc + dzb - dzbc)
            dw_s[rows] = jnp.where(whole, dw, 0.0) + diag
            db_s[rows] = jnp.where(whole, db, 0.0) + lane_sum(dzc + dzbc)
        return carry

    lax.fori_loop(0, chunks, chunk, 0)


def ttt_backward(joined, rate_t, seg, seg_t, w0, b0, gain, shift, saved, dy, hd, heads):
    length = joined.shape[0]
    span = heads * hd
    shape = jax.ShapeDtypeStruct
    return pl.pallas_call(
        functools.partial(backward_body, hd=hd, heads=heads),
        out_shape=(
            shape((length, span), f32),
            shape((length, span), f32),
            shape((length, span), f32),
            shape((heads, length), f32),
            shape((span, CH), f32),
            shape((span, 1), f32),
            shape((span, 1), f32),
            shape((span, 1), f32),
        ),
        scratch_shapes=[
            pltpu.VMEM((span, CH), f32),
            pltpu.VMEM((span, 1), f32),
        ]
        + [pltpu.VMEM((span, CH), f32)] * 8
        + [
            pltpu.VMEM((heads, CH, 2 * CH), bf16),
            pltpu.VMEM((heads, CH, CH), f32),
        ],
        compiler_params=pltpu.CompilerParams(vmem_limit_bytes=48 << 20),
        name="inner_backward",
    )(joined, rate_t, seg, seg_t, w0, b0, gain, shift, *saved, dy)


def state_in(inner_weight, inner_bias):
    heads, hd, _ = inner_weight.shape
    per = CH // hd
    w_t = jnp.swapaxes(inner_weight, 1, 2)
    w_t = w_t - jnp.mean(w_t, axis=1, keepdims=True)
    placed = [
        jnp.pad(w_t[h], ((0, 0), ((h % per) * hd, CH - hd - (h % per) * hd)))
        for h in range(heads)
    ]
    b = inner_bias - jnp.mean(inner_bias, axis=1, keepdims=True)
    return jnp.concatenate(placed, axis=0), b.reshape(heads * hd, 1)


def state_back(dw, db, heads, hd):
    per = CH // hd
    parts = [
        dw[h * hd : (h + 1) * hd, (h % per) * hd : (h % per + 1) * hd] for h in range(heads)
    ]
    d = jnp.stack(parts)
    d = jnp.swapaxes(d - jnp.mean(d, axis=1, keepdims=True), 1, 2)
    b = db.reshape(heads, hd)
    return d, b - jnp.mean(b, axis=1, keepdims=True)


def product(left, right):
    return jnp.dot(left, right, precision=lax.Precision.HIGH, preferred_element_type=f32)


def left_product(left, right):
    return lax.dot_general(
        left, right, (((0,), (0,)), ((), ())), precision=lax.Precision.HIGH,
        preferred_element_type=f32,
    )


def right_product(left, right):
    return lax.dot_general(
        left, right, (((1,), (1,)), ((), ())), precision=lax.Precision.HIGH,
        preferred_element_type=f32,
    )


def heads_grid():
    size = lax.axis_size("heads")
    deep = 4 if size % 4 == 0 else 1
    return deep, size // deep


def heads_place():
    _, across = heads_grid()
    index = lax.axis_index("heads")
    return index // across, index % across


def shift(value, dz, dx):
    deep, across = heads_grid()
    pairs = [
        (h, (h // across + dz) % deep * across + (h % across + dx) % across)
        for h in range(deep * across)
    ]
    return lax.ppermute(value, "heads", pairs)


def swap(value, axis, bit):
    return lax.ppermute(value, axis, [(i, i ^ bit) for i in range(lax.axis_size(axis))])


def row_shift(value, step):
    size = lax.axis_size("rows")
    return lax.ppermute(value, "rows", [(r, (r + 2 * step) % size) for r in range(size)])


def butterfly(value, axis, hooks=()):
    size = lax.axis_size(axis)
    bits = [1 << i for i in range(size.bit_length() - 1)][::-1]
    for index, bit in enumerate(bits):
        (other,) = meet([swap(value, axis, bit)], turn(hooks, index))
        value = value + other
    return value


def small_gather(value, hooks=()):
    size = lax.axis_size("heads")
    place = jnp.arange(size) == lax.axis_index("heads")
    place = place.reshape((size,) + (1,) * value.ndim)
    return butterfly(jnp.where(place, value[None], 0.0), "heads", hooks)


class Held:
    def __init__(self, value):
        self.value = value


def meet(values, held=()):
    out = lax.optimization_barrier(tuple(values) + tuple(item.value for item in held))
    for item, value in zip(held, out[len(values) :]):
        item.value = value
    return list(out[: len(values)])


def meet_one(value, *held):
    return meet([value], held)[0]


def turn(hooks, index):
    hook = hooks[index] if index < len(hooks) else ()
    return hook() if callable(hook) else hook


def gather_columns(value, hooks=()):
    deep, across = heads_grid()
    z, x = heads_place()
    rows, cols = value.shape
    out = jnp.zeros((rows, cols * deep * across), value.dtype)
    here, ready = value, [(0, 0, value)]
    for dz in range(deep):
        moved = [shift(here, 0, dx) for dx in range(1, across)]
        if dz + 1 < deep:
            moved.append(shift(here, 1, 0))
        for oz, ox, item in ready:
            column = ((z - oz) % deep * across + (x - ox) % across) * cols
            out = lax.dynamic_update_slice(out, item, (0, column))
        *moved, out = meet(moved + [out], turn(hooks, dz))
        ready = [(dz, dx, moved[dx - 1]) for dx in range(1, across)]
        if dz + 1 < deep:
            here = moved[-1]
            ready.append((dz + 1, 0, here))
    for oz, ox, item in ready:
        column = ((z - oz) % deep * across + (x - ox) % across) * cols
        out = lax.dynamic_update_slice(out, item, (0, column))
    return out


def scatter_columns(value, extra=None, hooks=()):
    deep, across = heads_grid()
    z, x = heads_place()
    rows, width = value.shape
    cols = width // (deep * across)

    def piece(dz, dx):
        column = ((z - dz) % deep * across + (x - dx) % across) * cols
        block = lax.dynamic_slice(value, (0, column), (rows, cols))
        if extra is not None:
            tail = lax.dynamic_slice(extra, (0, column), (extra.shape[0], cols))
            block = jnp.concatenate([block, tail], 0)
        return block

    total = None
    for index, dz in enumerate(list(range(1, deep)) + [0]):
        moved = [shift(piece(dz, dx), 0, dx) for dx in range(1, across)]
        if total is not None:
            moved.append(shift(total, 1, 0))
        total = piece(dz, 0)
        for item in meet(moved, turn(hooks, index)):
            total = total + item
    return total


def half_of(value, index, axis):
    size = value.shape[axis] // 2
    return lax.dynamic_slice_in_dim(value, index * size, size, axis)


def both_cores(value):
    return jnp.concatenate([value, swap(value, "rows", 1)], 0)


def tokens_half(value, core):
    return jnp.concatenate(
        [half_of(value, core, 1), swap(half_of(value, 1 - core, 1), "rows", 1)], 0
    )


def chips_along():
    return lax.axis_size("rows") // 2


def other_chips(value):
    return [row_shift(value, step) for step in range(1, chips_along())]


def place_body(core, own, other, *outs, axis, widths):
    first = core[0] == 0
    at = 0
    for out, width in zip(outs, widths):
        mine, its = (own[:, at : at + width], other[:, at : at + width]) if axis == 0 else (own[...], other[...])
        low = jnp.where(first, mine, its)
        high = jnp.where(first, its, mine)
        if axis == 0:
            out[0] = low
            out[1] = high
        else:
            out[:, : low.shape[1]] = low
            out[:, low.shape[1] :] = high
        at += width


def place(own, other, core, axis, widths):
    rows, cols = own.shape
    steps = max(n for n in (1, 2, 4) if rows % (8 * n) == 0)
    size = rows // steps
    part = pl.BlockSpec((size, cols), lambda i: (i, 0))
    if axis == 0:
        shapes = [(2, rows, width) for width in widths]
        specs = [pl.BlockSpec((2, size, width), lambda i: (0, i, 0)) for width in widths]
    else:
        shapes = [(rows, 2 * cols)]
        specs = [pl.BlockSpec((size, 2 * cols), lambda i: (i, 0))]
    out = pl.pallas_call(
        functools.partial(place_body, axis=axis, widths=widths),
        grid=(steps,),
        out_shape=[jax.ShapeDtypeStruct(shape, f32) for shape in shapes],
        in_specs=[pl.BlockSpec(memory_space=pltpu.SMEM), part, part],
        out_specs=specs,
        compiler_params=pltpu.CompilerParams(vmem_limit_bytes=48 << 20),
        name="place",
    )(core.reshape(1).astype(jnp.int32), own, other)
    return [o.reshape(2 * rows, -1) if axis == 0 else o for o in out]


def finish(total, core, axis, widths=None):
    widths = (total.shape[1],) if widths is None else widths
    return place(total, swap(total, "rows", 1), core, axis, widths)


def row_products(lefts, rights):
    total = None
    for left, right in zip(lefts, rights):
        part = left_product(left, right)
        total = part if total is None else total + part
    return total


class Along:
    def __init__(self, value, parts=4, axis=0):
        self.own = value
        self.axis = axis
        pieces = jnp.split(value, parts, axis)
        self.steps = [
            [Held(row_shift(piece, step)) for piece in pieces] for step in range(1, chips_along())
        ]

    def __getitem__(self, i):
        return [step[i] for step in self.steps]

    def all(self):
        return [self.own] + [
            step[0].value if len(step) == 1
            else jnp.concatenate([item.value for item in step], self.axis)
            for step in self.steps
        ]


def silu_parts(a):
    sig = jax.nn.sigmoid(a)
    return a * sig, sig * (1.0 + a * (1.0 - sig))


def gelu_parts(v):
    k = 0.7978845608028654
    inner = k * (v + 0.044715 * v * v * v)
    th = jnp.tanh(inner)
    slope = 0.5 * (1.0 + th) + 0.5 * v * (1.0 - th * th) * k * (1.0 + 3 * 0.044715 * v * v)
    return 0.5 * v * (1.0 + th), slope


def on_device(
    stream,
    doc_starts,
    valid_mask,
    first_gain,
    w_query,
    w_key,
    w_value,
    w_rate,
    b_rate,
    inner_weight,
    inner_bias,
    inner_gain,
    inner_shift,
    post_gain,
    post_shift,
    w_gate_attn,
    w_out,
    second_gain,
    w_gate,
    w_up,
    w_down,
    cotangent,
):
    _, length, width = stream.shape
    tokens = stream.reshape(length, width)
    slab = second_gain.shape[0]
    column = lax.axis_index("heads") * slab
    core = lax.axis_index("rows") % 2
    heads, hd = inner_bias.shape
    span = heads * hd
    total_span = span * lax.axis_size("heads")
    grad_output = cotangent.reshape(length, slab)
    early = {}

    def first():
        early["r1"] = Held(lax.rsqrt(jnp.mean(tokens * tokens, -1, keepdims=True) + epsilon))
        return [early["r1"]]

    def second():
        early["unit"] = Held(tokens * early["r1"].value)
        return [early["unit"]]

    def third():
        early["pair"] = Held(half_of(early["unit"].value, core, 1))
        return [early["pair"]]

    gains = small_gather(jnp.stack([first_gain, second_gain]), [first, second, third])
    gain_one = gains[:, 0].reshape(width)
    gain_two = gains[:, 1].reshape(width)
    r1, unit = early["r1"].value, early["unit"].value
    dy_in, gain_one = lax.optimization_barrier((grad_output, gain_one))
    unit_y = Along(
        jnp.concatenate(
            [early["pair"].value, swap(half_of(unit, 1 - core, 1), "rows", 1)], 0
        )
    )
    w_joined = jnp.concatenate([w_query, w_key, w_value, w_gate_attn], axis=1)
    normed = unit * gain_one
    joined = product(normed, w_joined)
    rate_pre = lax.dot_general(
        w_rate, normed, (((0,), (1,)), ((), ())), precision=lax.Precision.HIGH,
        preferred_element_type=f32,
    )
    joined = Held(joined)
    after = {}

    def run_inner():
        after["mixed"] = [
            Held(item) for item in ttt_forward(
                joined.value, rate, rate_t, seg, seg_t, w0, b0, gain_col, shift_col, hd, heads
            )
        ]
        return [*after["mixed"], *unit_y[1]]

    sig = jax.nn.sigmoid(rate_pre + b_rate[:, None])
    rate_t = sig / hd
    rate = rate_t.T
    seg = jnp.cumsum(doc_starts.reshape(length)).astype(f32)
    seg, seg_t = seg[:, None], seg[None]
    w0, b0 = state_in(inner_weight, inner_bias)
    gain_col, shift_col = inner_gain.reshape(span, 1), inner_shift.reshape(span, 1)
    dy_held = Held(gather_columns(dy_in, [[], [joined, *unit_y[0]], run_inner]))
    joined = joined.value
    gate_pre = joined[:, 3 * span :]
    mixed, *saved = [item.value for item in after["mixed"]]
    row_sums = butterfly(jnp.stack([jnp.sum(mixed, 1), jnp.sum(mixed * mixed, 1)]), "heads")
    row_sums = meet_one(row_sums, *unit_y[2], dy_held)
    row_mean = row_sums[0] / total_span
    inv_std = lax.rsqrt(row_sums[1] / total_span - row_mean * row_mean + epsilon)[:, None]
    centered = (mixed - row_mean[:, None]) * inv_std
    shaped = centered * post_gain + post_shift
    gate_act, gate_slope = gelu_parts(gate_pre)
    gathered = gather_columns(gate_act * shaped, [(), unit_y[3]])
    gathered_pair = tokens_half(gathered, core)
    attn = product(gathered, w_out)
    stream_cols = lax.dynamic_slice_in_dim(tokens, column, slab, 1)
    hidden = stream_cols + attn
    whole = gather_columns(hidden)
    dy_full = dy_held.value

    r2 = lax.rsqrt(jnp.mean(whole * whole, -1, keepdims=True) + epsilon)
    hnorm = whole * r2 * gain_two
    hnorm_y = Along(tokens_half(hnorm, core), 8)
    a = product(hnorm, w_gate)
    c = product(hnorm, w_up)
    act, slope = silu_parts(a)
    m = act * c
    ffn_part = product(m, w_down)
    deep, across = heads_grid()
    z, x = heads_place()

    dy_full, ffn_part = meet([dy_full, ffn_part], hnorm_y[0])

    def ffn_piece(dz, dx):
        place_of = (z - dz) % deep * across + (x - dx) % across
        return lax.dynamic_slice_in_dim(ffn_part, place_of * slab, slab, 1)

    def ffn_across(dz):
        return [Held(shift(ffn_piece(dz, dx), 0, dx)) for dx in range(1, across)]

    soon = [dz for dz in (1, 2) if dz < deep]
    ffn_x = {dz: ffn_across(dz) for dz in soon}
    soon_x = [item for dz in soon for item in ffn_x[dz]]
    dm = right_product(dy_full, w_down)
    da = meet_one(dm * c * slope, *hnorm_y[1])
    dc = dm * act
    da_y, dc_y = Along(da, 2), Along(dc, 2)
    dhnorm = meet_one(right_product(da, w_gate), *soon_x, *hnorm_y[2], *hnorm_y[3])
    dhnorm = dhnorm + right_product(dc, w_up)
    dhnorm = meet_one(dhnorm, *hnorm_y[4])

    def ffn_tile(dz):
        out = ffn_piece(dz, 0)
        for item in ffn_x[dz]:
            out = out + item.value
        return out

    ffn_steps = []

    def ffn_step(dz):
        ffn_steps.append(Held(shift(ffn_steps[-1].value + ffn_tile(dz) if ffn_steps else ffn_tile(dz), 1, 0)))
        return ffn_steps[-1]

    d_gain_two = jnp.sum(dhnorm * whole * r2, 0, keepdims=True)
    weighted = dhnorm * gain_two
    d_whole = r2 * weighted - whole * (r2 * r2 * r2) * jnp.mean(
        whole * weighted, -1, keepdims=True
    )
    pad = jnp.zeros((7, width), f32)
    da_pair, dc_pair = both_cores(da), both_cores(dc)
    own_gate = Held(left_product(da_pair, hnorm_y.own))
    own_up = Held(left_product(dc_pair, hnorm_y.own))
    own_down = Held(left_product(both_cores(m), tokens_half(dy_full, core)))
    d_part = scatter_columns(
        d_whole,
        jnp.concatenate([d_gain_two, pad], 0),
        [
            [*hnorm_y[5], *hnorm_y[6]],
            [*hnorm_y[7], *da_y[0], own_down],
            lambda: [*da_y[1], own_gate, *([ffn_step(1)] if deep > 1 else [])],
            [*dc_y[0], own_up],
        ],
    )
    d_hidden = grad_output + d_part[:length]
    d_gain_two = d_part[length]
    own_out = Held(left_product(gathered_pair, both_cores(d_hidden)))
    down_y = Along(own_down.value, 4, 1)
    late = {}

    def cores(values):
        return [both_cores(value) for value in values]

    def total(name, own, lefts, rights):
        for left, right in zip(lefts[1:], rights[1:]):
            own = own + left_product(left, right)
        late[name] = Held(own)
        return late[name]

    def placed(name, value, axis, widths=None):
        late[name] = [Held(item) for item in finish(value, core, axis, widths)]
        return late[name]

    d_gated = scatter_columns(
        right_product(d_hidden, w_out),
        None,
        [
            lambda: [*dc_y[1], *([ffn_step(2)] if deep > 2 else [])],
            [*down_y[0], own_out],
            lambda: [
                *down_y[1],
                total("gate", own_gate.value, cores(da_y.all()), hnorm_y.all()),
            ],
            lambda: [
                *down_y[2],
                total("up", own_up.value, cores(dc_y.all()), hnorm_y.all()),
            ],
        ],
    )
    out_y = Along(own_out.value, 1)
    d_shaped = d_gated * gate_act
    d_gate_pre = d_gated * shaped * gate_slope
    d_post_gain = jnp.sum(d_shaped * centered, 0)
    d_post_shift = jnp.sum(d_shaped, 0)
    d_center = d_shaped * post_gain
    gain_half = half_of(gain_one, core, 0)
    normed_pairs = [pair * gain_half for pair in unit_y.all()]
    d_gate_y = Along(d_gate_pre, 1)
    own_attn = Held(left_product(normed_pairs[0], both_cores(d_gate_pre)))
    back_sums = butterfly(
        jnp.stack([jnp.sum(d_center, 1), jnp.sum(d_center * centered, 1)]), "heads"
    )
    back_sums, ffn_part = meet([back_sums, ffn_part], ffn_steps[-1:])
    for dz in range(deep):
        if dz not in ffn_x:
            ffn_x[dz] = ffn_across(dz)
    for dz in range(3, deep):
        ffn_step(dz)
    ffn = Held((ffn_steps[-1].value if ffn_steps else 0.0) + ffn_tile(0))
    d_mixed = inv_std * (
        d_center - back_sums[0][:, None] / total_span
        - centered * back_sums[1][:, None] / total_span
    )
    dq, dk, dv, d_rate, dw, db, dg, dsh = ttt_backward(
        joined, rate_t, seg, seg_t, w0, b0, gain_col, shift_col, saved, d_mixed, hd, heads
    )
    dq = meet_one(dq, *down_y[3], own_attn)
    d_inner_weight, d_inner_bias = state_back(dw, db, heads, hd)
    d_rate_pre = d_rate * rate_t * (1.0 - sig)
    d_three = jnp.concatenate([dq, dk, dv], 1)
    d_three_y, d_rate_y = Along(d_three, 1), Along(d_rate_pre, 1)
    d_joined = jnp.concatenate([d_three, d_gate_pre], 1)
    d_normed = right_product(d_joined, w_joined) + lax.dot_general(
        d_rate_pre, w_rate, (((0,), (1,)), ((), ())), precision=lax.Precision.HIGH,
        preferred_element_type=f32,
    )
    d_normed = meet_one(d_normed, *d_gate_y[0], *out_y[0], ffn)
    ffn = ffn.value
    output = hidden + ffn
    d_gain_one = jnp.sum(d_normed * tokens * r1, 0, keepdims=True)
    weighted = d_normed * gain_one
    d_tokens = r1 * weighted - tokens * (r1 * r1 * r1) * jnp.mean(
        tokens * weighted, -1, keepdims=True
    )

    own_three = Held(left_product(normed_pairs[0], both_cores(d_three)))
    weights = valid_mask.reshape(-1).astype(f32)[:, None]
    stats = jnp.stack(
        [
            jnp.sum(weights * member * member)
            for member in (stream_cols, attn, hidden, ffn, output)
        ]
        + [jnp.sum(weights) / lax.axis_size("heads")]
    )
    def rate_total():
        out = None
        for pair, d in zip(normed_pairs, d_rate_y.all()):
            part = product(jnp.concatenate([d, swap(d, "rows", 1)], 1), pair)
            out = part if out is None else out + part
        late["rate"] = Held(out)
        return late["rate"]

    hooks = [
        lambda: [own_three, *placed("g_gate", late["gate"].value, 1)],
        lambda: [
            total("attn", own_attn.value, normed_pairs, cores(d_gate_y.all())),
            *placed("g_up", late["up"].value, 1),
        ],
        lambda: [
            *d_three_y[0],
            *placed("g_down", sum(down_y.all()), 1),
        ],
        lambda: [
            total("three", own_three.value, normed_pairs, cores(d_three_y.all())),
            *placed("g_attn", late["attn"].value, 0),
            *d_rate_y[0],
        ],
    ]
    across_slabs = jnp.tile(jnp.pad(stats, (0, slab - stats.size)), width // slab)[None]
    d_part = scatter_columns(
        d_tokens,
        jnp.concatenate([d_gain_one, across_slabs, pad[1:]], 0),
        hooks,
    )
    d_stream = d_hidden + d_part[:length]
    d_gain_one = d_part[length]
    stats = d_part[length + 1, : stats.size]

    placed("g_out", sum(out_y.all()), 0)
    g_query, g_key, g_value = finish(late["three"].value, core, 0, (span,) * 3)
    ((g_gate,), (g_up,), (g_down,), (g_out,), (g_gate_attn,)) = (
        [item.value for item in late[name]]
        for name in ("g_gate", "g_up", "g_down", "g_out", "g_attn")
    )
    g_rate = rate_total().value
    ends = (g_rate, swap(g_rate, "rows", 1))
    g_rate = jnp.where(core == 0, jnp.concatenate(ends, 1), jnp.concatenate(ends[::-1], 1))

    small = [
        d_gain_one, jnp.sum(d_rate_pre, 1), d_inner_weight, d_inner_bias, dg, dsh,
        d_post_gain, d_post_shift, d_gain_two, stats,
    ]
    packed = butterfly(jnp.concatenate([item.reshape(-1) for item in small]), "rows")
    parts = []
    at = 0
    for item in small:
        parts.append(packed[at : at + item.size])
        at += item.size
    stats = parts[9]
    rms_values = jnp.sqrt(stats[:5] / (stats[5] * width))
    return (
        output.reshape(1, length, slab),
        d_stream.reshape(1, length, slab),
        parts[0],
        g_query,
        g_key,
        g_value,
        g_rate.T,
        parts[1],
        parts[2].reshape(heads, hd, hd),
        parts[3].reshape(heads, hd),
        parts[4].reshape(heads, hd),
        parts[5].reshape(heads, hd),
        parts[6],
        parts[7],
        g_gate_attn,
        g_out,
        parts[8],
        g_gate.T,
        g_up.T,
        g_down,
        rms_values,
    )


def solution(mesh):
    in_specs = (
        P("rows", None, None),
        P("rows", None),
        P("rows", None),
        P("heads"),
        P(None, "heads"),
        P(None, "heads"),
        P(None, "heads"),
        P(None, "heads"),
        P("heads"),
        P("heads", None, None),
        P("heads", None),
        P("heads", None),
        P("heads", None),
        P("heads"),
        P("heads"),
        P(None, "heads"),
        P(None, "heads"),
        P("heads"),
        P(None, "heads"),
        P(None, "heads"),
        P("heads", None),
        P("rows", None, "heads"),
    )
    out_specs = (
        P("rows", None, "heads"),
        P("rows", None, "heads"),
        P("heads"),
        P(None, "heads"),
        P(None, "heads"),
        P(None, "heads"),
        P(None, "heads"),
        P("heads"),
        P("heads", None, None),
        P("heads", None),
        P("heads", None),
        P("heads", None),
        P("heads"),
        P("heads"),
        P(None, "heads"),
        P(None, "heads"),
        P("heads"),
        P(None, "heads"),
        P(None, "heads"),
        P("heads", None),
        P(),
    )
    return jax.shard_map(
        on_device, mesh=mesh, in_specs=in_specs, out_specs=out_specs, check_vma=False
    )
```

```python
import functools
import jax, jax.numpy as jnp
from jax import lax
from jax.experimental import pallas as pl
from jax.experimental.pallas import tpu as pltpu

from jax.sharding import PartitionSpec as P

MB = 16
CH = 128
epsilon = 1e-06
f32 = jnp.float32
bf16 = jnp.bfloat16
NN = ((1,), (0,))


def split(x):
    hi = x.astype(bf16)
    return hi, (x - hi.astype(f32)).astype(bf16)


def mm(a, b, dims=NN):
    def one(p, q):
        return lax.dot_general(p, q, (dims, ((), ())), preferred_element_type=f32)

    return one(a[0], b[0]) + (one(a[0], b[1]) + one(a[1], b[0]))


def wide(x):
    hi, lo = split(x)
    return jnp.concatenate([hi, lo], axis=1)


def tall_dot(x, pair):
    rows = x.shape[0]
    cols = pair.shape[1] // 2
    hi, lo = split(x)
    out = lax.dot_general(
        jnp.concatenate([hi, lo], axis=0), pair, (NN, ((), ())), preferred_element_type=f32
    )
    top, low = out[:rows], out[rows:]
    return top[:, :cols] + (top[:, cols:] + low[:, :cols])


def iota(shape, dim):
    return lax.broadcasted_iota(jnp.int32, shape, dim)


def head_sum(x, hd):
    rows, cols = x.shape
    parts = [
        jnp.broadcast_to(jnp.sum(x[i : i + hd], axis=0, keepdims=True), (hd, cols))
        for i in range(0, rows, hd)
    ]
    return parts[0] if len(parts) == 1 else jnp.concatenate(parts, axis=0)


def lane_sum(x):
    return jnp.sum(x, axis=1, keepdims=True)


def coefficients(transposed):
    source = iota((CH, CH), 1 if transposed else 0)
    target = iota((CH, CH), 0 if transposed else 1)
    before = (source // MB < target // MB).astype(f32) * (1.0 / MB)
    inside = ((source // MB == target // MB) & (source <= target)).astype(f32)
    return before, before + inside / ((target % MB) + 1).astype(f32)


def forward_body(
    joined, rate, rate_t, seg, seg_t, w0, b0, gain, shift, mixed, z_out, zb_out, w_out, b_out,
    w_s, b_s, z_s, tau_s, a_s, m_s, *, hd, heads,
):
    pairs = heads * hd // CH
    per = CH // hd
    span = heads * hd
    chunks = joined.shape[0] // CH
    n_inv = 1.0 / hd
    row_head = iota((CH, CH), 0) // hd
    lane_head = iota((CH, CH), 1) // hd
    lane_block = iota((hd, CH), 1) // MB
    block_diag = row_head == lane_head
    w_s[...] = jnp.zeros_like(w_s)
    b_s[...] = jnp.zeros_like(b_s)

    def chunk(c, carry):
        ts = pl.multiple_of(c * CH, CH)
        here = pl.ds(ts, CH)
        seg_row = seg_t[:, here]
        seg_col = seg[here, :]
        last_seg = seg_row[:, CH - 1 : CH]
        prev = jnp.max(jnp.where(iota(seg_t.shape, 1) < ts, seg_t[...], 0.0), keepdims=True)
        carried = seg_row == prev
        in_last = (seg_row == last_seg).astype(f32)
        whole = last_seg == prev
        same = seg_col == seg_row
        before, within = coefficients(False)
        before = jnp.where(same, before, 0.0)
        within = jnp.where(same, within, 0.0)
        for p in range(pairs):
            rows = slice(p * CH, (p + 1) * CH)
            kn = joined[here, span + p * CH : span + (p + 1) * CH]
            qn = joined[here, p * CH : (p + 1) * CH]
            vn = joined[here, 2 * span + p * CH : 2 * span + (p + 1) * CH]
            k_t, q_t, v_t = kn.T, qn.T, vn.T
            ks, kts, qts = split(kn), split(k_t), split(q_t)
            ws, w0s = split(w_s[rows]), split(w0[rows])
            bias = jnp.where(carried, b_s[rows], b0[rows])
            z_s[rows] = jnp.where(carried, mm(ws, kts), mm(w0s, kts)) + bias
            zb_out[rows, here] = jnp.where(carried, mm(ws, qts), mm(w0s, qts)) + bias
            w_out[c, rows] = w_s[rows]
            b_out[c, rows] = b_s[rows]
            tau_s[rows] = gain[rows] * (shift[rows] - v_t + k_t)
            for hh in range(per):
                h = p * per + hh
                own = (row_head == hh).astype(bf16)
                r_col = rate[here, h : h + 1]
                score = mm(ks, (kts[0] * own, kts[1] * own))
                a_s[h] = wide((score + 1.0) * (before * r_col))
                score = mm(ks, (qts[0] * own, qts[1] * own))
                m_s[h] = wide((score + 1.0) * (within * r_col))

        gsq = [jnp.broadcast_to(gain[h * hd : (h + 1) * hd] ** 2, (hd, CH)) for h in range(heads)]
        tsum = [
            jnp.sum(tau_s[h * hd : (h + 1) * hd], axis=0, keepdims=True) * n_inv
            for h in range(heads)
        ]

        def inner(h, z):
            tau = tau_s[h * hd : (h + 1) * hd]
            zg = z * gsq[h]
            m2 = jnp.sum(z * z, axis=0, keepdims=True) * n_inv
            a1 = jnp.sum(zg, axis=0, keepdims=True) * n_inv
            a2 = jnp.sum(z * zg, axis=0, keepdims=True) * n_inv
            a3 = jnp.sum(z * tau, axis=0, keepdims=True) * n_inv
            s = lax.rsqrt(m2 + epsilon)
            c_eu = s * (s * a2 + a3)
            e_mean = s * a1 + tsum[h]
            return (s * s) * (zg - c_eu * z) + s * (tau - e_mean)

        def step(t, zs):
            now = lane_block == t
            new = []
            for h in range(heads):
                g = jnp.where(now, inner(h, zs[h]), 0.0)
                new.append(zs[h] - tall_dot(g, a_s[h]))
            return tuple(new)

        zs = tuple(z_s[h * hd : (h + 1) * hd] for h in range(heads))
        zs = lax.fori_loop(0, CH // MB - 1, step, zs)
        for p in range(pairs):
            rows = slice(p * CH, (p + 1) * CH)
            gs = []
            outs = []
            for hh in range(per):
                h = p * per + hh
                hr = slice(h * hd, (h + 1) * hd)
                z_out[hr, here] = zs[h]
                g = inner(h, zs[h])
                zb = zb_out[hr, here] - tall_dot(g, m_s[h])
                zb_out[hr, here] = zb
                sb = lax.rsqrt(jnp.sum(zb * zb, axis=0, keepdims=True) * n_inv + epsilon)
                outs.append(zb * sb * gain[hr] + shift[hr])
                gs.append(g * (rate_t[h : h + 1, here] * in_last * (1.0 / MB)))
            gw = jnp.concatenate(gs, axis=0)
            lanes = slice(p * CH, (p + 1) * CH)
            mixed[here, lanes] = joined[here, lanes] + jnp.concatenate(outs, axis=0).T
            kn = joined[here, span + p * CH : span + (p + 1) * CH]
            upd = mm(split(gw), split(kn))
            w_s[rows] = jnp.where(whole, w_s[rows], w0[rows]) - jnp.where(block_diag, upd, 0.0)
            b_s[rows] = jnp.where(whole, b_s[rows], b0[rows]) - lane_sum(gw)
        return carry

    lax.fori_loop(0, chunks, chunk, 0)


def ttt_forward(joined, rate, rate_t, seg, seg_t, w0, b0, gain, shift, hd, heads):
    length = joined.shape[0]
    span = heads * hd
    chunks = length // CH
    shape = jax.ShapeDtypeStruct
    return pl.pallas_call(
        functools.partial(forward_body, hd=hd, heads=heads),
        out_shape=(
            shape((length, span), f32),
            shape((span, length), f32),
            shape((span, length), f32),
            shape((chunks, span, CH), f32),
            shape((chunks, span, 1), f32),
        ),
        scratch_shapes=[
            pltpu.VMEM((span, CH), f32),
            pltpu.VMEM((span, 1), f32),
            pltpu.VMEM((span, CH), f32),
            pltpu.VMEM((span, CH), f32),
            pltpu.VMEM((heads, CH, 2 * CH), bf16),
            pltpu.VMEM((heads, CH, 2 * CH), bf16),
        ],
        compiler_params=pltpu.CompilerParams(vmem_limit_bytes=48 << 20),
        name="inner_forward",
    )(joined, rate, rate_t, seg, seg_t, w0, b0, gain, shift)


def backward_body(
    joined, rate_t, seg, seg_t, w0, b0, gain, shift, z_in, zb_in, w_in, b_in, dy,
    dq_out, dk_out, dv_out, dr_out, dw_out, db_out, dg_out, dsh_out,
    dw_s, db_s, p_s, u_s, f_s, bb_s, e2_s, u2_s, gt_s, dzb_s, at_s, sc_s,
    *, hd, heads,
):
    pairs = heads * hd // CH
    per = CH // hd
    span = heads * hd
    chunks = joined.shape[0] // CH
    n_inv = 1.0 / hd
    row_head = iota((CH, CH), 0) // hd
    lane_head = iota((CH, CH), 1) // hd
    lane_block = iota((hd, CH), 1) // MB
    block_diag = row_head == lane_head
    for ref in (dw_s, db_s, dw_out, db_out, dg_out, dsh_out):
        ref[...] = jnp.zeros_like(ref)

    def mean(x):
        return head_sum(x, hd) * n_inv

    def chunk(index, carry):
        c = chunks - 1 - index
        ts = pl.multiple_of(c * CH, CH)
        here = pl.ds(ts, CH)
        seg_row = seg_t[:, here]
        seg_col = seg[here, :]
        last_seg = seg_row[:, CH - 1 : CH]
        prev = jnp.max(jnp.where(iota(seg_t.shape, 1) < ts, seg_t[...], 0.0), keepdims=True)
        carried = seg_row == prev
        carried_col = seg_col == prev
        in_last = (seg_row == last_seg).astype(f32)
        whole = last_seg == prev
        same = seg_col == seg_row
        before, within = coefficients(True)
        before = jnp.where(same, before, 0.0)
        within = jnp.where(same, within, 0.0)
        consts = {}
        for p in range(pairs):
            rows = slice(p * CH, (p + 1) * CH)
            lanes = slice(p * CH, (p + 1) * CH)
            qn = joined[here, p * CH : (p + 1) * CH]
            kn = joined[here, span + p * CH : span + (p + 1) * CH]
            vn = joined[here, 2 * span + p * CH : 2 * span + (p + 1) * CH]
            k_t, v_t, dy_t = kn.T, vn.T, dy[here, lanes].T
            qs, ks, kts = split(qn), split(kn), split(k_t)
            g_col = gain[rows]
            gsq = g_col * g_col
            zb = zb_in[rows, here]
            sb = lax.rsqrt(mean(zb * zb) + epsilon)
            ub = zb * sb
            dg_out[rows] += lane_sum(dy_t * ub)
            dsh_out[rows] += lane_sum(dy_t)
            pb = dy_t * g_col
            dzb = sb * (pb - mean(pb) - ub * mean(pb * ub))
            dzb_s[rows] = dzb
            z = z_in[rows, here]
            s = lax.rsqrt(mean(z * z) + epsilon)
            u = z * s
            gu = gsq * u
            e = gu + g_col * (shift[rows] - v_t + k_t)
            c_eu = mean(e * u)
            g_t = s * (e - mean(e) - u * c_eu)
            gt_s[rows] = g_t
            u_s[rows] = u
            f_s[rows] = g_t + s * gu
            bb_s[rows] = (s * s) * (gsq - c_eu)
            e2_s[rows] = (s * s) * (e + gu)
            u2_s[rows] = s * u
            h1 = s * mean(gu)
            h2 = 2.0 * s * c_eu + s * mean(gu * u)
            dzbs = split(dzb)
            gts = split(g_t)
            dzbn = split(dzb.T)
            from_state = mm(split(dw_s[rows]), kts) + db_s[rows]
            pieces = []
            dq = dy[here, lanes]
            dk = jnp.zeros((CH, CH), f32)
            for hh in range(per):
                h = p * per + hh
                hr = slice(hh * hd, (hh + 1) * hd)
                r_row = rate_t[h : h + 1, here]
                consts[h] = (h1[hh * hd : hh * hd + 1], h2[hh * hd : hh * hd + 1])
                own = (row_head == hh).astype(bf16)
                own_lane = (lane_head == hh).astype(bf16)
                kt_h = (kts[0] * own, kts[1] * own)
                sc = (mm(ks, kt_h) + 1.0) * before
                sc_s[h] = sc
                at_s[h] = wide(sc * r_row)
                scq = (mm(qs, kt_h) + 1.0) * within
                pt = mm(dzbn, (gts[0] * own, gts[1] * own))
                dr_out[h : h + 1, here] = -jnp.sum(pt * scq, axis=0, keepdims=True) - (
                    (1.0 / MB) * in_last
                ) * jnp.sum(g_t[hr] * from_state[hr], axis=0, keepdims=True)
                pm = pt * (within * r_row)
                pms = split(pm)
                pmts = split(pm.T)
                kn_h = (ks[0] * own_lane, ks[1] * own_lane)
                qn_h = (qs[0] * own_lane, qs[1] * own_lane)
                dq = dq - mm(pms, kn_h)
                dk = dk - mm(pmts, qn_h)
                pieces.append(
                    -mm((dzbs[0][hr], dzbs[1][hr]), split(scq * r_row))
                    - from_state[hr] * (r_row * in_last * (1.0 / MB))
                )
            p_s[rows] = jnp.concatenate(pieces, axis=0)
            w0s = split(w0[rows])
            wd = split(w_in[c, rows] - w0[rows])
            zero = jnp.zeros((), bf16)
            dzbn_c = (jnp.where(carried_col, dzbn[0], zero), jnp.where(carried_col, dzbn[1], zero))
            dq_out[here, lanes] = dq + mm(dzbn, w0s) + mm(dzbn_c, wd)
            dk_out[here, lanes] = dk

        def upstream(h, pv):
            hr = slice(h * hd, (h + 1) * hd)
            h1, h2 = consts[h]
            pm = jnp.sum(pv, axis=0, keepdims=True) * n_inv
            q = jnp.sum(pv * u_s[hr], axis=0, keepdims=True) * n_inv
            kf = jnp.sum(pv * f_s[hr], axis=0, keepdims=True) * n_inv
            kappa = kf - h1 * pm - h2 * q
            dz = (pv - pm) * bb_s[hr] - q * e2_s[hr] - kappa * u2_s[hr]
            return dz, pm, q

        def step(index, ps):
            now = lane_block == (CH // MB - 1 - index)
            new = []
            for h in range(heads):
                dz = jnp.where(now, upstream(h, ps[h])[0], 0.0)
                new.append(ps[h] - tall_dot(dz, at_s[h]))
            return tuple(new)

        ps = tuple(p_s[h * hd : (h + 1) * hd] for h in range(heads))
        ps = lax.fori_loop(0, CH // MB - 1, step, ps)

        for p in range(pairs):
            rows = slice(p * CH, (p + 1) * CH)
            lanes = slice(p * CH, (p + 1) * CH)
            qn = joined[here, p * CH : (p + 1) * CH]
            kn = joined[here, span + p * CH : span + (p + 1) * CH]
            vn = joined[here, 2 * span + p * CH : 2 * span + (p + 1) * CH]
            qs, ks = split(qn), split(kn)
            g_t = gt_s[rows]
            gts = split(g_t)
            dzs, des = [], []
            for hh in range(per):
                h = p * per + hh
                hr = slice(h * hd, (h + 1) * hd)
                dz, pm, q = upstream(h, ps[h])
                dzs.append(dz - jnp.sum(dz, axis=0, keepdims=True) * n_inv)
                z = z_in[hr, here]
                s = lax.rsqrt(jnp.sum(z * z, axis=0, keepdims=True) * n_inv + epsilon)
                des.append(s * (ps[h] - pm - u_s[hr] * q))
            dz = jnp.concatenate(dzs, axis=0)
            de = jnp.concatenate(des, axis=0)
            g_col = gain[rows]
            gde = g_col * de
            t_t = shift[rows] + (kn - vn).T
            dg_out[rows] += lane_sum((2.0 * g_col * u_s[rows] + t_t) * de)
            dsh_out[rows] += lane_sum(gde)
            gden = gde.T
            dv_out[here, lanes] = -gden
            dzn = split(dz.T)
            dk = dk_out[here, lanes] + gden
            r_rows = []
            for hh in range(per):
                h = p * per + hh
                r_row = rate_t[h : h + 1, here]
                own = (row_head == hh).astype(bf16)
                own_lane = (lane_head == hh).astype(bf16)
                rt = mm(dzn, (gts[0] * own, gts[1] * own))
                dr_out[h : h + 1, here] -= jnp.sum(rt * sc_s[h], axis=0, keepdims=True)
                ra = rt * (before * r_row)
                dk = dk - mm(split(ra + ra.T), (ks[0] * own_lane, ks[1] * own_lane))
                r_rows.append(jnp.broadcast_to(r_row * in_last * (1.0 / MB), (hd, CH)))
            gw = g_t * jnp.concatenate(r_rows, axis=0)
            w0s = split(w0[rows])
            wd = split(w_in[c, rows] - w0[rows])
            zero = jnp.zeros((), bf16)
            dzn_c = (jnp.where(carried_col, dzn[0], zero), jnp.where(carried_col, dzn[1], zero))
            dk = dk + mm(dzn, w0s) + mm(dzn_c, wd) - mm(split(gw.T), split(dw_s[rows]))
            dk_out[here, lanes] = dk
            dzb = dzb_s[rows]
            dzc = jnp.where(carried, dz, 0.0)
            dzbc = jnp.where(carried, dzb, 0.0)
            diag = jnp.where(block_diag, mm(split(dzc), ks) + mm(split(dzbc), qs), 0.0)
            rest = jnp.where(
                block_diag, mm(split(dz - dzc), ks) + mm(split(dzb - dzbc), qs), 0.0
            )
            dw = dw_s[rows]
            db = db_s[rows]
            dw_out[rows] += jnp.where(whole, 0.0, dw) + rest
            db_out[rows] += jnp.where(whole, 0.0, db) + lane_sum(dz - dzc + dzb - dzbc)
            dw_s[rows] = jnp.where(whole, dw, 0.0) + diag
            db_s[rows] = jnp.where(whole, db, 0.0) + lane_sum(dzc + dzbc)
        return carry

    lax.fori_loop(0, chunks, chunk, 0)


def ttt_backward(joined, rate_t, seg, seg_t, w0, b0, gain, shift, saved, dy, hd, heads):
    length = joined.shape[0]
    span = heads * hd
    shape = jax.ShapeDtypeStruct
    return pl.pallas_call(
        functools.partial(backward_body, hd=hd, heads=heads),
        out_shape=(
            shape((length, span), f32),
            shape((length, span), f32),
            shape((length, span), f32),
            shape((heads, length), f32),
            shape((span, CH), f32),
            shape((span, 1), f32),
            shape((span, 1), f32),
            shape((span, 1), f32),
        ),
        scratch_shapes=[
            pltpu.VMEM((span, CH), f32),
            pltpu.VMEM((span, 1), f32),
        ]
        + [pltpu.VMEM((span, CH), f32)] * 8
        + [
            pltpu.VMEM((heads, CH, 2 * CH), bf16),
            pltpu.VMEM((heads, CH, CH), f32),
        ],
        compiler_params=pltpu.CompilerParams(vmem_limit_bytes=48 << 20),
        name="inner_backward",
    )(joined, rate_t, seg, seg_t, w0, b0, gain, shift, *saved, dy)


def state_in(inner_weight, inner_bias):
    heads, hd, _ = inner_weight.shape
    per = CH // hd
    w_t = jnp.swapaxes(inner_weight, 1, 2)
    w_t = w_t - jnp.mean(w_t, axis=1, keepdims=True)
    placed = [
        jnp.pad(w_t[h], ((0, 0), ((h % per) * hd, CH - hd - (h % per) * hd)))
        for h in range(heads)
    ]
    b = inner_bias - jnp.mean(inner_bias, axis=1, keepdims=True)
    return jnp.concatenate(placed, axis=0), b.reshape(heads * hd, 1)


def state_back(dw, db, heads, hd):
    per = CH // hd
    parts = [
        dw[h * hd : (h + 1) * hd, (h % per) * hd : (h % per + 1) * hd] for h in range(heads)
    ]
    d = jnp.stack(parts)
    d = jnp.swapaxes(d - jnp.mean(d, axis=1, keepdims=True), 1, 2)
    b = db.reshape(heads, hd)
    return d, b - jnp.mean(b, axis=1, keepdims=True)


def product(left, right):
    return jnp.dot(left, right, precision=lax.Precision.HIGH, preferred_element_type=f32)


def left_product(left, right):
    return lax.dot_general(
        left, right, (((0,), (0,)), ((), ())), precision=lax.Precision.HIGH,
        preferred_element_type=f32,
    )


def right_product(left, right):
    return lax.dot_general(
        left, right, (((1,), (1,)), ((), ())), precision=lax.Precision.HIGH,
        preferred_element_type=f32,
    )


def heads_grid():
    size = lax.axis_size("heads")
    deep = 4 if size % 4 == 0 else 1
    return deep, size // deep


def heads_place():
    _, across = heads_grid()
    index = lax.axis_index("heads")
    return index // across, index % across


def shift(value, dz, dx):
    deep, across = heads_grid()
    pairs = [
        (h, (h // across + dz) % deep * across + (h % across + dx) % across)
        for h in range(deep * across)
    ]
    return lax.ppermute(value, "heads", pairs)


def swap(value, axis, bit):
    return lax.ppermute(value, axis, [(i, i ^ bit) for i in range(lax.axis_size(axis))])


def row_shift(value, step):
    size = lax.axis_size("rows")
    return lax.ppermute(value, "rows", [(r, (r + 2 * step) % size) for r in range(size)])


def butterfly(value, axis, hooks=()):
    size = lax.axis_size(axis)
    bits = [1 << i for i in range(size.bit_length() - 1)][::-1]
    for index, bit in enumerate(bits):
        (other,) = meet([swap(value, axis, bit)], turn(hooks, index))
        value = value + other
    return value


def small_gather(value, hooks=()):
    size = lax.axis_size("heads")
    place = jnp.arange(size) == lax.axis_index("heads")
    place = place.reshape((size,) + (1,) * value.ndim)
    return butterfly(jnp.where(place, value[None], 0.0), "heads", hooks)


class Held:
    def __init__(self, value):
        self.value = value


def meet(values, held=()):
    out = lax.optimization_barrier(tuple(values) + tuple(item.value for item in held))
    for item, value in zip(held, out[len(values) :]):
        item.value = value
    return list(out[: len(values)])


def meet_one(value, *held):
    return meet([value], held)[0]


def turn(hooks, index):
    hook = hooks[index] if index < len(hooks) else ()
    return hook() if callable(hook) else hook


def gather_columns(value, hooks=()):
    deep, across = heads_grid()
    z, x = heads_place()
    rows, cols = value.shape
    out = jnp.zeros((rows, cols * deep * across), value.dtype)
    here, ready = value, [(0, 0, value)]
    for dz in range(deep):
        moved = [shift(here, 0, dx) for dx in range(1, across)]
        if dz + 1 < deep:
            moved.append(shift(here, 1, 0))
        for oz, ox, item in ready:
            column = ((z - oz) % deep * across + (x - ox) % across) * cols
            out = lax.dynamic_update_slice(out, item, (0, column))
        *moved, out = meet(moved + [out], turn(hooks, dz))
        ready = [(dz, dx, moved[dx - 1]) for dx in range(1, across)]
        if dz + 1 < deep:
            here = moved[-1]
            ready.append((dz + 1, 0, here))
    for oz, ox, item in ready:
        column = ((z - oz) % deep * across + (x - ox) % across) * cols
        out = lax.dynamic_update_slice(out, item, (0, column))
    return out


def scatter_columns(value, extra=None, hooks=()):
    deep, across = heads_grid()
    z, x = heads_place()
    rows, width = value.shape
    cols = width // (deep * across)

    def piece(dz, dx):
        column = ((z - dz) % deep * across + (x - dx) % across) * cols
        block = lax.dynamic_slice(value, (0, column), (rows, cols))
        if extra is not None:
            tail = lax.dynamic_slice(extra, (0, column), (extra.shape[0], cols))
            block = jnp.concatenate([block, tail], 0)
        return block

    total = None
    for index, dz in enumerate(list(range(1, deep)) + [0]):
        moved = [shift(piece(dz, dx), 0, dx) for dx in range(1, across)]
        if total is not None:
            moved.append(shift(total, 1, 0))
        total = piece(dz, 0)
        for item in meet(moved, turn(hooks, index)):
            total = total + item
    return total


def half_of(value, index, axis):
    size = value.shape[axis] // 2
    return lax.dynamic_slice_in_dim(value, index * size, size, axis)


def both_cores(value):
    return jnp.concatenate([value, swap(value, "rows", 1)], 0)


def tokens_half(value, core):
    return jnp.concatenate(
        [half_of(value, core, 1), swap(half_of(value, 1 - core, 1), "rows", 1)], 0
    )


def chips_along():
    return lax.axis_size("rows") // 2


def other_chips(value):
    return [row_shift(value, step) for step in range(1, chips_along())]


def place_body(core, own, other, *outs, axis, widths):
    first = core[0] == 0
    at = 0
    for out, width in zip(outs, widths):
        mine, its = (own[:, at : at + width], other[:, at : at + width]) if axis == 0 else (own[...], other[...])
        low = jnp.where(first, mine, its)
        high = jnp.where(first, its, mine)
        if axis == 0:
            out[0] = low
            out[1] = high
        else:
            out[:, : low.shape[1]] = low
            out[:, low.shape[1] :] = high
        at += width


def place(own, other, core, axis, widths):
    rows, cols = own.shape
    steps = max(n for n in (1, 2, 4) if rows % (8 * n) == 0)
    size = rows // steps
    part = pl.BlockSpec((size, cols), lambda i: (i, 0))
    if axis == 0:
        shapes = [(2, rows, width) for width in widths]
        specs = [pl.BlockSpec((2, size, width), lambda i: (0, i, 0)) for width in widths]
    else:
        shapes = [(rows, 2 * cols)]
        specs = [pl.BlockSpec((size, 2 * cols), lambda i: (i, 0))]
    out = pl.pallas_call(
        functools.partial(place_body, axis=axis, widths=widths),
        grid=(steps,),
        out_shape=[jax.ShapeDtypeStruct(shape, f32) for shape in shapes],
        in_specs=[pl.BlockSpec(memory_space=pltpu.SMEM), part, part],
        out_specs=specs,
        compiler_params=pltpu.CompilerParams(vmem_limit_bytes=48 << 20),
        name="place",
    )(core.reshape(1).astype(jnp.int32), own, other)
    return [o.reshape(2 * rows, -1) if axis == 0 else o for o in out]


def finish(total, core, axis, widths=None):
    widths = (total.shape[1],) if widths is None else widths
    return place(total, swap(total, "rows", 1), core, axis, widths)


def row_products(lefts, rights):
    total = None
    for left, right in zip(lefts, rights):
        part = left_product(left, right)
        total = part if total is None else total + part
    return total


class Along:
    def __init__(self, value, parts=4, axis=0):
        self.own = value
        self.axis = axis
        pieces = jnp.split(value, parts, axis)
        self.steps = [
            [Held(row_shift(piece, step)) for piece in pieces] for step in range(1, chips_along())
        ]

    def __getitem__(self, i):
        return [step[i] for step in self.steps]

    def all(self):
        return [self.own] + [
            step[0].value if len(step) == 1
            else jnp.concatenate([item.value for item in step], self.axis)
            for step in self.steps
        ]


def silu_parts(a):
    sig = jax.nn.sigmoid(a)
    return a * sig, sig * (1.0 + a * (1.0 - sig))


def gelu_parts(v):
    k = 0.7978845608028654
    inner = k * (v + 0.044715 * v * v * v)
    th = jnp.tanh(inner)
    slope = 0.5 * (1.0 + th) + 0.5 * v * (1.0 - th * th) * k * (1.0 + 3 * 0.044715 * v * v)
    return 0.5 * v * (1.0 + th), slope


def on_device(
    stream,
    doc_starts,
    valid_mask,
    first_gain,
    w_query,
    w_key,
    w_value,
    w_rate,
    b_rate,
    inner_weight,
    inner_bias,
    inner_gain,
    inner_shift,
    post_gain,
    post_shift,
    w_gate_attn,
    w_out,
    second_gain,
    w_gate,
    w_up,
    w_down,
    cotangent,
):
    _, length, width = stream.shape
    tokens = stream.reshape(length, width)
    slab = second_gain.shape[0]
    column = lax.axis_index("heads") * slab
    core = lax.axis_index("rows") % 2
    heads, hd = inner_bias.shape
    span = heads * hd
    total_span = span * lax.axis_size("heads")
    grad_output = cotangent.reshape(length, slab)
    early = {}

    def first():
        early["r1"] = Held(lax.rsqrt(jnp.mean(tokens * tokens, -1, keepdims=True) + epsilon))
        return [early["r1"]]

    def second():
        early["unit"] = Held(tokens * early["r1"].value)
        return [early["unit"]]

    def third():
        early["pair"] = Held(half_of(early["unit"].value, core, 1))
        return [early["pair"]]

    gains = small_gather(jnp.stack([first_gain, second_gain]), [first, second, third])
    gain_one = gains[:, 0].reshape(width)
    gain_two = gains[:, 1].reshape(width)
    r1, unit = early["r1"].value, early["unit"].value
    dy_in, gain_one = lax.optimization_barrier((grad_output, gain_one))
    unit_y = Along(
        jnp.concatenate(
            [early["pair"].value, swap(half_of(unit, 1 - core, 1), "rows", 1)], 0
        )
    )
    w_joined = jnp.concatenate([w_query, w_key, w_value, w_gate_attn], axis=1)
    normed = unit * gain_one
    joined = product(normed, w_joined)
    rate_pre = lax.dot_general(
        w_rate, normed, (((0,), (1,)), ((), ())), precision=lax.Precision.HIGH,
        preferred_element_type=f32,
    )
    joined = Held(joined)
    after = {}

    def run_inner():
        after["mixed"] = [
            Held(item) for item in ttt_forward(
                joined.value, rate, rate_t, seg, seg_t, w0, b0, gain_col, shift_col, hd, heads
            )
        ]
        return [*after["mixed"], *unit_y[1]]

    sig = jax.nn.sigmoid(rate_pre + b_rate[:, None])
    rate_t = sig / hd
    rate = rate_t.T
    seg = jnp.cumsum(doc_starts.reshape(length)).astype(f32)
    seg, seg_t = seg[:, None], seg[None]
    w0, b0 = state_in(inner_weight, inner_bias)
    gain_col, shift_col = inner_gain.reshape(span, 1), inner_shift.reshape(span, 1)
    dy_held = Held(gather_columns(dy_in, [[], [joined, *unit_y[0]], run_inner]))
    joined = joined.value
    gate_pre = joined[:, 3 * span :]
    mixed, *saved = [item.value for item in after["mixed"]]
    row_sums = butterfly(jnp.stack([jnp.sum(mixed, 1), jnp.sum(mixed * mixed, 1)]), "heads")
    row_sums = meet_one(row_sums, *unit_y[2], dy_held)
    row_mean = row_sums[0] / total_span
    inv_std = lax.rsqrt(row_sums[1] / total_span - row_mean * row_mean + epsilon)[:, None]
    centered = (mixed - row_mean[:, None]) * inv_std
    shaped = centered * post_gain + post_shift
    gate_act, gate_slope = gelu_parts(gate_pre)
    gathered = gather_columns(gate_act * shaped, [(), unit_y[3]])
    gathered_pair = tokens_half(gathered, core)
    attn = product(gathered, w_out)
    stream_cols = lax.dynamic_slice_in_dim(tokens, column, slab, 1)
    hidden = stream_cols + attn
    whole = gather_columns(hidden)
    dy_full = dy_held.value

    r2 = lax.rsqrt(jnp.mean(whole * whole, -1, keepdims=True) + epsilon)
    hnorm = whole * r2 * gain_two
    hnorm_y = Along(tokens_half(hnorm, core), 8)
    a = product(hnorm, w_gate)
    c = product(hnorm, w_up)
    act, slope = silu_parts(a)
    m = act * c
    ffn_part = product(m, w_down)
    deep, across = heads_grid()
    z, x = heads_place()

    dy_full, ffn_part = meet([dy_full, ffn_part], hnorm_y[0])

    def ffn_piece(dz, dx):
        place_of = (z - dz) % deep * across + (x - dx) % across
        return lax.dynamic_slice_in_dim(ffn_part, place_of * slab, slab, 1)

    def ffn_across(dz):
        return [Held(shift(ffn_piece(dz, dx), 0, dx)) for dx in range(1, across)]

    soon = [dz for dz in (1, 2) if dz < deep]
    ffn_x = {dz: ffn_across(dz) for dz in soon}
    soon_x = [item for dz in soon for item in ffn_x[dz]]
    dm = right_product(dy_full, w_down)
    da = meet_one(dm * c * slope, *hnorm_y[1], *soon_x[: across - 1])
    dc = dm * act
    da_y, dc_y = Along(da, 2), Along(dc, 2)
    dhnorm = meet_one(right_product(da, w_gate), *soon_x[across - 1 :], *hnorm_y[2], *hnorm_y[3])
    dhnorm = dhnorm + right_product(dc, w_up)
    dhnorm = meet_one(dhnorm, *hnorm_y[4], *hnorm_y[5])

    def ffn_tile(dz):
        out = ffn_piece(dz, 0)
        for item in ffn_x[dz]:
            out = out + item.value
        return out

    ffn_steps = []

    def ffn_step(dz):
        ffn_steps.append(Held(shift(ffn_steps[-1].value + ffn_tile(dz) if ffn_steps else ffn_tile(dz), 1, 0)))
        return ffn_steps[-1]

    d_gain_two = jnp.sum(dhnorm * whole * r2, 0, keepdims=True)
    weighted = dhnorm * gain_two
    d_whole = r2 * weighted - whole * (r2 * r2 * r2) * jnp.mean(
        whole * weighted, -1, keepdims=True
    )
    pad = jnp.zeros((7, width), f32)
    da_pair, dc_pair = both_cores(da), both_cores(dc)
    own_gate = Held(left_product(da_pair, hnorm_y.own))
    own_up = Held(left_product(dc_pair, hnorm_y.own))
    own_down = Held(left_product(both_cores(m), tokens_half(dy_full, core)))
    d_part = scatter_columns(
        d_whole,
        jnp.concatenate([d_gain_two, pad], 0),
        [
            [*hnorm_y[6], *hnorm_y[7]],
            [*da_y[0], own_down],
            lambda: [*da_y[1], own_gate, *([ffn_step(1)] if deep > 1 else [])],
            [*dc_y[0], own_up],
        ],
    )
    d_hidden = grad_output + d_part[:length]
    d_gain_two = d_part[length]
    own_out = Held(left_product(gathered_pair, both_cores(d_hidden)))
    down_y = Along(own_down.value, 4, 1)
    late = {}

    def cores(values):
        return [both_cores(value) for value in values]

    def total(name, own, lefts, rights):
        for left, right in zip(lefts[1:], rights[1:]):
            own = own + left_product(left, right)
        late[name] = Held(own)
        return late[name]

    def placed(name, value, axis, widths=None):
        late[name] = [Held(item) for item in finish(value, core, axis, widths)]
        return late[name]

    d_gated = scatter_columns(
        right_product(d_hidden, w_out),
        None,
        [
            lambda: [*dc_y[1], *([ffn_step(2)] if deep > 2 else [])],
            [*down_y[0], own_out],
            lambda: [
                *down_y[1],
                total("gate", own_gate.value, cores(da_y.all()), hnorm_y.all()),
            ],
            lambda: [
                *down_y[2],
                total("up", own_up.value, cores(dc_y.all()), hnorm_y.all()),
            ],
        ],
    )
    out_y = Along(own_out.value, 1)
    d_shaped = d_gated * gate_act
    d_gate_pre = d_gated * shaped * gate_slope
    d_post_gain = jnp.sum(d_shaped * centered, 0)
    d_post_shift = jnp.sum(d_shaped, 0)
    d_center = d_shaped * post_gain
    gain_half = half_of(gain_one, core, 0)
    normed_pairs = [pair * gain_half for pair in unit_y.all()]
    d_gate_y = Along(d_gate_pre, 1)
    own_attn = Held(left_product(normed_pairs[0], both_cores(d_gate_pre)))
    back_sums = butterfly(
        jnp.stack([jnp.sum(d_center, 1), jnp.sum(d_center * centered, 1)]), "heads"
    )
    back_sums, ffn_part = meet([back_sums, ffn_part], ffn_steps[-1:])
    for dz in range(deep):
        if dz not in ffn_x:
            ffn_x[dz] = ffn_across(dz)
    for dz in range(3, deep):
        ffn_step(dz)
    ffn = Held((ffn_steps[-1].value if ffn_steps else 0.0) + ffn_tile(0))
    d_mixed = inv_std * (
        d_center - back_sums[0][:, None] / total_span
        - centered * back_sums[1][:, None] / total_span
    )
    dq, dk, dv, d_rate, dw, db, dg, dsh = ttt_backward(
        joined, rate_t, seg, seg_t, w0, b0, gain_col, shift_col, saved, d_mixed, hd, heads
    )
    dq = meet_one(dq, *down_y[3], own_attn)
    d_inner_weight, d_inner_bias = state_back(dw, db, heads, hd)
    d_rate_pre = d_rate * rate_t * (1.0 - sig)
    d_three = jnp.concatenate([dq, dk, dv], 1)
    d_three_y, d_rate_y = Along(d_three, 1), Along(d_rate_pre, 1)
    d_joined = jnp.concatenate([d_three, d_gate_pre], 1)
    d_normed = right_product(d_joined, w_joined) + lax.dot_general(
        d_rate_pre, w_rate, (((0,), (1,)), ((), ())), precision=lax.Precision.HIGH,
        preferred_element_type=f32,
    )
    d_normed = meet_one(d_normed, *d_gate_y[0], *out_y[0], ffn)
    ffn = ffn.value
    output = hidden + ffn
    d_gain_one = jnp.sum(d_normed * tokens * r1, 0, keepdims=True)
    weighted = d_normed * gain_one
    d_tokens = r1 * weighted - tokens * (r1 * r1 * r1) * jnp.mean(
        tokens * weighted, -1, keepdims=True
    )

    own_three = Held(left_product(normed_pairs[0], both_cores(d_three)))
    weights = valid_mask.reshape(-1).astype(f32)[:, None]
    stats = jnp.stack(
        [
            jnp.sum(weights * member * member)
            for member in (stream_cols, attn, hidden, ffn, output)
        ]
        + [jnp.sum(weights) / lax.axis_size("heads")]
    )
    def rate_total():
        out = None
        for pair, d in zip(normed_pairs, d_rate_y.all()):
            part = product(jnp.concatenate([d, swap(d, "rows", 1)], 1), pair)
            out = part if out is None else out + part
        late["rate"] = Held(out)
        return late["rate"]

    hooks = [
        lambda: [own_three, *placed("g_gate", late["gate"].value, 1)],
        lambda: [
            total("attn", own_attn.value, normed_pairs, cores(d_gate_y.all())),
            *placed("g_up", late["up"].value, 1),
        ],
        lambda: [
            *d_three_y[0],
            *placed("g_down", sum(down_y.all()), 1),
        ],
        lambda: [
            total("three", own_three.value, normed_pairs, cores(d_three_y.all())),
            *placed("g_attn", late["attn"].value, 0),
            *d_rate_y[0],
        ],
    ]
    across_slabs = jnp.tile(jnp.pad(stats, (0, slab - stats.size)), width // slab)[None]
    d_part = scatter_columns(
        d_tokens,
        jnp.concatenate([d_gain_one, across_slabs, pad[1:]], 0),
        hooks,
    )
    d_stream = d_hidden + d_part[:length]
    d_gain_one = d_part[length]
    stats = d_part[length + 1, : stats.size]

    placed("g_out", sum(out_y.all()), 0)
    g_query, g_key, g_value = finish(late["three"].value, core, 0, (span,) * 3)
    ((g_gate,), (g_up,), (g_down,), (g_out,), (g_gate_attn,)) = (
        [item.value for item in late[name]]
        for name in ("g_gate", "g_up", "g_down", "g_out", "g_attn")
    )
    g_rate = rate_total().value
    ends = (g_rate, swap(g_rate, "rows", 1))
    g_rate = jnp.where(core == 0, jnp.concatenate(ends, 1), jnp.concatenate(ends[::-1], 1))

    small = [
        d_gain_one, jnp.sum(d_rate_pre, 1), d_inner_weight, d_inner_bias, dg, dsh,
        d_post_gain, d_post_shift, d_gain_two, stats,
    ]
    packed = butterfly(jnp.concatenate([item.reshape(-1) for item in small]), "rows")
    parts = []
    at = 0
    for item in small:
        parts.append(packed[at : at + item.size])
        at += item.size
    stats = parts[9]
    rms_values = jnp.sqrt(stats[:5] / (stats[5] * width))
    return (
        output.reshape(1, length, slab),
        d_stream.reshape(1, length, slab),
        parts[0],
        g_query,
        g_key,
        g_value,
        g_rate.T,
        parts[1],
        parts[2].reshape(heads, hd, hd),
        parts[3].reshape(heads, hd),
        parts[4].reshape(heads, hd),
        parts[5].reshape(heads, hd),
        parts[6],
        parts[7],
        g_gate_attn,
        g_out,
        parts[8],
        g_gate.T,
        g_up.T,
        g_down,
        rms_values,
    )


def solution(mesh):
    in_specs = (
        P("rows", None, None),
        P("rows", None),
        P("rows", None),
        P("heads"),
        P(None, "heads"),
        P(None, "heads"),
        P(None, "heads"),
        P(None, "heads"),
        P("heads"),
        P("heads", None, None),
        P("heads", None),
        P("heads", None),
        P("heads", None),
        P("heads"),
        P("heads"),
        P(None, "heads"),
        P(None, "heads"),
        P("heads"),
        P(None, "heads"),
        P(None, "heads"),
        P("heads", None),
        P("rows", None, "heads"),
    )
    out_specs = (
        P("rows", None, "heads"),
        P("rows", None, "heads"),
        P("heads"),
        P(None, "heads"),
        P(None, "heads"),
        P(None, "heads"),
        P(None, "heads"),
        P("heads"),
        P("heads", None, None),
        P("heads", None),
        P("heads", None),
        P("heads", None),
        P("heads"),
        P("heads"),
        P(None, "heads"),
        P(None, "heads"),
        P("heads"),
        P(None, "heads"),
        P(None, "heads"),
        P("heads", None),
        P(),
    )
    return jax.shard_map(
        on_device, mesh=mesh, in_specs=in_specs, out_specs=out_specs, check_vma=False
    )
```
